512 devices in a mesh: group: 64 (over z, y_hi, core), tp: 8 (over x, y_lo).
Axes of the slice: x: 4, y: 4 (y_hi: 2, y_lo: 2; y = y_hi * 2 + y_lo), z: 16, core: 2. Of those that a mesh axis runs over, the one named last changes fastest.
Arguments:
- queries: bfloat16 [4096, 2048], P('group', 'tp'), may hold values from -22 to 22
- new_kv: bfloat16 [4096, 1024], P('group', 'tp'), may hold values from -6 to 6
- local_cache: bfloat16 [16384, 1024], P('group', 'tp'), may hold values from -6 to 6
- remote_pool: bfloat16 [32768, 1024], P('group', 'tp'), may hold values from -6 to 6
- page_index: int32 [64, 64], P('group'), may hold values from 0 to 63, each once within a row
- lengths: int32 [64], P('group'), may hold values from 256 to 768, as said below
- sinks: float32 [32], P('tp'), may hold values from 4 to 8
- out_weight: bfloat16 [2048, 2880], P('tp'), may hold values from -0.125 to 0.125
- residual: bfloat16 [4096, 2880], P('group', 'tp'), may hold values from -6 to 6
- norm_gain: float32 [2880], replicated, may hold values from 0.5 to 2
- routes: int32 [4096, 4], P('group'), may hold values from 0 to 31, all different within a row; in each aligned block of 64 rows (0 to 63, 64 to 127, ...) at most 10 rows name the same one
- route_weights: float32 [4096, 4], P('group'), may hold values from 0.1 to 1
- expert_gate: bfloat16 [64, 2880, 1440], P('group', None, 'tp'), may hold values from -0.109375 to 0.109375
- expert_up: bfloat16 [64, 2880, 1440], P('group', None, 'tp'), may hold values from -0.109375 to 0.109375
- expert_down: bfloat16 [64, 1440, 2880], P('group', None, 'tp'), may hold values from -0.109375 to 0.109375
Outputs:
- layer_out: bfloat16 [4096, 2880], P('group', 'tp')
The draws below stay inside these ranges and needn't reach their ends.
Inputs may be any that keep to these rules, and one draw needn't show every extreme that they name: `lengths`: every request has at least 256 cached positions; some request has exactly 256, some exactly 768. `routes`: within the rows of one request no expert is named by more than 10 rows. `page_index`: each row is a permutation.
All inputs are finite; a program needn't handle non-finite values.
Results may differ from the reference program's by a relative error of at most 0.013.
Values may be sent and summed in bfloat16 or wider, within the bound.
A program may use at most 64 MiB of HBM per device.

```python
import math
import jax
import jax.numpy as jnp
import numpy as np
from jax import lax

D = 2880
FF = 2880
HQ = 32
HK = 8
HEAD = 64
TOPK = 4
NEW_TOK = 64
LOCAL_LEN = 256
PAGE = 8
REQS = 64
TOKENS = 4096
EXPERTS = 32
CAP = 10


def cached_lengths(key):
    longest = LOCAL_LEN + REQS * PAGE
    values = jax.random.randint(jax.random.fold_in(key, 101), (REQS,), LOCAL_LEN, longest + 1, dtype=jnp.int32)
    chosen = jax.random.randint(jax.random.fold_in(key, 102), (), 0, REQS, dtype=jnp.int32)
    values = values.at[chosen].set(longest)
    values = values.at[(chosen + 1) % REQS].set(LOCAL_LEN)
    return values


def draw_lengths(key, part):
    return cached_lengths(key)


def draw_local_cache(key, part):
    base = jnp.clip(jax.random.normal(jax.random.fold_in(key, 201), (REQS * LOCAL_LEN, HK * 2 * HEAD), jnp.float32), -6.0, 6.0)
    return base.astype(jnp.bfloat16)


def draw_queries(key, part):
    base = 1.5 * jnp.clip(jax.random.normal(jax.random.fold_in(key, 301), (TOKENS, HQ * HEAD), jnp.float32), -6.0, 6.0)
    return base.astype(jnp.bfloat16)


def block_levels(own_key, dims, cuts, low, largest):
    def one(position, shards_of):
        steps = jax.random.uniform(jax.random.fold_in(jax.random.fold_in(own_key, 6), position), (shards_of,), jnp.float32, low / len(cuts), largest / len(cuts))
        return jnp.repeat(jnp.exp(steps), dims[position] // shards_of).reshape((-1,) + (1,) * (len(dims) - position - 1))

    factor_of = one(*cuts[0])
    for cut in cuts[1:]:
        factor_of = factor_of * one(*cut)
    return factor_of


def deal_out(own_key, own, number, rows, amount, top, most, slope):
    sequence = jax.random.permutation(own_key, amount)
    heavy_load, usual = portions_of(amount, rows * top, most, slope, True), portions_of(amount, rows * top, most, slope, False)
    places = jnp.arange(amount)

    def named(sizes, rotation):
        used = int((sizes > 0).sum())
        fixed = max(1, used // 4)
        passed = fixed + (places - fixed + rotation * (used - fixed)) % max(1, amount - fixed)
        return jnp.zeros((amount,), jnp.int32).at[sequence[jnp.where(places < fixed, places, passed)]].set(jnp.asarray(sizes, jnp.int32))

    sizes = jnp.where(number % 4 == 0, named(heavy_load, number // 4), named(usual, number - number // 4 - 1))
    mixed = jax.random.permutation(jax.random.fold_in(own, 3), amount)
    source_of, receiver = mixed[0:amount // 2 * 2:2], mixed[1:amount // 2 * 2:2]
    margin = jnp.minimum(sizes[source_of] - 1, most - sizes[receiver]) // 2
    margin = jnp.where((source_of == sequence[0]) | (receiver == sequence[0]) | (sizes[receiver] == 0), 0, jnp.maximum(margin, 0))
    passed = jax.random.randint(jax.random.fold_in(own, 4), (amount // 2,), 0, 1 << 20) % (margin + 1)
    sizes = sizes.at[source_of].add(-passed).at[receiver].add(passed)
    labels = jnp.searchsorted(jnp.cumsum(sizes), jnp.arange(rows * top), side="right").astype(jnp.int32)
    table = labels.reshape(top, rows).T
    table = table[jax.random.permutation(jax.random.fold_in(own, 1), rows)]
    rotation = jax.random.randint(jax.random.fold_in(own, 2), (rows, 1), 0, top)
    return jnp.take_along_axis(table, (jnp.arange(top)[None, :] + rotation) % top, axis=1)


def portions_of(count, total, most, lean, full):
    weights = [(1 << 20) // math.isqrt(grade ** lean) + 1 for grade in range(1, count + 1)]
    largest = most if full else min(most, max(-(-total // count), total * weights[0] // sum(weights)))
    least = 1 if total - largest >= count - 1 else 0
    holding, rest = [largest] + [least] * (count - 1), total - largest - least * (count - 1)
    while rest > 0:
        candidates = [i for i in range(1, count) if holding[i] < largest] or [i for i in range(1, count) if holding[i] < most]
        mass, remaining = sum([weights[i] for i in candidates]), rest
        for i in candidates:
            more = min(most - holding[i], max(1, remaining * weights[i] // mass), rest)
            holding[i] = holding[i] + more
            rest = rest - more
    return np.array(holding)


def gaussian(rng, shape, spread, most, shards=(), held_as=jnp.bfloat16):
    values = spread * jax.random.normal(rng, shape, jnp.float32)
    if shards:
        values = values * block_levels(rng, shape, shards, -0.22, 0.18)
    return jnp.clip(values, -most, most).astype(held_as)


def setup_inputs(seed: int = 0) -> dict:
    keys = jax.random.split(jax.random.key(seed), 16)
    queries = draw_queries(jax.random.fold_in(keys[15], 71), 0)
    new_kv = gaussian(keys[1], (TOKENS, HK * 2 * HEAD), 1.0, 6.0, ((0, 64), (1, 8)))
    local_cache = draw_local_cache(jax.random.fold_in(keys[15], 71), 0)
    remote_pool = gaussian(keys[3], (REQS * REQS * PAGE, HK * 2 * HEAD), 1.0, 6.0, ((0, 64), (1, 8)))
    page_index = jax.vmap(lambda own: jax.random.permutation(own, REQS))(jax.random.split(keys[4], REQS)).reshape((REQS, REQS)).astype(jnp.int32)
    lengths = draw_lengths(jax.random.fold_in(keys[15], 71), 0)
    sinks = jnp.clip(4.0 + 4.0 * jax.random.uniform(keys[6], (HQ,), jnp.float32) ** block_levels(keys[6], (HQ,), ((0, 8),), -0.2, 0.2), 4.0, 8.0)
    out_weight = gaussian(keys[7], (HQ * HEAD, D), (HQ * HEAD) ** -0.5, 0.125, ((0, 8),))
    residual = gaussian(keys[8], (TOKENS, D), 1.0, 6.0, ((0, 64), (1, 8)))
    norm_gain = jnp.clip(jnp.exp(jax.random.uniform(keys[9], (D,), jnp.float32, math.log(0.5), math.log(2.0))), 0.5, 2.0)
    routes_keys = jax.random.split(jax.random.fold_in(keys[10], 1), TOKENS // NEW_TOK)
    routes_turns = jax.random.permutation(jax.random.fold_in(keys[10], 3), TOKENS // NEW_TOK)
    routes = jax.vmap(lambda own, number: deal_out(jax.random.fold_in(keys[10], 2), own, number, NEW_TOK, EXPERTS, TOPK, CAP, 2))(routes_keys, routes_turns).reshape((TOKENS, TOPK))
    route_weights = jnp.clip(jnp.exp(math.log(1.0) - 2.3025851 * jax.random.uniform(keys[11], (TOKENS, TOPK), jnp.float32) ** block_levels(keys[11], (TOKENS, TOPK), ((0, 64),), -0.2, 0.2)), 0.1, 1.0)
    expert_gate = gaussian(keys[12], (2 * EXPERTS, D, FF // 2), D ** -0.5, 0.109375, ((0, 64), (2, 8)))
    expert_up = gaussian(keys[13], (2 * EXPERTS, D, FF // 2), D ** -0.5, 0.109375, ((0, 64), (2, 8)))
    expert_down = gaussian(keys[14], (2 * EXPERTS, FF // 2, D), FF ** -0.5, 0.109375, ((0, 64), (2, 8)))
    return dict(queries=queries, new_kv=new_kv, local_cache=local_cache, remote_pool=remote_pool, page_index=page_index, lengths=lengths, sinks=sinks, out_weight=out_weight, residual=residual, norm_gain=norm_gain, routes=routes, route_weights=route_weights, expert_gate=expert_gate, expert_up=expert_up, expert_down=expert_down)


THETA = 150000.0
ALPHA = 1.702
EPSILON = 1e-05

def rotate(values, positions):
    half_dim = values.shape[-1] // 2
    inverse = THETA ** (-2.0 * jnp.arange(half_dim, dtype=jnp.float32) / values.shape[-1])
    angles = positions[:, None, None] * inverse[None, None, :]
    cosine = jnp.cos(angles)
    sine_part = jnp.sin(angles)
    first_part = values[..., :half_dim]
    second_part = values[..., half_dim:]
    return jnp.concatenate([first_part * cosine - second_part * sine_part, second_part * cosine + first_part * sine_part], axis=-1)

def attend(query_rows, kv_rows, cache_kv, cache_valid, sinks, length):
    block_len = query_rows.shape[0]
    kv_heads = kv_rows.shape[1] // (2 * HEAD)
    query_heads = query_rows.shape[1] // HEAD
    group_size = query_heads // kv_heads
    positions = (length + jnp.arange(block_len, dtype=jnp.int32)).astype(jnp.float32)
    query_rot = rotate(query_rows.astype(jnp.float32).reshape(block_len, query_heads, HEAD), positions).astype(jnp.bfloat16)
    kv_parts = kv_rows.reshape(block_len, kv_heads, 2, HEAD)
    key_rot = rotate(kv_parts[:, :, 0].astype(jnp.float32), positions).astype(jnp.bfloat16)
    cache_parts = cache_kv.reshape(cache_kv.shape[0], kv_heads, 2, HEAD)
    all_keys = jnp.concatenate([cache_parts[:, :, 0], key_rot], axis=0)
    all_values = jnp.concatenate([cache_parts[:, :, 1], kv_parts[:, :, 1]], axis=0)
    token_order = jnp.arange(block_len, dtype=jnp.int32)
    causal = token_order[None, :] <= token_order[:, None]
    allowed = jnp.concatenate([jnp.broadcast_to(cache_valid[None, :], (block_len, cache_valid.shape[0])), causal], axis=1)
    row_allowed = jnp.repeat(allowed, group_size, axis=0)
    score_scale = HEAD ** (-0.5)
    outputs = []
    for kv_head in range(kv_heads):
        query_block = query_rot[:, kv_head * group_size:(kv_head + 1) * group_size].reshape(block_len * group_size, HEAD)
        scores = jnp.dot(query_block, all_keys[:, kv_head].T, preferred_element_type=jnp.float32) * score_scale
        scores = jnp.where(row_allowed, scores, -jnp.inf)
        sink_rows = jnp.tile(sinks[kv_head * group_size:(kv_head + 1) * group_size], block_len)
        row_max = jnp.maximum(lax.optimization_barrier(jnp.max(scores, axis=1)), sink_rows)
        weights = jnp.exp(scores - row_max[:, None])
        denominator = lax.optimization_barrier(jnp.sum(weights, axis=1)) + jnp.exp(sink_rows - row_max)
        blended = jnp.dot(weights.astype(jnp.bfloat16), all_values[:, kv_head], preferred_element_type=jnp.float32) / denominator[:, None]
        outputs.append(blended.astype(jnp.bfloat16).reshape(block_len, group_size * HEAD))
    return jnp.concatenate(outputs, axis=1)

def reference(queries, new_kv, local_cache, remote_pool, page_index, lengths, sinks, out_weight, residual, norm_gain, routes, route_weights, expert_gate, expert_up, expert_down):
    lane_count = new_kv.shape[1]
    remote_rows = remote_pool.reshape(REQS, REQS, PAGE, lane_count).transpose(1, 0, 2, 3).reshape(REQS, REQS * PAGE, lane_count)
    local_rows = local_cache.reshape(REQS, LOCAL_LEN, lane_count)
    offsets = jnp.arange(PAGE, dtype=jnp.int32)

    def one_request(request_items):
        query_rows, kv_rows, local_part, remote_part, page_row, length = request_items
        remote_pos = LOCAL_LEN + page_row[:, None] * PAGE + offsets[None, :]
        cache_valid = jnp.concatenate([jnp.ones((LOCAL_LEN,), jnp.bool_), (remote_pos < length).reshape(-1)])
        cache_kv = jnp.concatenate([local_part, remote_part], axis=0)
        return attend(query_rows, kv_rows, cache_kv, cache_valid, sinks, length)
    attended = lax.map(one_request, (queries.reshape(REQS, NEW_TOK, -1), new_kv.reshape(REQS, NEW_TOK, lane_count), local_rows, remote_rows, page_index, lengths))
    attended = attended.reshape(TOKENS, -1)
    hidden_state = residual.astype(jnp.float32) + jnp.dot(attended, out_weight, preferred_element_type=jnp.float32)
    mean_square = lax.optimization_barrier(jnp.mean(hidden_state * hidden_state, axis=1, keepdims=True))
    normed = (hidden_state * lax.rsqrt(mean_square + EPSILON) * norm_gain).astype(jnp.bfloat16)
    mixing = route_weights / lax.optimization_barrier(jnp.sum(route_weights, axis=1, keepdims=True))
    capacity = REQS * CAP

    def one_expert(running, expert):
        chosen = routes == expert
        member = jnp.any(chosen, axis=1)
        weight = lax.optimization_barrier(jnp.sum(jnp.where(chosen, mixing, 0.0), axis=1))
        token_index = jnp.nonzero(member, size=capacity, fill_value=0)[0].astype(jnp.int32)
        filled = (jnp.arange(capacity, dtype=jnp.int32) < jnp.sum(member.astype(jnp.int32))).astype(jnp.float32)
        token_rows = normed[token_index]
        summed = jnp.zeros((capacity, D), jnp.float32)
        for which_half in range(2):
            slot_id = 2 * expert + which_half
            gate_val = jnp.dot(token_rows, expert_gate[slot_id], preferred_element_type=jnp.float32)
            up_val = jnp.dot(token_rows, expert_up[slot_id], preferred_element_type=jnp.float32)
            active = (gate_val * jax.nn.sigmoid(ALPHA * gate_val) * (up_val + 1.0)).astype(jnp.bfloat16)
            half_out = jnp.dot(active, expert_down[slot_id], preferred_element_type=jnp.float32).astype(jnp.bfloat16)
            summed = summed + half_out.astype(jnp.float32)
        contrib = (weight[token_index] * filled)[:, None] * summed
        return (running.at[token_index].add(contrib), None)
    moe_out, unused = lax.scan(one_expert, jnp.zeros((TOKENS, D), jnp.float32), jnp.arange(EXPERTS, dtype=jnp.int32))
    return (hidden_state + moe_out).astype(jnp.bfloat16)
```

```python
import jax
import jax.numpy as jnp
from jax import lax
from jax.sharding import PartitionSpec as P

HEAD = 64


THETA = 150000.0
ALPHA = 1.702
EPSILON = 1e-05


def rotate(values, positions):
    half_dim = values.shape[-1] // 2
    inverse = THETA ** (-2.0 * jnp.arange(half_dim, dtype=jnp.float32) / values.shape[-1])
    angles = positions[:, None, None] * inverse[None, None, :]
    cosine = jnp.cos(angles)
    sine_part = jnp.sin(angles)
    first_part = values[..., :half_dim]
    second_part = values[..., half_dim:]
    return jnp.concatenate(
        [
            first_part * cosine - second_part * sine_part,
            second_part * cosine + first_part * sine_part,
        ],
        axis=-1,
    )


def attend(query_rows, kv_rows, cache_kv, cache_valid, sinks, length):
    block_len = query_rows.shape[0]
    kv_heads = kv_rows.shape[1] // (2 * HEAD)
    query_heads = query_rows.shape[1] // HEAD
    group_size = query_heads // kv_heads
    positions = (length + jnp.arange(block_len, dtype=jnp.int32)).astype(jnp.float32)
    query_rot = rotate(
        query_rows.astype(jnp.float32).reshape(block_len, query_heads, HEAD), positions
    ).astype(jnp.bfloat16)
    kv_parts = kv_rows.reshape(block_len, kv_heads, 2, HEAD)
    key_rot = rotate(kv_parts[:, :, 0].astype(jnp.float32), positions).astype(jnp.bfloat16)
    cache_parts = cache_kv.reshape(cache_kv.shape[0], kv_heads, 2, HEAD)
    all_keys = jnp.concatenate([cache_parts[:, :, 0], key_rot], axis=0)
    all_values = jnp.concatenate([cache_parts[:, :, 1], kv_parts[:, :, 1]], axis=0)
    token_order = jnp.arange(block_len, dtype=jnp.int32)
    causal = token_order[None, :] <= token_order[:, None]
    allowed = jnp.concatenate(
        [jnp.broadcast_to(cache_valid[None, :], (block_len, cache_valid.shape[0])), causal], axis=1
    )
    row_allowed = jnp.repeat(allowed, group_size, axis=0)
    score_scale = HEAD ** (-0.5)
    query_block = query_rot.reshape(block_len * group_size, HEAD)
    scores = (
        jnp.dot(query_block, all_keys[:, 0].T, preferred_element_type=jnp.float32) * score_scale
    )
    scores = jnp.where(row_allowed, scores, -jnp.inf)
    sink_rows = jnp.tile(sinks, block_len)
    row_max = jnp.maximum(jnp.max(scores, axis=1), sink_rows)
    weights = jnp.exp(scores - row_max[:, None])
    denominator = jnp.sum(weights, axis=1) + jnp.exp(sink_rows - row_max)
    blended = (
        jnp.dot(weights.astype(jnp.bfloat16), all_values[:, 0], preferred_element_type=jnp.float32)
        / denominator[:, None]
    )
    outputs = blended.astype(jnp.bfloat16).reshape(block_len, group_size * HEAD)
    return outputs


def on_device(
    queries,
    new_kv,
    local_cache,
    remote_pool,
    page_index,
    lengths,
    sinks,
    out_weight,
    residual,
    norm_gain,
    routes,
    route_weights,
    expert_gate,
    expert_up,
    expert_down,
):
    groups = lax.axis_size("group")
    lane_count = remote_pool.shape[1]
    local_len = local_cache.shape[0]
    fetched = lax.all_to_all(
        remote_pool.reshape(groups, -1, lane_count),
        "group",
        split_axis=0,
        concat_axis=0,
        tiled=True,
    )
    page_len = fetched.shape[1]
    length = lengths[0]
    offsets = jnp.arange(page_len, dtype=jnp.int32)
    remote_pos = local_len + page_index[0][:, None] * page_len + offsets[None, :]
    cache_valid = jnp.concatenate(
        [jnp.ones((local_len,), jnp.bool_), (remote_pos < length).reshape(-1)]
    )
    cache_kv = jnp.concatenate([local_cache, fetched.reshape(-1, lane_count)], axis=0)
    attended = attend(queries, new_kv, cache_kv, cache_valid, sinks, length)
    width = residual.shape[1]
    tp_count = lax.axis_size("tp")
    start = lax.axis_index("tp") * width
    own_gain = lax.dynamic_slice_in_dim(norm_gain, start, width, 0)
    partial_sum = jnp.dot(attended, out_weight, preferred_element_type=jnp.float32)
    partial_blocks = partial_sum.reshape(partial_sum.shape[0], tp_count, width).transpose(1, 0, 2)
    own_attn = lax.psum_scatter(partial_blocks, "tp", scatter_dimension=0, tiled=False)
    own_state = own_attn + residual.astype(jnp.float32)
    square_sum = lax.psum(jnp.sum(own_state * own_state, axis=1, keepdims=True), "tp")
    mean_square = square_sum / (width * tp_count)
    normed_own = (own_state * lax.rsqrt(mean_square + EPSILON) * own_gain).astype(jnp.bfloat16)
    block_len = normed_own.shape[0]
    top_count = routes.shape[1]
    experts = groups // 2
    capacity = 5 * block_len * top_count // (4 * experts)
    member = jnp.any(
        routes[:, :, None] == jnp.arange(experts, dtype=jnp.int32)[None, None, :], axis=1
    ).astype(jnp.int32)
    slot_rank = jnp.cumsum(member, axis=0) - member
    slot_hit = member[:, :, None] * (
        slot_rank[:, :, None] == jnp.arange(capacity, dtype=jnp.int32)[None, None, :]
    ).astype(jnp.int32)
    slot_token = jnp.sum(slot_hit * jnp.arange(block_len, dtype=jnp.int32)[:, None, None], axis=0)
    slot_valid = jnp.sum(slot_hit, axis=0)
    send_own = jnp.take(normed_own, slot_token.reshape(-1), axis=0) * slot_valid.reshape(
        -1, 1
    ).astype(jnp.bfloat16)
    hidden_part = expert_gate.shape[2]
    gate_and_up = jnp.concatenate([expert_gate[0], expert_up[0]], axis=1)
    outgoing = send_own
    feature_count = outgoing.shape[1]
    outgoing = outgoing.reshape(experts, 1, capacity, feature_count)
    outgoing = jnp.broadcast_to(outgoing, (experts, 2, capacity, feature_count)).reshape(
        groups, capacity, feature_count
    )
    received = lax.all_to_all(outgoing, "group", split_axis=0, concat_axis=0, tiled=True)
    sources, slot_count, part_features = received.shape
    whole = lax.all_gather(received.reshape(sources * slot_count, part_features), "tp", axis=0)
    gate_blocks = gate_and_up.reshape(tp_count, part_features, gate_and_up.shape[1])
    both = jnp.einsum("tsf,tfh->sh", whole, gate_blocks, preferred_element_type=jnp.float32)
    gate_val = both[:, :hidden_part]
    up_val = both[:, hidden_part:]
    active = (gate_val * jax.nn.sigmoid(ALPHA * gate_val) * (up_val + 1.0)).astype(jnp.bfloat16)
    joined = lax.all_gather(active, "tp", axis=0)
    down_blocks = expert_down[0].reshape(tp_count, hidden_part, expert_down.shape[2])
    result = jnp.einsum("tsh,thd->sd", joined, down_blocks, preferred_element_type=jnp.float32).astype(
        jnp.bfloat16
    )
    returned = result.reshape(sources, slot_count, result.shape[1])
    arrived = lax.all_to_all(returned, "group", split_axis=0, concat_axis=0, tiled=True)
    halves = arrived.reshape(experts, 2, capacity, width).astype(jnp.float32)
    summed = (halves[:, 0] + halves[:, 1]).reshape(experts * capacity, width)
    rank_at = jnp.take_along_axis(slot_rank, routes, axis=1)
    picked = jnp.take(summed, (routes * capacity + rank_at).reshape(-1), axis=0).reshape(
        block_len, top_count, width
    )
    mixing = route_weights / jnp.sum(route_weights, axis=1, keepdims=True)
    moe_out = jnp.sum(mixing[:, :, None] * picked, axis=1)
    return (own_state + moe_out).astype(jnp.bfloat16)


def solution(mesh):
    return jax.shard_map(
        on_device,
        mesh=mesh,
        in_specs=(
            P("group", "tp"),
            P("group", "tp"),
            P("group", "tp"),
            P("group", "tp"),
            P("group", None),
            P("group"),
            P("tp"),
            P("tp", None),
            P("group", "tp"),
            P(),
            P("group", None),
            P("group", None),
            P("group", None, "tp"),
            P("group", None, "tp"),
            P("group", None, "tp"),
        ),
        out_specs=P("group", "tp"),
        check_vma=False,
    )
```

```python
import jax
import jax.numpy as jnp
from jax import lax
from jax.experimental import pallas as pl
from jax.experimental.pallas import tpu as pltpu
from jax.sharding import PartitionSpec as P

HEAD = 64


THETA = 150000.0
ALPHA = 1.702
EPSILON = 1e-05


def _exchange_kernel(x_ref, o_ref, buf, send_sem, recv_sem, local_sem):
    count = x_ref.shape[0]
    me = lax.axis_index("group")
    lane = lax.axis_index("tp")
    barrier = pltpu.get_barrier_semaphore()

    def greet(step, carry):
        peer = lax.rem(me + step, count)
        pl.semaphore_signal(barrier, inc=1, device_id=(peer, lane), device_id_type=pl.DeviceIdType.MESH)
        return carry

    lax.fori_loop(1, count, greet, 0)
    pl.semaphore_wait(barrier, count - 1)
    local = pltpu.make_async_copy(x_ref.at[me], buf.at[me], local_sem)
    local.start()

    def send(step, carry):
        peer = lax.rem(me + step, count)
        pltpu.make_async_remote_copy(
            src_ref=x_ref.at[peer],
            dst_ref=buf.at[me],
            send_sem=send_sem,
            recv_sem=recv_sem,
            device_id=(peer, lane),
            device_id_type=pl.DeviceIdType.MESH,
        ).start()
        return carry

    lax.fori_loop(1, count, send, 0)
    local.wait()
    every = pltpu.make_async_remote_copy(
        src_ref=x_ref.at[pl.ds(0, count - 1)],
        dst_ref=buf.at[pl.ds(0, count - 1)],
        send_sem=send_sem,
        recv_sem=recv_sem,
        device_id=(lax.rem(me + 1, count), lane),
        device_id_type=pl.DeviceIdType.MESH,
    )
    every.wait_send()
    every.wait_recv()
    o_ref[...] = buf[...]


def group_exchange(x, collective_id):
    return pl.pallas_call(
        _exchange_kernel,
        out_shape=jax.ShapeDtypeStruct(x.shape, x.dtype),
        in_specs=[pl.BlockSpec(memory_space=pltpu.VMEM)],
        out_specs=pl.BlockSpec(memory_space=pltpu.VMEM),
        scratch_shapes=[
            pltpu.VMEM(x.shape, x.dtype),
            pltpu.SemaphoreType.DMA(()),
            pltpu.SemaphoreType.DMA(()),
            pltpu.SemaphoreType.DMA(()),
        ],
        compiler_params=pltpu.CompilerParams(collective_id=collective_id, has_side_effects=True),
    )(x)


def rotate(values, positions):
    half_dim = values.shape[-1] // 2
    inverse = THETA ** (-2.0 * jnp.arange(half_dim, dtype=jnp.float32) / values.shape[-1])
    angles = positions[:, None, None] * inverse[None, None, :]
    cosine = jnp.cos(angles)
    sine_part = jnp.sin(angles)
    first_part = values[..., :half_dim]
    second_part = values[..., half_dim:]
    return jnp.concatenate(
        [
            first_part * cosine - second_part * sine_part,
            second_part * cosine + first_part * sine_part,
        ],
        axis=-1,
    )


def attend(query_rows, kv_rows, cache_kv, cache_valid, sinks, length):
    block_len = query_rows.shape[0]
    kv_heads = kv_rows.shape[1] // (2 * HEAD)
    query_heads = query_rows.shape[1] // HEAD
    group_size = query_heads // kv_heads
    positions = (length + jnp.arange(block_len, dtype=jnp.int32)).astype(jnp.float32)
    query_rot = rotate(
        query_rows.astype(jnp.float32).reshape(block_len, query_heads, HEAD), positions
    ).astype(jnp.bfloat16)
    kv_parts = kv_rows.reshape(block_len, kv_heads, 2, HEAD)
    key_rot = rotate(kv_parts[:, :, 0].astype(jnp.float32), positions).astype(jnp.bfloat16)
    cache_parts = cache_kv.reshape(cache_kv.shape[0], kv_heads, 2, HEAD)
    all_keys = jnp.concatenate([cache_parts[:, :, 0], key_rot], axis=0)
    all_values = jnp.concatenate([cache_parts[:, :, 1], kv_parts[:, :, 1]], axis=0)
    token_order = jnp.arange(block_len, dtype=jnp.int32)
    causal = token_order[None, :] <= token_order[:, None]
    allowed = jnp.concatenate(
        [jnp.broadcast_to(cache_valid[None, :], (block_len, cache_valid.shape[0])), causal], axis=1
    )
    row_allowed = jnp.repeat(allowed, group_size, axis=0)
    score_scale = HEAD ** (-0.5)
    query_block = query_rot.reshape(block_len * group_size, HEAD)
    scores = (
        jnp.dot(query_block, all_keys[:, 0].T, preferred_element_type=jnp.float32) * score_scale
    )
    scores = jnp.where(row_allowed, scores, -jnp.inf)
    sink_rows = jnp.tile(sinks, block_len)
    row_max = jnp.maximum(jnp.max(scores, axis=1), sink_rows)
    weights = jnp.exp(scores - row_max[:, None])
    denominator = jnp.sum(weights, axis=1) + jnp.exp(sink_rows - row_max)
    blended = (
        jnp.dot(weights.astype(jnp.bfloat16), all_values[:, 0], preferred_element_type=jnp.float32)
        / denominator[:, None]
    )
    outputs = blended.astype(jnp.bfloat16).reshape(block_len, group_size * HEAD)
    return outputs


def on_device(
    queries,
    new_kv,
    local_cache,
    remote_pool,
    page_index,
    lengths,
    sinks,
    out_weight,
    residual,
    norm_gain,
    routes,
    route_weights,
    expert_gate,
    expert_up,
    expert_down,
):
    groups = lax.axis_size("group")
    lane_count = remote_pool.shape[1]
    local_len = local_cache.shape[0]
    fetched = group_exchange(remote_pool.reshape(groups, -1, lane_count), 1)
    page_len = fetched.shape[1]
    length = lengths[0]
    offsets = jnp.arange(page_len, dtype=jnp.int32)
    remote_pos = local_len + page_index[0][:, None] * page_len + offsets[None, :]
    cache_valid = jnp.concatenate(
        [jnp.ones((local_len,), jnp.bool_), (remote_pos < length).reshape(-1)]
    )
    cache_kv = jnp.concatenate([local_cache, fetched.reshape(-1, lane_count)], axis=0)
    attended = attend(queries, new_kv, cache_kv, cache_valid, sinks, length)
    width = residual.shape[1]
    tp_count = lax.axis_size("tp")
    start = lax.axis_index("tp") * width
    own_gain = lax.dynamic_slice_in_dim(norm_gain, start, width, 0)
    partial_sum = jnp.dot(attended, out_weight, preferred_element_type=jnp.float32)
    partial_blocks = partial_sum.reshape(partial_sum.shape[0], tp_count, width).transpose(1, 0, 2)
    own_attn = lax.psum_scatter(partial_blocks, "tp", scatter_dimension=0, tiled=False)
    own_state = own_attn + residual.astype(jnp.float32)
    square_sum = lax.psum(jnp.sum(own_state * own_state, axis=1, keepdims=True), "tp")
    mean_square = square_sum / (width * tp_count)
    normed_own = (own_state * lax.rsqrt(mean_square + EPSILON) * own_gain).astype(jnp.bfloat16)
    block_len = normed_own.shape[0]
    top_count = routes.shape[1]
    experts = groups // 2
    capacity = 5 * block_len * top_count // (4 * experts)
    member = jnp.any(
        routes[:, :, None] == jnp.arange(experts, dtype=jnp.int32)[None, None, :], axis=1
    ).astype(jnp.int32)
    slot_rank = jnp.cumsum(member, axis=0) - member
    slot_hit = member[:, :, None] * (
        slot_rank[:, :, None] == jnp.arange(capacity, dtype=jnp.int32)[None, None, :]
    ).astype(jnp.int32)
    slot_token = jnp.sum(slot_hit * jnp.arange(block_len, dtype=jnp.int32)[:, None, None], axis=0)
    slot_valid = jnp.sum(slot_hit, axis=0)
    send_own = jnp.take(normed_own, slot_token.reshape(-1), axis=0) * slot_valid.reshape(
        -1, 1
    ).astype(jnp.bfloat16)
    hidden_part = expert_gate.shape[2]
    gate_and_up = jnp.concatenate([expert_gate[0], expert_up[0]], axis=1)
    outgoing = send_own
    feature_count = outgoing.shape[1]
    outgoing = outgoing.reshape(experts, 1, capacity, feature_count)
    outgoing = jnp.broadcast_to(outgoing, (experts, 2, capacity, feature_count)).reshape(
        groups, capacity, feature_count
    )
    received = group_exchange(outgoing, 2)
    sources, slot_count, part_features = received.shape
    whole = lax.all_gather(received.reshape(sources * slot_count, part_features), "tp", axis=0)
    gate_blocks = gate_and_up.reshape(tp_count, part_features, gate_and_up.shape[1])
    both = jnp.einsum("tsf,tfh->sh", whole, gate_blocks, preferred_element_type=jnp.float32)
    gate_val = both[:, :hidden_part]
    up_val = both[:, hidden_part:]
    active = (gate_val * jax.nn.sigmoid(ALPHA * gate_val) * (up_val + 1.0)).astype(jnp.bfloat16)
    joined = lax.all_gather(active, "tp", axis=0)
    down_blocks = expert_down[0].reshape(tp_count, hidden_part, expert_down.shape[2])
    result = jnp.einsum("tsh,thd->sd", joined, down_blocks, preferred_element_type=jnp.float32).astype(
        jnp.bfloat16
    )
    returned = result.reshape(sources, slot_count, result.shape[1])
    arrived = group_exchange(returned, 3)
    halves = arrived.reshape(experts, 2, capacity, width).astype(jnp.float32)
    summed = (halves[:, 0] + halves[:, 1]).reshape(experts * capacity, width)
    rank_at = jnp.take_along_axis(slot_rank, routes, axis=1)
    picked = jnp.take(summed, (routes * capacity + rank_at).reshape(-1), axis=0).reshape(
        block_len, top_count, width
    )
    mixing = route_weights / jnp.sum(route_weights, axis=1, keepdims=True)
    moe_out = jnp.sum(mixing[:, :, None] * picked, axis=1)
    return (own_state + moe_out).astype(jnp.bfloat16)


def solution(mesh):
    return jax.shard_map(
        on_device,
        mesh=mesh,
        in_specs=(
            P("group", "tp"),
            P("group", "tp"),
            P("group", "tp"),
            P("group", "tp"),
            P("group", None),
            P("group"),
            P("tp"),
            P("tp", None),
            P("group", "tp"),
            P(),
            P("group", None),
            P("group", None),
            P("group", None, "tp"),
            P("group", None, "tp"),
            P("group", None, "tp"),
        ),
        out_specs=P("group", "tp"),
        check_vma=False,
    )
```

```python
import functools

import jax
import jax.numpy as jnp
from jax import lax
from jax.experimental import pallas as pl
from jax.experimental.pallas import tpu as pltpu
from jax.sharding import PartitionSpec as P

HEAD = 64


THETA = 150000.0
ALPHA = 1.702
EPSILON = 1e-05


def _transfer_kernel(axis, gather, x_ref, o_ref, buf, send_sem, recv_sem, local_sem):
    count = buf.shape[0]
    group_at = lax.axis_index("group")
    tp_at = lax.axis_index("tp")
    me = tp_at if axis == "tp" else group_at

    def device(peer):
        return (group_at, peer) if axis == "tp" else (peer, tp_at)

    def piece(peer):
        return x_ref if gather else x_ref.at[peer]

    barrier = pltpu.get_barrier_semaphore()

    def greet(step, carry):
        peer = lax.rem(me + step, count)
        pl.semaphore_signal(barrier, inc=1, device_id=device(peer), device_id_type=pl.DeviceIdType.MESH)
        return carry

    lax.fori_loop(1, count, greet, 0)
    pl.semaphore_wait(barrier, count - 1)
    local = pltpu.make_async_copy(piece(me), buf.at[me], local_sem)
    local.start()

    def send(step, carry):
        peer = lax.rem(me + step, count)
        pltpu.make_async_remote_copy(
            src_ref=piece(peer),
            dst_ref=buf.at[me],
            send_sem=send_sem,
            recv_sem=recv_sem,
            device_id=device(peer),
            device_id_type=pl.DeviceIdType.MESH,
        ).start()
        return carry

    lax.fori_loop(1, count, send, 0)
    local.wait()
    every = pltpu.make_async_remote_copy(
        src_ref=buf.at[pl.ds(0, count - 1)],
        dst_ref=buf.at[pl.ds(0, count - 1)],
        send_sem=send_sem,
        recv_sem=recv_sem,
        device_id=device(lax.rem(me + 1, count)),
        device_id_type=pl.DeviceIdType.MESH,
    )
    every.wait_send()
    every.wait_recv()
    o_ref[...] = buf[...]


def _transfer(x, axis, gather, collective_id):
    count = lax.axis_size(axis)
    shape = ((count,) + x.shape) if gather else x.shape
    return pl.pallas_call(
        functools.partial(_transfer_kernel, axis, gather),
        out_shape=jax.ShapeDtypeStruct(shape, x.dtype),
        in_specs=[pl.BlockSpec(memory_space=pltpu.VMEM)],
        out_specs=pl.BlockSpec(memory_space=pltpu.VMEM),
        scratch_shapes=[
            pltpu.VMEM(shape, x.dtype),
            pltpu.SemaphoreType.DMA(()),
            pltpu.SemaphoreType.DMA(()),
            pltpu.SemaphoreType.DMA(()),
        ],
        compiler_params=pltpu.CompilerParams(collective_id=collective_id, has_side_effects=True),
    )(x)


def group_exchange(x, collective_id):
    return _transfer(x, "group", False, collective_id)


def tp_gather(x, collective_id):
    return _transfer(x, "tp", True, collective_id)


def rotate(values, positions):
    half_dim = values.shape[-1] // 2
    inverse = THETA ** (-2.0 * jnp.arange(half_dim, dtype=jnp.float32) / values.shape[-1])
    angles = positions[:, None, None] * inverse[None, None, :]
    cosine = jnp.cos(angles)
    sine_part = jnp.sin(angles)
    first_part = values[..., :half_dim]
    second_part = values[..., half_dim:]
    return jnp.concatenate(
        [
            first_part * cosine - second_part * sine_part,
            second_part * cosine + first_part * sine_part,
        ],
        axis=-1,
    )


def attend(query_rows, kv_rows, cache_kv, cache_valid, sinks, length):
    block_len = query_rows.shape[0]
    kv_heads = kv_rows.shape[1] // (2 * HEAD)
    query_heads = query_rows.shape[1] // HEAD
    group_size = query_heads // kv_heads
    positions = (length + jnp.arange(block_len, dtype=jnp.int32)).astype(jnp.float32)
    query_rot = rotate(
        query_rows.astype(jnp.float32).reshape(block_len, query_heads, HEAD), positions
    ).astype(jnp.bfloat16)
    kv_parts = kv_rows.reshape(block_len, kv_heads, 2, HEAD)
    key_rot = rotate(kv_parts[:, :, 0].astype(jnp.float32), positions).astype(jnp.bfloat16)
    cache_parts = cache_kv.reshape(cache_kv.shape[0], kv_heads, 2, HEAD)
    all_keys = jnp.concatenate([cache_parts[:, :, 0], key_rot], axis=0)
    all_values = jnp.concatenate([cache_parts[:, :, 1], kv_parts[:, :, 1]], axis=0)
    token_order = jnp.arange(block_len, dtype=jnp.int32)
    causal = token_order[None, :] <= token_order[:, None]
    allowed = jnp.concatenate(
        [jnp.broadcast_to(cache_valid[None, :], (block_len, cache_valid.shape[0])), causal], axis=1
    )
    row_allowed = jnp.repeat(allowed, group_size, axis=0)
    score_scale = HEAD ** (-0.5)
    query_block = query_rot.reshape(block_len * group_size, HEAD)
    scores = (
        jnp.dot(query_block, all_keys[:, 0].T, preferred_element_type=jnp.float32) * score_scale
    )
    scores = jnp.where(row_allowed, scores, -jnp.inf)
    sink_rows = jnp.tile(sinks, block_len)
    row_max = jnp.maximum(jnp.max(scores, axis=1), sink_rows)
    weights = jnp.exp(scores - row_max[:, None])
    denominator = jnp.sum(weights, axis=1) + jnp.exp(sink_rows - row_max)
    blended = (
        jnp.dot(weights.astype(jnp.bfloat16), all_values[:, 0], preferred_element_type=jnp.float32)
        / denominator[:, None]
    )
    outputs = blended.astype(jnp.bfloat16).reshape(block_len, group_size * HEAD)
    return outputs


def on_device(
    queries,
    new_kv,
    local_cache,
    remote_pool,
    page_index,
    lengths,
    sinks,
    out_weight,
    residual,
    norm_gain,
    routes,
    route_weights,
    expert_gate,
    expert_up,
    expert_down,
):
    groups = lax.axis_size("group")
    lane_count = remote_pool.shape[1]
    local_len = local_cache.shape[0]
    fetched = group_exchange(remote_pool.reshape(groups, -1, lane_count), 1)
    page_len = fetched.shape[1]
    length = lengths[0]
    offsets = jnp.arange(page_len, dtype=jnp.int32)
    remote_pos = local_len + page_index[0][:, None] * page_len + offsets[None, :]
    cache_valid = jnp.concatenate(
        [jnp.ones((local_len,), jnp.bool_), (remote_pos < length).reshape(-1)]
    )
    cache_kv = jnp.concatenate([local_cache, fetched.reshape(-1, lane_count)], axis=0)
    attended = attend(queries, new_kv, cache_kv, cache_valid, sinks, length)
    width = residual.shape[1]
    tp_count = lax.axis_size("tp")
    start = lax.axis_index("tp") * width
    own_gain = lax.dynamic_slice_in_dim(norm_gain, start, width, 0)
    partial_sum = jnp.dot(attended, out_weight, preferred_element_type=jnp.float32)
    partial_blocks = partial_sum.reshape(partial_sum.shape[0], tp_count, width).transpose(1, 0, 2)
    own_attn = lax.psum_scatter(partial_blocks, "tp", scatter_dimension=0, tiled=False)
    own_state = own_attn + residual.astype(jnp.float32)
    square_sum = lax.psum(jnp.sum(own_state * own_state, axis=1, keepdims=True), "tp")
    mean_square = square_sum / (width * tp_count)
    normed_own = (own_state * lax.rsqrt(mean_square + EPSILON) * own_gain).astype(jnp.bfloat16)
    block_len = normed_own.shape[0]
    top_count = routes.shape[1]
    experts = groups // 2
    capacity = 5 * block_len * top_count // (4 * experts)
    member = jnp.any(
        routes[:, :, None] == jnp.arange(experts, dtype=jnp.int32)[None, None, :], axis=1
    ).astype(jnp.int32)
    slot_rank = jnp.cumsum(member, axis=0) - member
    slot_hit = member[:, :, None] * (
        slot_rank[:, :, None] == jnp.arange(capacity, dtype=jnp.int32)[None, None, :]
    ).astype(jnp.int32)
    slot_token = jnp.sum(slot_hit * jnp.arange(block_len, dtype=jnp.int32)[:, None, None], axis=0)
    slot_valid = jnp.sum(slot_hit, axis=0)
    send_own = jnp.take(normed_own, slot_token.reshape(-1), axis=0) * slot_valid.reshape(
        -1, 1
    ).astype(jnp.bfloat16)
    hidden_part = expert_gate.shape[2]
    gate_and_up = jnp.concatenate([expert_gate[0], expert_up[0]], axis=1)
    outgoing = send_own
    feature_count = outgoing.shape[1]
    outgoing = outgoing.reshape(experts, 1, capacity, feature_count)
    outgoing = jnp.broadcast_to(outgoing, (experts, 2, capacity, feature_count)).reshape(
        groups, capacity, feature_count
    )
    received = group_exchange(outgoing, 2)
    sources, slot_count, part_features = received.shape
    whole = tp_gather(received.reshape(sources * slot_count, part_features), 4)
    gate_blocks = gate_and_up.reshape(tp_count, part_features, gate_and_up.shape[1])
    both = jnp.einsum("tsf,tfh->sh", whole, gate_blocks, preferred_element_type=jnp.float32)
    gate_val = both[:, :hidden_part]
    up_val = both[:, hidden_part:]
    active = (gate_val * jax.nn.sigmoid(ALPHA * gate_val) * (up_val + 1.0)).astype(jnp.bfloat16)
    joined = tp_gather(active.T, 5)
    down_blocks = expert_down[0].reshape(tp_count, hidden_part, expert_down.shape[2])
    result = jnp.einsum("ths,thd->sd", joined, down_blocks, preferred_element_type=jnp.float32).astype(
        jnp.bfloat16
    )
    returned = result.reshape(sources, slot_count, result.shape[1])
    arrived = group_exchange(returned, 3)
    halves = arrived.reshape(experts, 2, capacity, width).astype(jnp.float32)
    summed = (halves[:, 0] + halves[:, 1]).reshape(experts * capacity, width)
    rank_at = jnp.take_along_axis(slot_rank, routes, axis=1)
    picked = jnp.take(summed, (routes * capacity + rank_at).reshape(-1), axis=0).reshape(
        block_len, top_count, width
    )
    mixing = route_weights / jnp.sum(route_weights, axis=1, keepdims=True)
    moe_out = jnp.sum(mixing[:, :, None] * picked, axis=1)
    return (own_state + moe_out).astype(jnp.bfloat16)


def solution(mesh):
    return jax.shard_map(
        on_device,
        mesh=mesh,
        in_specs=(
            P("group", "tp"),
            P("group", "tp"),
            P("group", "tp"),
            P("group", "tp"),
            P("group", None),
            P("group"),
            P("tp"),
            P("tp", None),
            P("group", "tp"),
            P(),
            P("group", None),
            P("group", None),
            P("group", None, "tp"),
            P("group", None, "tp"),
            P("group", None, "tp"),
        ),
        out_specs=P("group", "tp"),
        check_vma=False,
    )
```

```python
import functools

import jax
import jax.numpy as jnp
from jax import lax
from jax.experimental import pallas as pl
from jax.experimental.pallas import tpu as pltpu
from jax.sharding import PartitionSpec as P

HEAD = 64


THETA = 150000.0
ALPHA = 1.702
EPSILON = 1e-05


def _transfer_kernel(axis, gather, x_ref, o_ref, buf, send_sem, recv_sem, local_sem):
    count = buf.shape[0]
    group_at = lax.axis_index("group")
    tp_at = lax.axis_index("tp")
    core = lax.rem(group_at, 2)
    if axis == "tp":
        me = tp_at
    elif axis == "pair":
        me = lax.div(group_at, 2)
    else:
        me = group_at

    def device(peer):
        if axis == "tp":
            return (group_at, peer)
        if axis == "pair":
            return (2 * peer + core, tp_at)
        return (peer, tp_at)

    def piece(peer):
        return x_ref if gather else x_ref.at[peer]

    barrier = pltpu.get_barrier_semaphore()

    def greet(step, carry):
        peer = lax.rem(me + step, count)
        pl.semaphore_signal(barrier, inc=1, device_id=device(peer), device_id_type=pl.DeviceIdType.MESH)
        return carry

    lax.fori_loop(1, count, greet, 0)
    pl.semaphore_wait(barrier, count - 1)
    local = pltpu.make_async_copy(piece(me), buf.at[me], local_sem)
    local.start()

    def send(step, carry):
        peer = lax.rem(me + step, count)
        pltpu.make_async_remote_copy(
            src_ref=piece(peer),
            dst_ref=buf.at[me],
            send_sem=send_sem,
            recv_sem=recv_sem,
            device_id=device(peer),
            device_id_type=pl.DeviceIdType.MESH,
        ).start()
        return carry

    lax.fori_loop(1, count, send, 0)
    local.wait()
    every = pltpu.make_async_remote_copy(
        src_ref=buf.at[pl.ds(0, count - 1)],
        dst_ref=buf.at[pl.ds(0, count - 1)],
        send_sem=send_sem,
        recv_sem=recv_sem,
        device_id=device(lax.rem(me + 1, count)),
        device_id_type=pl.DeviceIdType.MESH,
    )
    every.wait_send()
    every.wait_recv()
    o_ref[...] = buf[...]


def _transfer(x, axis, gather, collective_id):
    count = lax.axis_size("group") // 2 if axis == "pair" else lax.axis_size(axis)
    shape = ((count,) + x.shape) if gather else x.shape
    return pl.pallas_call(
        functools.partial(_transfer_kernel, axis, gather),
        out_shape=jax.ShapeDtypeStruct(shape, x.dtype),
        in_specs=[pl.BlockSpec(memory_space=pltpu.VMEM)],
        out_specs=pl.BlockSpec(memory_space=pltpu.VMEM),
        scratch_shapes=[
            pltpu.VMEM(shape, x.dtype),
            pltpu.SemaphoreType.DMA(()),
            pltpu.SemaphoreType.DMA(()),
            pltpu.SemaphoreType.DMA(()),
        ],
        compiler_params=pltpu.CompilerParams(collective_id=collective_id, has_side_effects=True),
    )(x)


def _pair_gather_kernel(x_ref, o_ref, buf, send_sem, recv_sem, local_sem, pass_send, pass_recv):
    count = buf.shape[0]
    group_at = lax.axis_index("group")
    tp_at = lax.axis_index("tp")
    core = lax.rem(group_at, 2)
    sibling = (group_at + 1 - 2 * core, tp_at)
    barrier = pltpu.get_barrier_semaphore()

    def greet(step, carry):
        peer = lax.rem(tp_at + step, count)
        pl.semaphore_signal(barrier, inc=1, device_id=(group_at, peer), device_id_type=pl.DeviceIdType.MESH)
        return carry

    lax.fori_loop(1, count, greet, 0)
    pl.semaphore_signal(barrier, inc=1, device_id=sibling, device_id_type=pl.DeviceIdType.MESH)
    pl.semaphore_wait(barrier, count)
    local = pltpu.make_async_copy(x_ref, buf.at[tp_at, core], local_sem)
    local.start()

    def send(step, carry):
        peer = lax.rem(tp_at + step, count)
        pltpu.make_async_remote_copy(
            src_ref=x_ref,
            dst_ref=buf.at[tp_at, core],
            send_sem=send_sem,
            recv_sem=recv_sem,
            device_id=(group_at, peer),
            device_id_type=pl.DeviceIdType.MESH,
        ).start()
        return carry

    lax.fori_loop(1, count, send, 0)
    local.wait()
    every = pltpu.make_async_remote_copy(
        src_ref=buf.at[pl.ds(0, count - 1), 0],
        dst_ref=buf.at[pl.ds(0, count - 1), 0],
        send_sem=send_sem,
        recv_sem=recv_sem,
        device_id=(group_at, lax.rem(tp_at + 1, count)),
        device_id_type=pl.DeviceIdType.MESH,
    )
    every.wait_recv()
    onward = pltpu.make_async_remote_copy(
        src_ref=buf.at[:, core],
        dst_ref=buf.at[:, core],
        send_sem=pass_send,
        recv_sem=pass_recv,
        device_id=sibling,
        device_id_type=pl.DeviceIdType.MESH,
    )
    onward.start()
    every.wait_send()
    onward.wait_send()
    onward.wait_recv()
    o_ref[...] = buf[...]


def pair_gather(x, collective_id):
    shape = (lax.axis_size("tp"), 2) + x.shape
    return pl.pallas_call(
        _pair_gather_kernel,
        out_shape=jax.ShapeDtypeStruct(shape, x.dtype),
        in_specs=[pl.BlockSpec(memory_space=pltpu.VMEM)],
        out_specs=pl.BlockSpec(memory_space=pltpu.VMEM),
        scratch_shapes=[pltpu.VMEM(shape, x.dtype)] + [pltpu.SemaphoreType.DMA(())] * 5,
        compiler_params=pltpu.CompilerParams(collective_id=collective_id, has_side_effects=True),
    )(x)


def pair_exchange(x, collective_id):
    return _transfer(x, "pair", False, collective_id)


def group_exchange(x, collective_id):
    return _transfer(x, "group", False, collective_id)


def tp_gather(x, collective_id):
    return _transfer(x, "tp", True, collective_id)


def rotate(values, positions):
    half_dim = values.shape[-1] // 2
    inverse = THETA ** (-2.0 * jnp.arange(half_dim, dtype=jnp.float32) / values.shape[-1])
    angles = positions[:, None, None] * inverse[None, None, :]
    cosine = jnp.cos(angles)
    sine_part = jnp.sin(angles)
    first_part = values[..., :half_dim]
    second_part = values[..., half_dim:]
    return jnp.concatenate(
        [
            first_part * cosine - second_part * sine_part,
            second_part * cosine + first_part * sine_part,
        ],
        axis=-1,
    )


def attend(query_rows, kv_rows, cache_kv, cache_valid, sinks, length):
    block_len = query_rows.shape[0]
    kv_heads = kv_rows.shape[1] // (2 * HEAD)
    query_heads = query_rows.shape[1] // HEAD
    group_size = query_heads // kv_heads
    positions = (length + jnp.arange(block_len, dtype=jnp.int32)).astype(jnp.float32)
    query_rot = rotate(
        query_rows.astype(jnp.float32).reshape(block_len, query_heads, HEAD), positions
    ).astype(jnp.bfloat16)
    kv_parts = kv_rows.reshape(block_len, kv_heads, 2, HEAD)
    key_rot = rotate(kv_parts[:, :, 0].astype(jnp.float32), positions).astype(jnp.bfloat16)
    cache_parts = cache_kv.reshape(cache_kv.shape[0], kv_heads, 2, HEAD)
    all_keys = jnp.concatenate([cache_parts[:, :, 0], key_rot], axis=0)
    all_values = jnp.concatenate([cache_parts[:, :, 1], kv_parts[:, :, 1]], axis=0)
    token_order = jnp.arange(block_len, dtype=jnp.int32)
    causal = token_order[None, :] <= token_order[:, None]
    allowed = jnp.concatenate(
        [jnp.broadcast_to(cache_valid[None, :], (block_len, cache_valid.shape[0])), causal], axis=1
    )
    row_allowed = jnp.repeat(allowed, group_size, axis=0)
    score_scale = HEAD ** (-0.5)
    query_block = query_rot.reshape(block_len * group_size, HEAD)
    scores = (
        jnp.dot(query_block, all_keys[:, 0].T, preferred_element_type=jnp.float32) * score_scale
    )
    scores = jnp.where(row_allowed, scores, -jnp.inf)
    sink_rows = jnp.tile(sinks, block_len)
    row_max = jnp.maximum(jnp.max(scores, axis=1), sink_rows)
    weights = jnp.exp(scores - row_max[:, None])
    denominator = jnp.sum(weights, axis=1) + jnp.exp(sink_rows - row_max)
    blended = (
        jnp.dot(weights.astype(jnp.bfloat16), all_values[:, 0], preferred_element_type=jnp.float32)
        / denominator[:, None]
    )
    outputs = blended.astype(jnp.bfloat16).reshape(block_len, group_size * HEAD)
    return outputs


def on_device(
    queries,
    new_kv,
    local_cache,
    remote_pool,
    page_index,
    lengths,
    sinks,
    out_weight,
    residual,
    norm_gain,
    routes,
    route_weights,
    expert_gate,
    expert_up,
    expert_down,
):
    groups = lax.axis_size("group")
    lane_count = remote_pool.shape[1]
    local_len = local_cache.shape[0]
    fetched = group_exchange(remote_pool.reshape(groups, -1, lane_count), 1)
    page_len = fetched.shape[1]
    length = lengths[0]
    offsets = jnp.arange(page_len, dtype=jnp.int32)
    remote_pos = local_len + page_index[0][:, None] * page_len + offsets[None, :]
    cache_valid = jnp.concatenate(
        [jnp.ones((local_len,), jnp.bool_), (remote_pos < length).reshape(-1)]
    )
    cache_kv = jnp.concatenate([local_cache, fetched.reshape(-1, lane_count)], axis=0)
    attended = attend(queries, new_kv, cache_kv, cache_valid, sinks, length)
    width = residual.shape[1]
    tp_count = lax.axis_size("tp")
    start = lax.axis_index("tp") * width
    own_gain = lax.dynamic_slice_in_dim(norm_gain, start, width, 0)
    partial_sum = jnp.dot(attended, out_weight, preferred_element_type=jnp.float32)
    partial_blocks = partial_sum.reshape(partial_sum.shape[0], tp_count, width).transpose(1, 0, 2)
    own_attn = lax.psum_scatter(partial_blocks, "tp", scatter_dimension=0, tiled=False)
    own_state = own_attn + residual.astype(jnp.float32)
    square_sum = lax.psum(jnp.sum(own_state * own_state, axis=1, keepdims=True), "tp")
    mean_square = square_sum / (width * tp_count)
    normed_own = (own_state * lax.rsqrt(mean_square + EPSILON) * own_gain).astype(jnp.bfloat16)
    block_len = normed_own.shape[0]
    top_count = routes.shape[1]
    experts = groups // 2
    capacity = 5 * block_len * top_count // (4 * experts)
    member = jnp.any(
        routes[:, :, None] == jnp.arange(experts, dtype=jnp.int32)[None, None, :], axis=1
    ).astype(jnp.int32)
    slot_rank = jnp.cumsum(member, axis=0) - member
    slot_hit = member[:, :, None] * (
        slot_rank[:, :, None] == jnp.arange(capacity, dtype=jnp.int32)[None, None, :]
    ).astype(jnp.int32)
    slot_token = jnp.sum(slot_hit * jnp.arange(block_len, dtype=jnp.int32)[:, None, None], axis=0)
    slot_valid = jnp.sum(slot_hit, axis=0)
    send_own = jnp.take(normed_own, slot_token.reshape(-1), axis=0) * slot_valid.reshape(
        -1, 1
    ).astype(jnp.bfloat16)
    hidden_part = expert_gate.shape[2]
    gate_and_up = jnp.concatenate([expert_gate[0], expert_up[0]], axis=1)
    received = pair_exchange(send_own.reshape(experts, capacity, -1), 2)
    sources, slot_count, part_features = received.shape
    whole = pair_gather(received.reshape(sources * slot_count, part_features), 4)
    whole = whole.reshape(tp_count, 2 * sources * slot_count, part_features)
    gate_blocks = gate_and_up.reshape(tp_count, part_features, gate_and_up.shape[1])
    both = jnp.einsum("tsf,tfh->sh", whole, gate_blocks, preferred_element_type=jnp.float32)
    gate_val = both[:, :hidden_part]
    up_val = both[:, hidden_part:]
    active = (gate_val * jax.nn.sigmoid(ALPHA * gate_val) * (up_val + 1.0)).astype(jnp.bfloat16)
    joined = tp_gather(active.T, 5)
    down_blocks = expert_down[0].reshape(tp_count, hidden_part, expert_down.shape[2])
    result = jnp.einsum("ths,thd->sd", joined, down_blocks, preferred_element_type=jnp.float32).astype(
        jnp.bfloat16
    )
    halves = result.reshape(2, experts, capacity, width)
    core = lax.rem(lax.axis_index("group"), 2)
    groups_total = lax.axis_size("group")
    swap = [(i, i + 1 - 2 * (i % 2)) for i in range(groups_total)]
    mine = lax.dynamic_index_in_dim(halves, core, 0, keepdims=False)
    theirs = lax.dynamic_index_in_dim(halves, 1 - core, 0, keepdims=False)
    other_half = lax.ppermute(theirs, "group", swap)
    joined_halves = (mine.astype(jnp.float32) + other_half.astype(jnp.float32)).astype(jnp.bfloat16)
    arrived = pair_exchange(joined_halves, 3)
    summed = arrived.astype(jnp.float32).reshape(experts * capacity, width)
    rank_at = jnp.take_along_axis(slot_rank, routes, axis=1)
    picked = jnp.take(summed, (routes * capacity + rank_at).reshape(-1), axis=0).reshape(
        block_len, top_count, width
    )
    mixing = route_weights / jnp.sum(route_weights, axis=1, keepdims=True)
    moe_out = jnp.sum(mixing[:, :, None] * picked, axis=1)
    return (own_state + moe_out).astype(jnp.bfloat16)


def solution(mesh):
    return jax.shard_map(
        on_device,
        mesh=mesh,
        in_specs=(
            P("group", "tp"),
            P("group", "tp"),
            P("group", "tp"),
            P("group", "tp"),
            P("group", None),
            P("group"),
            P("tp"),
            P("tp", None),
            P("group", "tp"),
            P(),
            P("group", None),
            P("group", None),
            P("group", None, "tp"),
            P("group", None, "tp"),
            P("group", None, "tp"),
        ),
        out_specs=P("group", "tp"),
        check_vma=False,
    )
```

```python
import functools

import jax
import jax.numpy as jnp
from jax import lax
from jax.experimental import pallas as pl
from jax.experimental.pallas import tpu as pltpu
from jax.sharding import PartitionSpec as P

HEAD = 64


THETA = 150000.0
ALPHA = 1.702
EPSILON = 1e-05


def _transfer_kernel(axis, gather, x_ref, o_ref, buf, send_sem, recv_sem, local_sem):
    count = buf.shape[0]
    group_at = lax.axis_index("group")
    tp_at = lax.axis_index("tp")
    core = lax.rem(group_at, 2)
    if axis == "tp":
        me = tp_at
    elif axis == "pair":
        me = lax.div(group_at, 2)
    else:
        me = group_at

    def device(peer):
        if axis == "tp":
            return (group_at, peer)
        if axis == "pair":
            return (2 * peer + core, tp_at)
        return (peer, tp_at)

    def piece(peer):
        return x_ref if gather else x_ref.at[peer]

    barrier = pltpu.get_barrier_semaphore()

    def greet(step, carry):
        peer = lax.rem(me + step, count)
        pl.semaphore_signal(barrier, inc=1, device_id=device(peer), device_id_type=pl.DeviceIdType.MESH)
        return carry

    lax.fori_loop(1, count, greet, 0)
    pl.semaphore_wait(barrier, count - 1)
    local = pltpu.make_async_copy(piece(me), buf.at[me], local_sem)
    local.start()

    def send(step, carry):
        peer = lax.rem(me + step, count)
        pltpu.make_async_remote_copy(
            src_ref=piece(peer),
            dst_ref=buf.at[me],
            send_sem=send_sem,
            recv_sem=recv_sem,
            device_id=device(peer),
            device_id_type=pl.DeviceIdType.MESH,
        ).start()
        return carry

    lax.fori_loop(1, count, send, 0)
    local.wait()
    every = pltpu.make_async_remote_copy(
        src_ref=buf.at[pl.ds(0, count - 1)],
        dst_ref=buf.at[pl.ds(0, count - 1)],
        send_sem=send_sem,
        recv_sem=recv_sem,
        device_id=device(lax.rem(me + 1, count)),
        device_id_type=pl.DeviceIdType.MESH,
    )
    every.wait_send()
    every.wait_recv()
    o_ref[...] = buf[...]


def _transfer(x, axis, gather, collective_id):
    count = lax.axis_size("group") // 2 if axis == "pair" else lax.axis_size(axis)
    shape = ((count,) + x.shape) if gather else x.shape
    return pl.pallas_call(
        functools.partial(_transfer_kernel, axis, gather),
        out_shape=jax.ShapeDtypeStruct(shape, x.dtype),
        in_specs=[pl.BlockSpec(memory_space=pltpu.VMEM)],
        out_specs=pl.BlockSpec(memory_space=pltpu.VMEM),
        scratch_shapes=[
            pltpu.VMEM(shape, x.dtype),
            pltpu.SemaphoreType.DMA(()),
            pltpu.SemaphoreType.DMA(()),
            pltpu.SemaphoreType.DMA(()),
        ],
        compiler_params=pltpu.CompilerParams(collective_id=collective_id, has_side_effects=True),
    )(x)


def _pair_gather_kernel(x_ref, o_ref, buf, send_sem, recv_sem, local_sem, pass_send, pass_recv):
    count = buf.shape[0]
    group_at = lax.axis_index("group")
    tp_at = lax.axis_index("tp")
    core = lax.rem(group_at, 2)
    sibling = (group_at + 1 - 2 * core, tp_at)
    barrier = pltpu.get_barrier_semaphore()

    def greet(step, carry):
        peer = lax.rem(tp_at + step, count)
        pl.semaphore_signal(barrier, inc=1, device_id=(group_at, peer), device_id_type=pl.DeviceIdType.MESH)
        return carry

    lax.fori_loop(1, count, greet, 0)
    pl.semaphore_signal(barrier, inc=1, device_id=sibling, device_id_type=pl.DeviceIdType.MESH)
    pl.semaphore_wait(barrier, count)
    local = pltpu.make_async_copy(x_ref, buf.at[tp_at, core], local_sem)
    local.start()

    def send(step, carry):
        peer = lax.rem(tp_at + step, count)
        pltpu.make_async_remote_copy(
            src_ref=x_ref,
            dst_ref=buf.at[tp_at, core],
            send_sem=send_sem,
            recv_sem=recv_sem,
            device_id=(group_at, peer),
            device_id_type=pl.DeviceIdType.MESH,
        ).start()
        return carry

    lax.fori_loop(1, count, send, 0)
    local.wait()
    every = pltpu.make_async_remote_copy(
        src_ref=buf.at[pl.ds(0, count - 1), 0],
        dst_ref=buf.at[pl.ds(0, count - 1), 0],
        send_sem=send_sem,
        recv_sem=recv_sem,
        device_id=(group_at, lax.rem(tp_at + 1, count)),
        device_id_type=pl.DeviceIdType.MESH,
    )
    every.wait_recv()
    onward = pltpu.make_async_remote_copy(
        src_ref=buf.at[:, core],
        dst_ref=buf.at[:, core],
        send_sem=pass_send,
        recv_sem=pass_recv,
        device_id=sibling,
        device_id_type=pl.DeviceIdType.MESH,
    )
    onward.start()
    every.wait_send()
    onward.wait_send()
    onward.wait_recv()
    o_ref[...] = buf[...]


def pair_gather(x, collective_id):
    shape = (lax.axis_size("tp"), 2) + x.shape
    return pl.pallas_call(
        _pair_gather_kernel,
        out_shape=jax.ShapeDtypeStruct(shape, x.dtype),
        in_specs=[pl.BlockSpec(memory_space=pltpu.VMEM)],
        out_specs=pl.BlockSpec(memory_space=pltpu.VMEM),
        scratch_shapes=[pltpu.VMEM(shape, x.dtype)] + [pltpu.SemaphoreType.DMA(())] * 5,
        compiler_params=pltpu.CompilerParams(collective_id=collective_id, has_side_effects=True),
    )(x)


def pair_exchange(x, collective_id):
    return _transfer(x, "pair", False, collective_id)


def group_exchange(x, collective_id):
    return _transfer(x, "group", False, collective_id)


def tp_exchange(x, collective_id):
    return _transfer(x, "tp", False, collective_id)


def tp_gather(x, collective_id):
    return _transfer(x, "tp", True, collective_id)


def rotate(values, positions):
    half_dim = values.shape[-1] // 2
    inverse = THETA ** (-2.0 * jnp.arange(half_dim, dtype=jnp.float32) / values.shape[-1])
    angles = positions[:, None, None] * inverse[None, None, :]
    cosine = jnp.cos(angles)
    sine_part = jnp.sin(angles)
    first_part = values[..., :half_dim]
    second_part = values[..., half_dim:]
    return jnp.concatenate(
        [
            first_part * cosine - second_part * sine_part,
            second_part * cosine + first_part * sine_part,
        ],
        axis=-1,
    )


def attend(query_rows, kv_rows, cache_kv, cache_valid, sinks, length):
    block_len = query_rows.shape[0]
    kv_heads = kv_rows.shape[1] // (2 * HEAD)
    query_heads = query_rows.shape[1] // HEAD
    group_size = query_heads // kv_heads
    positions = (length + jnp.arange(block_len, dtype=jnp.int32)).astype(jnp.float32)
    query_rot = rotate(
        query_rows.astype(jnp.float32).reshape(block_len, query_heads, HEAD), positions
    ).astype(jnp.bfloat16)
    kv_parts = kv_rows.reshape(block_len, kv_heads, 2, HEAD)
    key_rot = rotate(kv_parts[:, :, 0].astype(jnp.float32), positions).astype(jnp.bfloat16)
    cache_parts = cache_kv.reshape(cache_kv.shape[0], kv_heads, 2, HEAD)
    all_keys = jnp.concatenate([cache_parts[:, :, 0], key_rot], axis=0)
    all_values = jnp.concatenate([cache_parts[:, :, 1], kv_parts[:, :, 1]], axis=0)
    token_order = jnp.arange(block_len, dtype=jnp.int32)
    causal = token_order[None, :] <= token_order[:, None]
    allowed = jnp.concatenate(
        [jnp.broadcast_to(cache_valid[None, :], (block_len, cache_valid.shape[0])), causal], axis=1
    )
    row_allowed = jnp.repeat(allowed, group_size, axis=0)
    score_scale = HEAD ** (-0.5)
    query_block = query_rot.reshape(block_len * group_size, HEAD)
    scores = (
        jnp.dot(query_block, all_keys[:, 0].T, preferred_element_type=jnp.float32) * score_scale
    )
    scores = jnp.where(row_allowed, scores, -jnp.inf)
    sink_rows = jnp.tile(sinks, block_len)
    row_max = jnp.maximum(jnp.max(scores, axis=1), sink_rows)
    weights = jnp.exp(scores - row_max[:, None])
    denominator = jnp.sum(weights, axis=1) + jnp.exp(sink_rows - row_max)
    blended = (
        jnp.dot(weights.astype(jnp.bfloat16), all_values[:, 0], preferred_element_type=jnp.float32)
        / denominator[:, None]
    )
    outputs = blended.astype(jnp.bfloat16).reshape(block_len, group_size * HEAD)
    return outputs


def on_device(
    queries,
    new_kv,
    local_cache,
    remote_pool,
    page_index,
    lengths,
    sinks,
    out_weight,
    residual,
    norm_gain,
    routes,
    route_weights,
    expert_gate,
    expert_up,
    expert_down,
):
    groups = lax.axis_size("group")
    lane_count = remote_pool.shape[1]
    local_len = local_cache.shape[0]
    fetched = group_exchange(remote_pool.reshape(groups, -1, lane_count), 1)
    page_len = fetched.shape[1]
    length = lengths[0]
    offsets = jnp.arange(page_len, dtype=jnp.int32)
    remote_pos = local_len + page_index[0][:, None] * page_len + offsets[None, :]
    cache_valid = jnp.concatenate(
        [jnp.ones((local_len,), jnp.bool_), (remote_pos < length).reshape(-1)]
    )
    cache_kv = jnp.concatenate([local_cache, fetched.reshape(-1, lane_count)], axis=0)
    attended = attend(queries, new_kv, cache_kv, cache_valid, sinks, length)
    width = residual.shape[1]
    tp_count = lax.axis_size("tp")
    start = lax.axis_index("tp") * width
    own_gain = lax.dynamic_slice_in_dim(norm_gain, start, width, 0)
    partial_sum = jnp.dot(attended, out_weight, preferred_element_type=jnp.float32)
    partial_blocks = partial_sum.reshape(partial_sum.shape[0], tp_count, width).transpose(1, 0, 2)
    own_attn = jnp.sum(tp_exchange(partial_blocks, 6), axis=0)
    own_state = own_attn + residual.astype(jnp.float32)
    square_sum = jnp.sum(own_state * own_state, axis=1, keepdims=True)
    square_high = square_sum.astype(jnp.bfloat16)
    square_low = (square_sum - square_high.astype(jnp.float32)).astype(jnp.bfloat16)
    row_width = -(-(width + 2) // 128) * 128
    scaled_own = (own_state * own_gain).astype(jnp.bfloat16)
    normed_own = jnp.concatenate(
        [scaled_own, square_high, square_low, jnp.zeros((own_state.shape[0], row_width - width - 2), jnp.bfloat16)],
        axis=1,
    )
    block_len = normed_own.shape[0]
    top_count = routes.shape[1]
    experts = groups // 2
    capacity = 5 * block_len * top_count // (4 * experts)
    member = jnp.any(
        routes[:, :, None] == jnp.arange(experts, dtype=jnp.int32)[None, None, :], axis=1
    ).astype(jnp.int32)
    slot_rank = jnp.cumsum(member, axis=0) - member
    slot_hit = member[:, :, None] * (
        slot_rank[:, :, None] == jnp.arange(capacity, dtype=jnp.int32)[None, None, :]
    ).astype(jnp.int32)
    slot_token = jnp.sum(slot_hit * jnp.arange(block_len, dtype=jnp.int32)[:, None, None], axis=0)
    slot_valid = jnp.sum(slot_hit, axis=0)
    send_own = jnp.take(normed_own, slot_token.reshape(-1), axis=0) * slot_valid.reshape(
        -1, 1
    ).astype(jnp.bfloat16)
    hidden_part = expert_gate.shape[2]
    gate_and_up = jnp.concatenate([expert_gate[0], expert_up[0]], axis=1)
    received = pair_exchange(send_own.reshape(experts, capacity, -1), 2)
    sources, slot_count, part_features = received.shape
    whole = pair_gather(received.reshape(sources * slot_count, part_features), 4)
    whole = whole.reshape(tp_count, 2 * sources * slot_count, part_features)
    gate_blocks = gate_and_up.reshape(tp_count, width, gate_and_up.shape[1])
    total_square = jnp.sum(whole[:, :, width:width + 2].astype(jnp.float32), axis=(0, 2))
    row_scale = lax.rsqrt(total_square / (width * tp_count) + EPSILON)
    both = jnp.einsum("tsf,tfh->sh", whole[:, :, :width], gate_blocks, preferred_element_type=jnp.float32)
    both = both * row_scale[:, None]
    gate_val = both[:, :hidden_part]
    up_val = both[:, hidden_part:]
    active = (gate_val * jax.nn.sigmoid(ALPHA * gate_val) * (up_val + 1.0)).astype(jnp.bfloat16)
    joined = tp_gather(active.T, 5)
    down_blocks = expert_down[0].reshape(tp_count, hidden_part, expert_down.shape[2])
    result = jnp.einsum("ths,thd->sd", joined, down_blocks, preferred_element_type=jnp.float32).astype(
        jnp.bfloat16
    )
    halves = result.reshape(2, experts, capacity, width)
    core = lax.rem(lax.axis_index("group"), 2)
    groups_total = lax.axis_size("group")
    swap = [(i, i + 1 - 2 * (i % 2)) for i in range(groups_total)]
    mine = lax.dynamic_index_in_dim(halves, core, 0, keepdims=False)
    theirs = lax.dynamic_index_in_dim(halves, 1 - core, 0, keepdims=False)
    other_half = lax.ppermute(theirs, "group", swap)
    joined_halves = (mine.astype(jnp.float32) + other_half.astype(jnp.float32)).astype(jnp.bfloat16)
    arrived = pair_exchange(joined_halves, 3)
    summed = arrived.astype(jnp.float32).reshape(experts * capacity, width)
    rank_at = jnp.take_along_axis(slot_rank, routes, axis=1)
    picked = jnp.take(summed, (routes * capacity + rank_at).reshape(-1), axis=0).reshape(
        block_len, top_count, width
    )
    mixing = route_weights / jnp.sum(route_weights, axis=1, keepdims=True)
    moe_out = jnp.sum(mixing[:, :, None] * picked, axis=1)
    return (own_state + moe_out).astype(jnp.bfloat16)


def solution(mesh):
    return jax.shard_map(
        on_device,
        mesh=mesh,
        in_specs=(
            P("group", "tp"),
            P("group", "tp"),
            P("group", "tp"),
            P("group", "tp"),
            P("group", None),
            P("group"),
            P("tp"),
            P("tp", None),
            P("group", "tp"),
            P(),
            P("group", None),
            P("group", None),
            P("group", None, "tp"),
            P("group", None, "tp"),
            P("group", None, "tp"),
        ),
        out_specs=P("group", "tp"),
        check_vma=False,
    )
```

```python
import functools

import jax
import jax.numpy as jnp
from jax import lax
from jax.experimental import pallas as pl
from jax.experimental.pallas import tpu as pltpu
from jax.sharding import PartitionSpec as P

HEAD = 64


THETA = 150000.0
ALPHA = 1.702
EPSILON = 1e-05


def _transfer_kernel(axis, gather, x_ref, o_ref, buf, send_sem, recv_sem, local_sem):
    count = buf.shape[0]
    group_at = lax.axis_index("group")
    tp_at = lax.axis_index("tp")
    core = lax.rem(group_at, 2)
    if axis == "tp":
        me = tp_at
    elif axis == "pair":
        me = lax.div(group_at, 2)
    else:
        me = group_at

    def device(peer):
        if axis == "tp":
            return (group_at, peer)
        if axis == "pair":
            return (2 * peer + core, tp_at)
        return (peer, tp_at)

    def piece(peer):
        return x_ref if gather else x_ref.at[peer]

    barrier = pltpu.get_barrier_semaphore()

    def greet(step, carry):
        peer = lax.rem(me + step, count)
        pl.semaphore_signal(barrier, inc=1, device_id=device(peer), device_id_type=pl.DeviceIdType.MESH)
        return carry

    lax.fori_loop(1, count, greet, 0)
    pl.semaphore_wait(barrier, count - 1)
    local = pltpu.make_async_copy(piece(me), buf.at[me], local_sem)
    local.start()

    def send(step, carry):
        peer = lax.rem(me + step, count)
        pltpu.make_async_remote_copy(
            src_ref=piece(peer),
            dst_ref=buf.at[me],
            send_sem=send_sem,
            recv_sem=recv_sem,
            device_id=device(peer),
            device_id_type=pl.DeviceIdType.MESH,
        ).start()
        return carry

    lax.fori_loop(1, count, send, 0)
    local.wait()
    every = pltpu.make_async_remote_copy(
        src_ref=buf.at[pl.ds(0, count - 1)],
        dst_ref=buf.at[pl.ds(0, count - 1)],
        send_sem=send_sem,
        recv_sem=recv_sem,
        device_id=device(lax.rem(me + 1, count)),
        device_id_type=pl.DeviceIdType.MESH,
    )
    every.wait_send()
    every.wait_recv()
    o_ref[...] = buf[...]


def _transfer(x, axis, gather, collective_id):
    count = lax.axis_size("group") // 2 if axis == "pair" else lax.axis_size(axis)
    shape = ((count,) + x.shape) if gather else x.shape
    return pl.pallas_call(
        functools.partial(_transfer_kernel, axis, gather),
        out_shape=jax.ShapeDtypeStruct(shape, x.dtype),
        in_specs=[pl.BlockSpec(memory_space=pltpu.VMEM)],
        out_specs=pl.BlockSpec(memory_space=pltpu.VMEM),
        scratch_shapes=[
            pltpu.VMEM(shape, x.dtype),
            pltpu.SemaphoreType.DMA(()),
            pltpu.SemaphoreType.DMA(()),
            pltpu.SemaphoreType.DMA(()),
        ],
        compiler_params=pltpu.CompilerParams(collective_id=collective_id, has_side_effects=True),
    )(x)


def _pair_gather_kernel(x_ref, o_ref, buf, send_sem, recv_sem, local_sem, pass_send, pass_recv):
    count = buf.shape[0]
    group_at = lax.axis_index("group")
    tp_at = lax.axis_index("tp")
    core = lax.rem(group_at, 2)
    sibling = (group_at + 1 - 2 * core, tp_at)
    barrier = pltpu.get_barrier_semaphore()

    def greet(step, carry):
        peer = lax.rem(tp_at + step, count)
        pl.semaphore_signal(barrier, inc=1, device_id=(group_at, peer), device_id_type=pl.DeviceIdType.MESH)
        return carry

    lax.fori_loop(1, count, greet, 0)
    pl.semaphore_signal(barrier, inc=1, device_id=sibling, device_id_type=pl.DeviceIdType.MESH)
    pl.semaphore_wait(barrier, count)
    local = pltpu.make_async_copy(x_ref, buf.at[tp_at, core], local_sem)
    local.start()

    def send(step, carry):
        peer = lax.rem(tp_at + step, count)
        pltpu.make_async_remote_copy(
            src_ref=x_ref,
            dst_ref=buf.at[tp_at, core],
            send_sem=send_sem,
            recv_sem=recv_sem,
            device_id=(group_at, peer),
            device_id_type=pl.DeviceIdType.MESH,
        ).start()
        return carry

    lax.fori_loop(1, count, send, 0)
    local.wait()
    every = pltpu.make_async_remote_copy(
        src_ref=buf.at[pl.ds(0, count - 1), 0],
        dst_ref=buf.at[pl.ds(0, count - 1), 0],
        send_sem=send_sem,
        recv_sem=recv_sem,
        device_id=(group_at, lax.rem(tp_at + 1, count)),
        device_id_type=pl.DeviceIdType.MESH,
    )
    every.wait_recv()
    onward = pltpu.make_async_remote_copy(
        src_ref=buf.at[:, core],
        dst_ref=buf.at[:, core],
        send_sem=pass_send,
        recv_sem=pass_recv,
        device_id=sibling,
        device_id_type=pl.DeviceIdType.MESH,
    )
    onward.start()
    every.wait_send()
    onward.wait_send()
    onward.wait_recv()
    o_ref[...] = buf[...]


def pair_gather(x, collective_id):
    shape = (lax.axis_size("tp"), 2) + x.shape
    return pl.pallas_call(
        _pair_gather_kernel,
        out_shape=jax.ShapeDtypeStruct(shape, x.dtype),
        in_specs=[pl.BlockSpec(memory_space=pltpu.VMEM)],
        out_specs=pl.BlockSpec(memory_space=pltpu.VMEM),
        scratch_shapes=[pltpu.VMEM(shape, x.dtype)] + [pltpu.SemaphoreType.DMA(())] * 5,
        compiler_params=pltpu.CompilerParams(collective_id=collective_id, has_side_effects=True),
    )(x)


def pair_exchange(x, collective_id):
    return _transfer(x, "pair", False, collective_id)


def group_exchange(x, collective_id):
    return _transfer(x, "group", False, collective_id)


def tp_exchange(x, collective_id):
    return _transfer(x, "tp", False, collective_id)


def tp_gather(x, collective_id):
    return _transfer(x, "tp", True, collective_id)


def rotate(values, positions):
    half_dim = values.shape[-1] // 2
    inverse = THETA ** (-2.0 * jnp.arange(half_dim, dtype=jnp.float32) / values.shape[-1])
    angles = positions[:, None, None] * inverse[None, None, :]
    cosine = jnp.cos(angles)
    sine_part = jnp.sin(angles)
    first_part = values[..., :half_dim]
    second_part = values[..., half_dim:]
    return jnp.concatenate(
        [
            first_part * cosine - second_part * sine_part,
            second_part * cosine + first_part * sine_part,
        ],
        axis=-1,
    )


def attend(query_rows, kv_rows, cache_kv, cache_valid, sinks, length):
    block_len = query_rows.shape[0]
    kv_heads = kv_rows.shape[1] // (2 * HEAD)
    query_heads = query_rows.shape[1] // HEAD
    group_size = query_heads // kv_heads
    positions = (length + jnp.arange(block_len, dtype=jnp.int32)).astype(jnp.float32)
    query_rot = rotate(
        query_rows.astype(jnp.float32).reshape(block_len, query_heads, HEAD), positions
    ).astype(jnp.bfloat16)
    kv_parts = kv_rows.reshape(block_len, kv_heads, 2, HEAD)
    key_rot = rotate(kv_parts[:, :, 0].astype(jnp.float32), positions).astype(jnp.bfloat16)
    cache_parts = cache_kv.reshape(cache_kv.shape[0], kv_heads, 2, HEAD)
    all_keys = jnp.concatenate([cache_parts[:, :, 0], key_rot], axis=0)
    all_values = jnp.concatenate([cache_parts[:, :, 1], kv_parts[:, :, 1]], axis=0)
    token_order = jnp.arange(block_len, dtype=jnp.int32)
    causal = token_order[None, :] <= token_order[:, None]
    allowed = jnp.concatenate(
        [jnp.broadcast_to(cache_valid[None, :], (block_len, cache_valid.shape[0])), causal], axis=1
    )
    row_allowed = jnp.repeat(allowed, group_size, axis=0)
    score_scale = HEAD ** (-0.5)
    query_block = query_rot.reshape(block_len * group_size, HEAD)
    scores = (
        jnp.dot(query_block, all_keys[:, 0].T, preferred_element_type=jnp.float32) * score_scale
    )
    scores = jnp.where(row_allowed, scores, -jnp.inf)
    sink_rows = jnp.tile(sinks, block_len)
    row_max = jnp.maximum(jnp.max(scores, axis=1), sink_rows)
    weights = jnp.exp(scores - row_max[:, None])
    denominator = jnp.sum(weights, axis=1) + jnp.exp(sink_rows - row_max)
    blended = (
        jnp.dot(weights.astype(jnp.bfloat16), all_values[:, 0], preferred_element_type=jnp.float32)
        / denominator[:, None]
    )
    outputs = blended.astype(jnp.bfloat16).reshape(block_len, group_size * HEAD)
    return outputs


def lane_dense(rows):
    count, length = rows.shape
    padded = -(-length // 128) * 128
    rows = jnp.pad(rows, ((0, 0), (0, padded - length)))
    return rows.reshape(count, padded // 128, 128)


def on_device(
    queries,
    new_kv,
    local_cache,
    remote_pool,
    page_index,
    lengths,
    sinks,
    out_weight,
    residual,
    norm_gain,
    routes,
    route_weights,
    expert_gate,
    expert_up,
    expert_down,
):
    groups = lax.axis_size("group")
    lane_count = remote_pool.shape[1]
    local_len = local_cache.shape[0]
    fetched = group_exchange(remote_pool.reshape(groups, -1, lane_count), 1)
    page_len = fetched.shape[1]
    length = lengths[0]
    offsets = jnp.arange(page_len, dtype=jnp.int32)
    remote_pos = local_len + page_index[0][:, None] * page_len + offsets[None, :]
    cache_valid = jnp.concatenate(
        [jnp.ones((local_len,), jnp.bool_), (remote_pos < length).reshape(-1)]
    )
    cache_kv = jnp.concatenate([local_cache, fetched.reshape(-1, lane_count)], axis=0)
    attended = attend(queries, new_kv, cache_kv, cache_valid, sinks, length)
    width = residual.shape[1]
    tp_count = lax.axis_size("tp")
    start = lax.axis_index("tp") * width
    own_gain = lax.dynamic_slice_in_dim(norm_gain, start, width, 0)
    partial_sum = jnp.dot(attended, out_weight, preferred_element_type=jnp.float32)
    partial_blocks = partial_sum.reshape(partial_sum.shape[0], tp_count, width).transpose(1, 0, 2)
    own_attn = jnp.sum(tp_exchange(partial_blocks, 6), axis=0)
    own_state = own_attn + residual.astype(jnp.float32)
    square_sum = jnp.sum(own_state * own_state, axis=1, keepdims=True)
    square_high = square_sum.astype(jnp.bfloat16)
    square_low = (square_sum - square_high.astype(jnp.float32)).astype(jnp.bfloat16)
    row_width = -(-(width + 2) // 128) * 128
    scaled_own = (own_state * own_gain).astype(jnp.bfloat16)
    normed_own = jnp.concatenate(
        [scaled_own, square_high, square_low, jnp.zeros((own_state.shape[0], row_width - width - 2), jnp.bfloat16)],
        axis=1,
    )
    block_len = normed_own.shape[0]
    top_count = routes.shape[1]
    experts = groups // 2
    capacity = 5 * block_len * top_count // (4 * experts)
    member = jnp.any(
        routes[:, :, None] == jnp.arange(experts, dtype=jnp.int32)[None, None, :], axis=1
    ).astype(jnp.int32)
    slot_rank = jnp.cumsum(member, axis=0) - member
    slot_hit = member[:, :, None] * (
        slot_rank[:, :, None] == jnp.arange(capacity, dtype=jnp.int32)[None, None, :]
    ).astype(jnp.int32)
    slot_token = jnp.sum(slot_hit * jnp.arange(block_len, dtype=jnp.int32)[:, None, None], axis=0)
    slot_valid = jnp.sum(slot_hit, axis=0)
    send_own = jnp.take(normed_own, slot_token.reshape(-1), axis=0) * slot_valid.reshape(
        -1, 1
    ).astype(jnp.bfloat16)
    hidden_part = expert_gate.shape[2]
    gate_and_up = jnp.concatenate([expert_gate[0], expert_up[0]], axis=1)
    row_width = send_own.shape[1]
    received = pair_exchange(lane_dense(send_own.reshape(experts, capacity * row_width)), 2)
    received = received.reshape(experts, -1)[:, : capacity * row_width].reshape(experts, capacity, row_width)
    sources, slot_count, part_features = received.shape
    whole = pair_gather(received.reshape(sources * slot_count, part_features), 4)
    whole = whole.reshape(tp_count, 2 * sources * slot_count, part_features)
    gate_blocks = gate_and_up.reshape(tp_count, width, gate_and_up.shape[1])
    total_square = jnp.sum(whole[:, :, width:width + 2].astype(jnp.float32), axis=(0, 2))
    row_scale = lax.rsqrt(total_square / (width * tp_count) + EPSILON)
    both = jnp.einsum("tsf,tfh->sh", whole[:, :, :width], gate_blocks, preferred_element_type=jnp.float32)
    both = both * row_scale[:, None]
    gate_val = both[:, :hidden_part]
    up_val = both[:, hidden_part:]
    active = (gate_val * jax.nn.sigmoid(ALPHA * gate_val) * (up_val + 1.0)).astype(jnp.bfloat16)
    joined = tp_gather(active.T, 5)
    down_blocks = expert_down[0].reshape(tp_count, hidden_part, expert_down.shape[2])
    result = jnp.einsum("ths,thd->sd", joined, down_blocks, preferred_element_type=jnp.float32).astype(
        jnp.bfloat16
    )
    halves = result.reshape(2, experts, capacity, width)
    core = lax.rem(lax.axis_index("group"), 2)
    groups_total = lax.axis_size("group")
    swap = [(i, i + 1 - 2 * (i % 2)) for i in range(groups_total)]
    mine = lax.dynamic_index_in_dim(halves, core, 0, keepdims=False)
    theirs = lax.dynamic_index_in_dim(halves, 1 - core, 0, keepdims=False)
    other_half = lax.ppermute(theirs, "group", swap)
    joined_halves = (mine.astype(jnp.float32) + other_half.astype(jnp.float32)).astype(jnp.bfloat16)
    arrived = pair_exchange(lane_dense(joined_halves.reshape(experts, capacity * width)), 3)
    summed = arrived.reshape(experts, -1)[:, : capacity * width].astype(jnp.float32).reshape(experts * capacity, width)
    rank_at = jnp.take_along_axis(slot_rank, routes, axis=1)
    picked = jnp.take(summed, (routes * capacity + rank_at).reshape(-1), axis=0).reshape(
        block_len, top_count, width
    )
    mixing = route_weights / jnp.sum(route_weights, axis=1, keepdims=True)
    moe_out = jnp.sum(mixing[:, :, None] * picked, axis=1)
    return (own_state + moe_out).astype(jnp.bfloat16)


def solution(mesh):
    return jax.shard_map(
        on_device,
        mesh=mesh,
        in_specs=(
            P("group", "tp"),
            P("group", "tp"),
            P("group", "tp"),
            P("group", "tp"),
            P("group", None),
            P("group"),
            P("tp"),
            P("tp", None),
            P("group", "tp"),
            P(),
            P("group", None),
            P("group", None),
            P("group", None, "tp"),
            P("group", None, "tp"),
            P("group", None, "tp"),
        ),
        out_specs=P("group", "tp"),
        check_vma=False,
    )
```

```python
import functools

import jax
import jax.numpy as jnp
from jax import lax
from jax.experimental import pallas as pl
from jax.experimental.pallas import tpu as pltpu
from jax.sharding import PartitionSpec as P

HEAD = 64


THETA = 150000.0
ALPHA = 1.702
EPSILON = 1e-05


def _transfer_kernel(axis, gather, x_ref, o_ref, buf, send_sem, recv_sem, local_sem):
    count = buf.shape[0]
    group_at = lax.axis_index("group")
    tp_at = lax.axis_index("tp")
    core = lax.rem(group_at, 2)
    if axis == "tp":
        me = tp_at
    elif axis == "pair":
        me = lax.div(group_at, 2)
    else:
        me = group_at

    def device(peer):
        if axis == "tp":
            return (group_at, peer)
        if axis == "pair":
            return (2 * peer + core, tp_at)
        return (peer, tp_at)

    def piece(peer):
        return x_ref if gather else x_ref.at[peer]

    barrier = pltpu.get_barrier_semaphore()

    def greet(step, carry):
        peer = lax.rem(me + step, count)
        pl.semaphore_signal(barrier, inc=1, device_id=device(peer), device_id_type=pl.DeviceIdType.MESH)
        return carry

    lax.fori_loop(1, count, greet, 0)
    pl.semaphore_wait(barrier, count - 1)
    local = pltpu.make_async_copy(piece(me), buf.at[me], local_sem)
    local.start()

    def send(step, carry):
        peer = lax.rem(me + step, count)
        pltpu.make_async_remote_copy(
            src_ref=piece(peer),
            dst_ref=buf.at[me],
            send_sem=send_sem,
            recv_sem=recv_sem,
            device_id=device(peer),
            device_id_type=pl.DeviceIdType.MESH,
        ).start()
        return carry

    lax.fori_loop(1, count, send, 0)
    local.wait()
    every = pltpu.make_async_remote_copy(
        src_ref=buf.at[pl.ds(0, count - 1)],
        dst_ref=buf.at[pl.ds(0, count - 1)],
        send_sem=send_sem,
        recv_sem=recv_sem,
        device_id=device(lax.rem(me + 1, count)),
        device_id_type=pl.DeviceIdType.MESH,
    )
    every.wait_send()
    every.wait_recv()
    o_ref[...] = buf[...]


def _transfer(x, axis, gather, collective_id):
    count = lax.axis_size("group") // 2 if axis == "pair" else lax.axis_size(axis)
    shape = ((count,) + x.shape) if gather else x.shape
    return pl.pallas_call(
        functools.partial(_transfer_kernel, axis, gather),
        out_shape=jax.ShapeDtypeStruct(shape, x.dtype),
        in_specs=[pl.BlockSpec(memory_space=pltpu.VMEM)],
        out_specs=pl.BlockSpec(memory_space=pltpu.VMEM),
        scratch_shapes=[
            pltpu.VMEM(shape, x.dtype),
            pltpu.SemaphoreType.DMA(()),
            pltpu.SemaphoreType.DMA(()),
            pltpu.SemaphoreType.DMA(()),
        ],
        compiler_params=pltpu.CompilerParams(collective_id=collective_id, has_side_effects=True),
    )(x)


def _pair_gather_kernel(x_ref, o_ref, buf, send_sem, recv_sem, local_sem, pass_send, pass_recv):
    count = buf.shape[0]
    group_at = lax.axis_index("group")
    tp_at = lax.axis_index("tp")
    core = lax.rem(group_at, 2)
    sibling = (group_at + 1 - 2 * core, tp_at)
    barrier = pltpu.get_barrier_semaphore()

    def greet(step, carry):
        peer = lax.rem(tp_at + step, count)
        pl.semaphore_signal(barrier, inc=1, device_id=(group_at, peer), device_id_type=pl.DeviceIdType.MESH)
        return carry

    lax.fori_loop(1, count, greet, 0)
    pl.semaphore_signal(barrier, inc=1, device_id=sibling, device_id_type=pl.DeviceIdType.MESH)
    pl.semaphore_wait(barrier, count)
    local = pltpu.make_async_copy(x_ref, buf.at[tp_at, core], local_sem)
    local.start()

    def send(step, carry):
        peer = lax.rem(tp_at + step, count)
        pltpu.make_async_remote_copy(
            src_ref=x_ref,
            dst_ref=buf.at[tp_at, core],
            send_sem=send_sem,
            recv_sem=recv_sem,
            device_id=(group_at, peer),
            device_id_type=pl.DeviceIdType.MESH,
        ).start()
        return carry

    lax.fori_loop(1, count, send, 0)
    local.wait()
    every = pltpu.make_async_remote_copy(
        src_ref=buf.at[pl.ds(0, count - 1), 0],
        dst_ref=buf.at[pl.ds(0, count - 1), 0],
        send_sem=send_sem,
        recv_sem=recv_sem,
        device_id=(group_at, lax.rem(tp_at + 1, count)),
        device_id_type=pl.DeviceIdType.MESH,
    )
    every.wait_recv()
    onward = pltpu.make_async_remote_copy(
        src_ref=buf.at[:, core],
        dst_ref=buf.at[:, core],
        send_sem=pass_send,
        recv_sem=pass_recv,
        device_id=sibling,
        device_id_type=pl.DeviceIdType.MESH,
    )
    onward.start()
    every.wait_send()
    onward.wait_send()
    onward.wait_recv()
    o_ref[...] = buf[...]


def pair_gather(x, collective_id):
    shape = (lax.axis_size("tp"), 2) + x.shape
    return pl.pallas_call(
        _pair_gather_kernel,
        out_shape=jax.ShapeDtypeStruct(shape, x.dtype),
        in_specs=[pl.BlockSpec(memory_space=pltpu.VMEM)],
        out_specs=pl.BlockSpec(memory_space=pltpu.VMEM),
        scratch_shapes=[pltpu.VMEM(shape, x.dtype)] + [pltpu.SemaphoreType.DMA(())] * 5,
        compiler_params=pltpu.CompilerParams(collective_id=collective_id, has_side_effects=True),
    )(x)


def pair_exchange(x, collective_id):
    return _transfer(x, "pair", False, collective_id)


def group_exchange(x, collective_id):
    return _transfer(x, "group", False, collective_id)


def tp_exchange(x, collective_id):
    return _transfer(x, "tp", False, collective_id)


def tp_gather(x, collective_id):
    return _transfer(x, "tp", True, collective_id)


def rotate(values, positions):
    half_dim = values.shape[-1] // 2
    inverse = THETA ** (-2.0 * jnp.arange(half_dim, dtype=jnp.float32) / values.shape[-1])
    angles = positions[:, None, None] * inverse[None, None, :]
    cosine = jnp.cos(angles)
    sine_part = jnp.sin(angles)
    first_part = values[..., :half_dim]
    second_part = values[..., half_dim:]
    return jnp.concatenate(
        [
            first_part * cosine - second_part * sine_part,
            second_part * cosine + first_part * sine_part,
        ],
        axis=-1,
    )


def attend(query_rows, kv_rows, cache_kv, cache_valid, sinks, length):
    block_len = query_rows.shape[0]
    kv_heads = kv_rows.shape[1] // (2 * HEAD)
    query_heads = query_rows.shape[1] // HEAD
    group_size = query_heads // kv_heads
    positions = (length + jnp.arange(block_len, dtype=jnp.int32)).astype(jnp.float32)
    query_rot = rotate(
        query_rows.astype(jnp.float32).reshape(block_len, query_heads, HEAD), positions
    ).astype(jnp.bfloat16)
    kv_parts = kv_rows.reshape(block_len, kv_heads, 2, HEAD)
    key_rot = rotate(kv_parts[:, :, 0].astype(jnp.float32), positions).astype(jnp.bfloat16)
    cache_parts = cache_kv.reshape(cache_kv.shape[0], kv_heads, 2, HEAD)
    all_keys = jnp.concatenate([cache_parts[:, :, 0], key_rot], axis=0)
    all_values = jnp.concatenate([cache_parts[:, :, 1], kv_parts[:, :, 1]], axis=0)
    token_order = jnp.arange(block_len, dtype=jnp.int32)
    causal = token_order[None, :] <= token_order[:, None]
    allowed = jnp.concatenate(
        [jnp.broadcast_to(cache_valid[None, :], (block_len, cache_valid.shape[0])), causal], axis=1
    )
    row_allowed = jnp.repeat(allowed, group_size, axis=0)
    score_scale = HEAD ** (-0.5)
    query_block = query_rot.reshape(block_len * group_size, HEAD)
    scores = (
        jnp.dot(query_block, all_keys[:, 0].T, preferred_element_type=jnp.float32) * score_scale
    )
    scores = jnp.where(row_allowed, scores, -jnp.inf)
    sink_rows = jnp.tile(sinks, block_len)
    row_max = jnp.maximum(jnp.max(scores, axis=1), sink_rows)
    weights = jnp.exp(scores - row_max[:, None])
    denominator = jnp.sum(weights, axis=1) + jnp.exp(sink_rows - row_max)
    blended = (
        jnp.dot(weights.astype(jnp.bfloat16), all_values[:, 0], preferred_element_type=jnp.float32)
        / denominator[:, None]
    )
    outputs = blended.astype(jnp.bfloat16).reshape(block_len, group_size * HEAD)
    return outputs


def lane_dense(rows):
    count, length = rows.shape
    padded = -(-length // 128) * 128
    rows = jnp.pad(rows, ((0, 0), (0, padded - length)))
    return rows.reshape(count, padded // 128, 128)


def on_device(
    queries,
    new_kv,
    local_cache,
    remote_pool,
    page_index,
    lengths,
    sinks,
    out_weight,
    residual,
    norm_gain,
    routes,
    route_weights,
    expert_gate,
    expert_up,
    expert_down,
):
    groups = lax.axis_size("group")
    lane_count = remote_pool.shape[1]
    local_len = local_cache.shape[0]
    fetched = group_exchange(remote_pool.reshape(groups, -1, lane_count), 1)
    page_len = fetched.shape[1]
    length = lengths[0]
    offsets = jnp.arange(page_len, dtype=jnp.int32)
    remote_pos = local_len + page_index[0][:, None] * page_len + offsets[None, :]
    cache_valid = jnp.concatenate(
        [jnp.ones((local_len,), jnp.bool_), (remote_pos < length).reshape(-1)]
    )
    cache_kv = jnp.concatenate([local_cache, fetched.reshape(-1, lane_count)], axis=0)
    attended = attend(queries, new_kv, cache_kv, cache_valid, sinks, length)
    width = residual.shape[1]
    tp_count = lax.axis_size("tp")
    start = lax.axis_index("tp") * width
    own_gain = lax.dynamic_slice_in_dim(norm_gain, start, width, 0)
    partial_sum = jnp.dot(attended, out_weight, preferred_element_type=jnp.float32)
    partial_blocks = partial_sum.reshape(partial_sum.shape[0], tp_count, width).transpose(1, 0, 2)
    own_attn = jnp.sum(tp_exchange(partial_blocks.astype(jnp.bfloat16), 6).astype(jnp.float32), axis=0)
    own_state = own_attn + residual.astype(jnp.float32)
    square_sum = jnp.sum(own_state * own_state, axis=1, keepdims=True)
    square_high = square_sum.astype(jnp.bfloat16)
    square_low = (square_sum - square_high.astype(jnp.float32)).astype(jnp.bfloat16)
    row_width = -(-(width + 2) // 128) * 128
    scaled_own = (own_state * own_gain).astype(jnp.bfloat16)
    normed_own = jnp.concatenate(
        [scaled_own, square_high, square_low, jnp.zeros((own_state.shape[0], row_width - width - 2), jnp.bfloat16)],
        axis=1,
    )
    block_len = normed_own.shape[0]
    top_count = routes.shape[1]
    experts = groups // 2
    capacity = 5 * block_len * top_count // (4 * experts)
    member = jnp.any(
        routes[:, :, None] == jnp.arange(experts, dtype=jnp.int32)[None, None, :], axis=1
    ).astype(jnp.int32)
    slot_rank = jnp.cumsum(member, axis=0) - member
    slot_hit = member[:, :, None] * (
        slot_rank[:, :, None] == jnp.arange(capacity, dtype=jnp.int32)[None, None, :]
    ).astype(jnp.int32)
    slot_token = jnp.sum(slot_hit * jnp.arange(block_len, dtype=jnp.int32)[:, None, None], axis=0)
    slot_valid = jnp.sum(slot_hit, axis=0)
    send_own = jnp.take(normed_own, slot_token.reshape(-1), axis=0) * slot_valid.reshape(
        -1, 1
    ).astype(jnp.bfloat16)
    hidden_part = expert_gate.shape[2]
    gate_and_up = jnp.concatenate([expert_gate[0], expert_up[0]], axis=1)
    row_width = send_own.shape[1]
    received = pair_exchange(lane_dense(send_own.reshape(experts, capacity * row_width)), 2)
    received = received.reshape(experts, -1)[:, : capacity * row_width].reshape(experts, capacity, row_width)
    sources, slot_count, part_features = received.shape
    whole = pair_gather(received.reshape(sources * slot_count, part_features), 4)
    whole = whole.reshape(tp_count, 2 * sources * slot_count, part_features)
    gate_blocks = gate_and_up.reshape(tp_count, width, gate_and_up.shape[1])
    total_square = jnp.sum(whole[:, :, width:width + 2].astype(jnp.float32), axis=(0, 2))
    row_scale = lax.rsqrt(total_square / (width * tp_count) + EPSILON)
    both = jnp.einsum("tsf,tfh->sh", whole[:, :, :width], gate_blocks, preferred_element_type=jnp.float32)
    both = both * row_scale[:, None]
    gate_val = both[:, :hidden_part]
    up_val = both[:, hidden_part:]
    active = (gate_val * jax.nn.sigmoid(ALPHA * gate_val) * (up_val + 1.0)).astype(jnp.bfloat16)
    joined = tp_gather(active.T, 5)
    down_blocks = expert_down[0].reshape(tp_count, hidden_part, expert_down.shape[2])
    result = jnp.einsum("ths,thd->sd", joined, down_blocks, preferred_element_type=jnp.float32).astype(
        jnp.bfloat16
    )
    halves = result.reshape(2, experts, capacity, width)
    core = lax.rem(lax.axis_index("group"), 2)
    groups_total = lax.axis_size("group")
    swap = [(i, i + 1 - 2 * (i % 2)) for i in range(groups_total)]
    mine = lax.dynamic_index_in_dim(halves, core, 0, keepdims=False)
    theirs = lax.dynamic_index_in_dim(halves, 1 - core, 0, keepdims=False)
    other_half = lax.ppermute(theirs, "group", swap)
    joined_halves = (mine.astype(jnp.float32) + other_half.astype(jnp.float32)).astype(jnp.bfloat16)
    arrived = pair_exchange(lane_dense(joined_halves.reshape(experts, capacity * width)), 3)
    summed = arrived.reshape(experts, -1)[:, : capacity * width].astype(jnp.float32).reshape(experts * capacity, width)
    rank_at = jnp.take_along_axis(slot_rank, routes, axis=1)
    picked = jnp.take(summed, (routes * capacity + rank_at).reshape(-1), axis=0).reshape(
        block_len, top_count, width
    )
    mixing = route_weights / jnp.sum(route_weights, axis=1, keepdims=True)
    moe_out = jnp.sum(mixing[:, :, None] * picked, axis=1)
    return (own_state + moe_out).astype(jnp.bfloat16)


def solution(mesh):
    return jax.shard_map(
        on_device,
        mesh=mesh,
        in_specs=(
            P("group", "tp"),
            P("group", "tp"),
            P("group", "tp"),
            P("group", "tp"),
            P("group", None),
            P("group"),
            P("tp"),
            P("tp", None),
            P("group", "tp"),
            P(),
            P("group", None),
            P("group", None),
            P("group", None, "tp"),
            P("group", None, "tp"),
            P("group", None, "tp"),
        ),
        out_specs=P("group", "tp"),
        check_vma=False,
    )
```

```python
import functools

import jax
import jax.numpy as jnp
from jax import lax
from jax.experimental import pallas as pl
from jax.experimental.pallas import tpu as pltpu
from jax.sharding import PartitionSpec as P

HEAD = 64


THETA = 150000.0
ALPHA = 1.702
EPSILON = 1e-05


def _transfer_kernel(axis, gather, x_ref, o_ref, buf, send_sem, recv_sem, local_sem):
    count = buf.shape[0]
    group_at = lax.axis_index("group")
    tp_at = lax.axis_index("tp")
    core = lax.rem(group_at, 2)
    if axis == "tp":
        me = tp_at
    elif axis == "pair":
        me = lax.div(group_at, 2)
    else:
        me = group_at

    def device(peer):
        if axis == "tp":
            return (group_at, peer)
        if axis == "pair":
            return (2 * peer + core, tp_at)
        return (peer, tp_at)

    def piece(peer):
        return x_ref if gather else x_ref.at[peer]

    barrier = pltpu.get_barrier_semaphore()

    def greet(step, carry):
        peer = lax.rem(me + step, count)
        pl.semaphore_signal(barrier, inc=1, device_id=device(peer), device_id_type=pl.DeviceIdType.MESH)
        return carry

    lax.fori_loop(1, count, greet, 0)
    pl.semaphore_wait(barrier, count - 1)
    local = pltpu.make_async_copy(piece(me), buf.at[me], local_sem)
    local.start()

    def send(step, carry):
        peer = lax.rem(me + step, count)
        pltpu.make_async_remote_copy(
            src_ref=piece(peer),
            dst_ref=buf.at[me],
            send_sem=send_sem,
            recv_sem=recv_sem,
            device_id=device(peer),
            device_id_type=pl.DeviceIdType.MESH,
        ).start()
        return carry

    lax.fori_loop(1, count, send, 0)
    local.wait()
    every = pltpu.make_async_remote_copy(
        src_ref=buf.at[pl.ds(0, count - 1)],
        dst_ref=buf.at[pl.ds(0, count - 1)],
        send_sem=send_sem,
        recv_sem=recv_sem,
        device_id=device(lax.rem(me + 1, count)),
        device_id_type=pl.DeviceIdType.MESH,
    )
    every.wait_send()
    every.wait_recv()
    o_ref[...] = buf[...]


def _transfer(x, axis, gather, collective_id):
    count = lax.axis_size("group") // 2 if axis == "pair" else lax.axis_size(axis)
    shape = ((count,) + x.shape) if gather else x.shape
    return pl.pallas_call(
        functools.partial(_transfer_kernel, axis, gather),
        out_shape=jax.ShapeDtypeStruct(shape, x.dtype),
        in_specs=[pl.BlockSpec(memory_space=pltpu.VMEM)],
        out_specs=pl.BlockSpec(memory_space=pltpu.VMEM),
        scratch_shapes=[
            pltpu.VMEM(shape, x.dtype),
            pltpu.SemaphoreType.DMA(()),
            pltpu.SemaphoreType.DMA(()),
            pltpu.SemaphoreType.DMA(()),
        ],
        compiler_params=pltpu.CompilerParams(collective_id=collective_id, has_side_effects=True),
    )(x)


def _pair_gather_kernel(x_ref, o_ref, buf, send_sem, recv_sem, local_sem, pass_send, pass_recv):
    count = buf.shape[0]
    group_at = lax.axis_index("group")
    tp_at = lax.axis_index("tp")
    core = lax.rem(group_at, 2)
    sibling = (group_at + 1 - 2 * core, tp_at)
    barrier = pltpu.get_barrier_semaphore()

    def greet(step, carry):
        peer = lax.rem(tp_at + step, count)
        pl.semaphore_signal(barrier, inc=1, device_id=(group_at, peer), device_id_type=pl.DeviceIdType.MESH)
        return carry

    lax.fori_loop(1, count, greet, 0)
    pl.semaphore_signal(barrier, inc=1, device_id=sibling, device_id_type=pl.DeviceIdType.MESH)
    pl.semaphore_wait(barrier, count)
    local = pltpu.make_async_copy(x_ref, buf.at[tp_at, core], local_sem)
    local.start()

    def send(step, carry):
        peer = lax.rem(tp_at + step, count)
        pltpu.make_async_remote_copy(
            src_ref=x_ref,
            dst_ref=buf.at[tp_at, core],
            send_sem=send_sem,
            recv_sem=recv_sem,
            device_id=(group_at, peer),
            device_id_type=pl.DeviceIdType.MESH,
        ).start()
        return carry

    lax.fori_loop(1, count, send, 0)
    local.wait()
    every = pltpu.make_async_remote_copy(
        src_ref=buf.at[pl.ds(0, count - 1), 0],
        dst_ref=buf.at[pl.ds(0, count - 1), 0],
        send_sem=send_sem,
        recv_sem=recv_sem,
        device_id=(group_at, lax.rem(tp_at + 1, count)),
        device_id_type=pl.DeviceIdType.MESH,
    )
    every.wait_recv()
    onward = pltpu.make_async_remote_copy(
        src_ref=buf.at[:, core],
        dst_ref=buf.at[:, core],
        send_sem=pass_send,
        recv_sem=pass_recv,
        device_id=sibling,
        device_id_type=pl.DeviceIdType.MESH,
    )
    onward.start()
    every.wait_send()
    onward.wait_send()
    onward.wait_recv()
    o_ref[...] = buf[...]


def pair_gather(x, collective_id):
    shape = (lax.axis_size("tp"), 2) + x.shape
    return pl.pallas_call(
        _pair_gather_kernel,
        out_shape=jax.ShapeDtypeStruct(shape, x.dtype),
        in_specs=[pl.BlockSpec(memory_space=pltpu.VMEM)],
        out_specs=pl.BlockSpec(memory_space=pltpu.VMEM),
        scratch_shapes=[pltpu.VMEM(shape, x.dtype)] + [pltpu.SemaphoreType.DMA(())] * 5,
        compiler_params=pltpu.CompilerParams(collective_id=collective_id, has_side_effects=True),
    )(x)


def pair_exchange(x, collective_id):
    return _transfer(x, "pair", False, collective_id)


def group_exchange(x, collective_id):
    return _transfer(x, "group", False, collective_id)


def tp_exchange(x, collective_id):
    return _transfer(x, "tp", False, collective_id)


def tp_gather(x, collective_id):
    return _transfer(x, "tp", True, collective_id)


def rotate(values, positions):
    half_dim = values.shape[-1] // 2
    inverse = THETA ** (-2.0 * jnp.arange(half_dim, dtype=jnp.float32) / values.shape[-1])
    angles = positions[:, None, None] * inverse[None, None, :]
    cosine = jnp.cos(angles)
    sine_part = jnp.sin(angles)
    first_part = values[..., :half_dim]
    second_part = values[..., half_dim:]
    return jnp.concatenate(
        [
            first_part * cosine - second_part * sine_part,
            second_part * cosine + first_part * sine_part,
        ],
        axis=-1,
    )


def attend(query_rows, kv_rows, cache_kv, cache_valid, sinks, length):
    block_len = query_rows.shape[0]
    kv_heads = kv_rows.shape[1] // (2 * HEAD)
    query_heads = query_rows.shape[1] // HEAD
    group_size = query_heads // kv_heads
    positions = (length + jnp.arange(block_len, dtype=jnp.int32)).astype(jnp.float32)
    query_rot = rotate(
        query_rows.astype(jnp.float32).reshape(block_len, query_heads, HEAD), positions
    ).astype(jnp.bfloat16)
    kv_parts = kv_rows.reshape(block_len, kv_heads, 2, HEAD)
    key_rot = rotate(kv_parts[:, :, 0].astype(jnp.float32), positions).astype(jnp.bfloat16)
    cache_parts = cache_kv.reshape(cache_kv.shape[0], kv_heads, 2, HEAD)
    all_keys = jnp.concatenate([cache_parts[:, :, 0], key_rot], axis=0)
    all_values = jnp.concatenate([cache_parts[:, :, 1], kv_parts[:, :, 1]], axis=0)
    token_order = jnp.arange(block_len, dtype=jnp.int32)
    causal = token_order[None, :] <= token_order[:, None]
    allowed = jnp.concatenate(
        [jnp.broadcast_to(cache_valid[None, :], (block_len, cache_valid.shape[0])), causal], axis=1
    )
    row_allowed = jnp.repeat(allowed, group_size, axis=0)
    score_scale = HEAD ** (-0.5)
    query_block = query_rot.reshape(block_len * group_size, HEAD)
    scores = (
        jnp.dot(query_block, all_keys[:, 0].T, preferred_element_type=jnp.float32) * score_scale
    )
    scores = jnp.where(row_allowed, scores, -jnp.inf)
    sink_rows = jnp.tile(sinks, block_len)
    row_max = jnp.maximum(jnp.max(scores, axis=1), sink_rows)
    weights = jnp.exp(scores - row_max[:, None])
    denominator = jnp.sum(weights, axis=1) + jnp.exp(sink_rows - row_max)
    blended = (
        jnp.dot(weights.astype(jnp.bfloat16), all_values[:, 0], preferred_element_type=jnp.float32)
        / denominator[:, None]
    )
    outputs = blended.astype(jnp.bfloat16).reshape(block_len, group_size * HEAD)
    return outputs


def lane_dense(rows):
    count, length = rows.shape
    padded = -(-length // 128) * 128
    rows = jnp.pad(rows, ((0, 0), (0, padded - length)))
    return rows.reshape(count, padded // 128, 128)


def on_device(
    queries,
    new_kv,
    local_cache,
    remote_pool,
    page_index,
    lengths,
    sinks,
    out_weight,
    residual,
    norm_gain,
    routes,
    route_weights,
    expert_gate,
    expert_up,
    expert_down,
):
    groups = lax.axis_size("group")
    lane_count = remote_pool.shape[1]
    local_len = local_cache.shape[0]
    fetched = group_exchange(remote_pool.reshape(groups, -1, lane_count), 1)
    page_len = fetched.shape[1]
    length = lengths[0]
    offsets = jnp.arange(page_len, dtype=jnp.int32)
    remote_pos = local_len + page_index[0][:, None] * page_len + offsets[None, :]
    cache_valid = jnp.concatenate(
        [jnp.ones((local_len,), jnp.bool_), (remote_pos < length).reshape(-1)]
    )
    cache_kv = jnp.concatenate([local_cache, fetched.reshape(-1, lane_count)], axis=0)
    attended = attend(queries, new_kv, cache_kv, cache_valid, sinks, length)
    width = residual.shape[1]
    tp_count = lax.axis_size("tp")
    start = lax.axis_index("tp") * width
    own_gain = lax.dynamic_slice_in_dim(norm_gain, start, width, 0)
    partial_sum = jnp.dot(attended, out_weight, preferred_element_type=jnp.float32)
    partial_blocks = partial_sum.reshape(partial_sum.shape[0], tp_count, width).transpose(1, 0, 2)
    own_attn = jnp.sum(tp_exchange(partial_blocks.astype(jnp.bfloat16), 6).astype(jnp.float32), axis=0)
    own_state = own_attn + residual.astype(jnp.float32)
    square_sum = jnp.sum(own_state * own_state, axis=1, keepdims=True)
    square_high = square_sum.astype(jnp.bfloat16)
    square_low = (square_sum - square_high.astype(jnp.float32)).astype(jnp.bfloat16)
    row_width = -(-(width + 2) // 128) * 128
    scaled_own = (own_state * own_gain).astype(jnp.bfloat16)
    normed_own = jnp.concatenate(
        [scaled_own, square_high, square_low, jnp.zeros((own_state.shape[0], row_width - width - 2), jnp.bfloat16)],
        axis=1,
    )
    block_len = normed_own.shape[0]
    top_count = routes.shape[1]
    experts = groups // 2
    capacity = 5 * block_len * top_count // (4 * experts)
    member = jnp.any(
        routes[:, :, None] == jnp.arange(experts, dtype=jnp.int32)[None, None, :], axis=1
    ).astype(jnp.int32)
    slot_rank = jnp.cumsum(member, axis=0) - member
    slot_hit = member[:, :, None] * (
        slot_rank[:, :, None] == jnp.arange(capacity, dtype=jnp.int32)[None, None, :]
    ).astype(jnp.int32)
    slot_matrix = slot_hit.transpose(1, 2, 0).reshape(experts * capacity, block_len)
    send_own = jnp.dot(
        slot_matrix.astype(jnp.bfloat16), normed_own, preferred_element_type=jnp.float32
    ).astype(jnp.bfloat16)
    hidden_part = expert_gate.shape[2]
    gate_and_up = jnp.concatenate([expert_gate[0], expert_up[0]], axis=1)
    row_width = send_own.shape[1]
    received = pair_exchange(lane_dense(send_own.reshape(experts, capacity * row_width)), 2)
    received = received.reshape(experts, -1)[:, : capacity * row_width].reshape(experts, capacity, row_width)
    sources, slot_count, part_features = received.shape
    whole = pair_gather(received.reshape(sources * slot_count, part_features), 4)
    whole = whole.reshape(tp_count, 2 * sources * slot_count, part_features)
    gate_blocks = gate_and_up.reshape(tp_count, width, gate_and_up.shape[1])
    total_square = jnp.sum(whole[:, :, width:width + 2].astype(jnp.float32), axis=(0, 2))
    row_scale = lax.rsqrt(total_square / (width * tp_count) + EPSILON)
    both = jnp.einsum("tsf,tfh->sh", whole[:, :, :width], gate_blocks, preferred_element_type=jnp.float32)
    both = both * row_scale[:, None]
    gate_val = both[:, :hidden_part]
    up_val = both[:, hidden_part:]
    active = (gate_val * jax.nn.sigmoid(ALPHA * gate_val) * (up_val + 1.0)).astype(jnp.bfloat16)
    joined = tp_gather(active.T, 5)
    down_blocks = expert_down[0].reshape(tp_count, hidden_part, expert_down.shape[2])
    result = jnp.einsum("ths,thd->sd", joined, down_blocks, preferred_element_type=jnp.float32).astype(
        jnp.bfloat16
    )
    halves = result.reshape(2, experts, capacity, width)
    core = lax.rem(lax.axis_index("group"), 2)
    groups_total = lax.axis_size("group")
    swap = [(i, i + 1 - 2 * (i % 2)) for i in range(groups_total)]
    mine = lax.dynamic_index_in_dim(halves, core, 0, keepdims=False)
    theirs = lax.dynamic_index_in_dim(halves, 1 - core, 0, keepdims=False)
    other_half = lax.ppermute(theirs, "group", swap)
    joined_halves = (mine.astype(jnp.float32) + other_half.astype(jnp.float32)).astype(jnp.bfloat16)
    arrived = pair_exchange(lane_dense(joined_halves.reshape(experts, capacity * width)), 3)
    summed = arrived.reshape(experts, -1)[:, : capacity * width].astype(jnp.float32).reshape(experts * capacity, width)
    mixing = route_weights / jnp.sum(route_weights, axis=1, keepdims=True)
    expert_weight = jnp.sum(
        jnp.where(routes[:, :, None] == jnp.arange(experts, dtype=jnp.int32)[None, None, :], mixing[:, :, None], 0.0),
        axis=1,
    )
    combine = (slot_hit.astype(jnp.float32) * expert_weight[:, :, None]).reshape(block_len, experts * capacity)
    moe_out = jnp.dot(combine, summed, precision=lax.Precision.HIGHEST, preferred_element_type=jnp.float32)
    return (own_state + moe_out).astype(jnp.bfloat16)


def solution(mesh):
    return jax.shard_map(
        on_device,
        mesh=mesh,
        in_specs=(
            P("group", "tp"),
            P("group", "tp"),
            P("group", "tp"),
            P("group", "tp"),
            P("group", None),
            P("group"),
            P("tp"),
            P("tp", None),
            P("group", "tp"),
            P(),
            P("group", None),
            P("group", None),
            P("group", None, "tp"),
            P("group", None, "tp"),
            P("group", None, "tp"),
        ),
        out_specs=P("group", "tp"),
        check_vma=False,
    )
```

```python
import functools

import jax
import jax.numpy as jnp
from jax import lax
from jax.experimental import pallas as pl
from jax.experimental.pallas import tpu as pltpu
from jax.sharding import PartitionSpec as P

HEAD = 64


THETA = 150000.0
ALPHA = 1.702
EPSILON = 1e-05


def _transfer_kernel(axis, gather, x_ref, o_ref, buf, send_sem, recv_sem, local_sem):
    count = buf.shape[0]
    group_at = lax.axis_index("group")
    tp_at = lax.axis_index("tp")
    core = lax.rem(group_at, 2)
    if axis == "tp":
        me = tp_at
    elif axis == "pair":
        me = lax.div(group_at, 2)
    else:
        me = group_at

    def device(peer):
        if axis == "tp":
            return (group_at, peer)
        if axis == "pair":
            return (2 * peer + core, tp_at)
        return (peer, tp_at)

    def piece(peer):
        return x_ref if gather else x_ref.at[peer]

    barrier = pltpu.get_barrier_semaphore()

    def greet(step, carry):
        peer = lax.rem(me + step, count)
        pl.semaphore_signal(barrier, inc=1, device_id=device(peer), device_id_type=pl.DeviceIdType.MESH)
        return carry

    lax.fori_loop(1, count, greet, 0)
    pl.semaphore_wait(barrier, count - 1)
    local = pltpu.make_async_copy(piece(me), buf.at[me], local_sem)
    local.start()

    def send(step, carry):
        peer = lax.rem(me + step, count)
        pltpu.make_async_remote_copy(
            src_ref=piece(peer),
            dst_ref=buf.at[me],
            send_sem=send_sem,
            recv_sem=recv_sem,
            device_id=device(peer),
            device_id_type=pl.DeviceIdType.MESH,
        ).start()
        return carry

    lax.fori_loop(1, count, send, 0)
    local.wait()
    every = pltpu.make_async_remote_copy(
        src_ref=buf.at[pl.ds(0, count - 1)],
        dst_ref=buf.at[pl.ds(0, count - 1)],
        send_sem=send_sem,
        recv_sem=recv_sem,
        device_id=device(lax.rem(me + 1, count)),
        device_id_type=pl.DeviceIdType.MESH,
    )
    every.wait_send()
    every.wait_recv()
    o_ref[...] = buf[...]


def _transfer(x, axis, gather, collective_id):
    count = lax.axis_size("group") // 2 if axis == "pair" else lax.axis_size(axis)
    shape = ((count,) + x.shape) if gather else x.shape
    return pl.pallas_call(
        functools.partial(_transfer_kernel, axis, gather),
        out_shape=jax.ShapeDtypeStruct(shape, x.dtype),
        in_specs=[pl.BlockSpec(memory_space=pltpu.VMEM)],
        out_specs=pl.BlockSpec(memory_space=pltpu.VMEM),
        scratch_shapes=[
            pltpu.VMEM(shape, x.dtype),
            pltpu.SemaphoreType.DMA(()),
            pltpu.SemaphoreType.DMA(()),
            pltpu.SemaphoreType.DMA(()),
        ],
        compiler_params=pltpu.CompilerParams(collective_id=collective_id, has_side_effects=True),
    )(x)


def _pair_gather_kernel(x_ref, o_ref, buf, send_sem, recv_sem, local_sem, pass_send, pass_recv):
    count = buf.shape[0]
    group_at = lax.axis_index("group")
    tp_at = lax.axis_index("tp")
    core = lax.rem(group_at, 2)
    sibling = (group_at + 1 - 2 * core, tp_at)
    barrier = pltpu.get_barrier_semaphore()

    def greet(step, carry):
        peer = lax.rem(tp_at + step, count)
        pl.semaphore_signal(barrier, inc=1, device_id=(group_at, peer), device_id_type=pl.DeviceIdType.MESH)
        return carry

    lax.fori_loop(1, count, greet, 0)
    pl.semaphore_signal(barrier, inc=1, device_id=sibling, device_id_type=pl.DeviceIdType.MESH)
    pl.semaphore_wait(barrier, count)
    local = pltpu.make_async_copy(x_ref, buf.at[tp_at, core], local_sem)
    local.start()

    def send(step, carry):
        peer = lax.rem(tp_at + step, count)
        pltpu.make_async_remote_copy(
            src_ref=x_ref,
            dst_ref=buf.at[tp_at, core],
            send_sem=send_sem,
            recv_sem=recv_sem,
            device_id=(group_at, peer),
            device_id_type=pl.DeviceIdType.MESH,
        ).start()
        return carry

    lax.fori_loop(1, count, send, 0)
    local.wait()
    every = pltpu.make_async_remote_copy(
        src_ref=buf.at[pl.ds(0, count - 1), 0],
        dst_ref=buf.at[pl.ds(0, count - 1), 0],
        send_sem=send_sem,
        recv_sem=recv_sem,
        device_id=(group_at, lax.rem(tp_at + 1, count)),
        device_id_type=pl.DeviceIdType.MESH,
    )
    every.wait_recv()
    onward = pltpu.make_async_remote_copy(
        src_ref=buf.at[:, core],
        dst_ref=buf.at[:, core],
        send_sem=pass_send,
        recv_sem=pass_recv,
        device_id=sibling,
        device_id_type=pl.DeviceIdType.MESH,
    )
    onward.start()
    every.wait_send()
    onward.wait_send()
    onward.wait_recv()
    o_ref[...] = buf[...]


def pair_gather(x, collective_id):
    shape = (lax.axis_size("tp"), 2) + x.shape
    return pl.pallas_call(
        _pair_gather_kernel,
        out_shape=jax.ShapeDtypeStruct(shape, x.dtype),
        in_specs=[pl.BlockSpec(memory_space=pltpu.VMEM)],
        out_specs=pl.BlockSpec(memory_space=pltpu.VMEM),
        scratch_shapes=[pltpu.VMEM(shape, x.dtype)] + [pltpu.SemaphoreType.DMA(())] * 5,
        compiler_params=pltpu.CompilerParams(collective_id=collective_id, has_side_effects=True),
    )(x)


def pair_exchange(x, collective_id):
    return _transfer(x, "pair", False, collective_id)


def group_exchange(x, collective_id):
    return _transfer(x, "group", False, collective_id)


def tp_exchange(x, collective_id):
    return _transfer(x, "tp", False, collective_id)


def tp_gather(x, collective_id):
    return _transfer(x, "tp", True, collective_id)


def rotate(values, positions):
    half_dim = values.shape[-1] // 2
    inverse = THETA ** (-2.0 * jnp.arange(half_dim, dtype=jnp.float32) / values.shape[-1])
    angles = positions[:, None, None] * inverse[None, None, :]
    cosine = jnp.cos(angles)
    sine_part = jnp.sin(angles)
    first_part = values[..., :half_dim]
    second_part = values[..., half_dim:]
    return jnp.concatenate(
        [
            first_part * cosine - second_part * sine_part,
            second_part * cosine + first_part * sine_part,
        ],
        axis=-1,
    )


def attend(query_rows, kv_rows, cache_kv, cache_valid, sinks, length):
    block_len = query_rows.shape[0]
    kv_heads = kv_rows.shape[1] // (2 * HEAD)
    query_heads = query_rows.shape[1] // HEAD
    group_size = query_heads // kv_heads
    positions = (length + jnp.arange(block_len, dtype=jnp.int32)).astype(jnp.float32)
    query_rot = rotate(
        query_rows.astype(jnp.float32).reshape(block_len, query_heads, HEAD), positions
    ).astype(jnp.bfloat16)
    kv_parts = kv_rows.reshape(block_len, kv_heads, 2, HEAD)
    key_rot = rotate(kv_parts[:, :, 0].astype(jnp.float32), positions).astype(jnp.bfloat16)
    cache_parts = cache_kv.reshape(cache_kv.shape[0], kv_heads, 2, HEAD)
    all_keys = jnp.concatenate([cache_parts[:, :, 0], key_rot], axis=0)
    all_values = jnp.concatenate([cache_parts[:, :, 1], kv_parts[:, :, 1]], axis=0)
    token_order = jnp.arange(block_len, dtype=jnp.int32)
    causal = token_order[None, :] <= token_order[:, None]
    allowed = jnp.concatenate(
        [jnp.broadcast_to(cache_valid[None, :], (block_len, cache_valid.shape[0])), causal], axis=1
    )
    row_allowed = jnp.repeat(allowed, group_size, axis=0)
    score_scale = HEAD ** (-0.5)
    query_block = query_rot.reshape(block_len * group_size, HEAD)
    scores = (
        jnp.dot(query_block, all_keys[:, 0].T, preferred_element_type=jnp.float32) * score_scale
    )
    scores = jnp.where(row_allowed, scores, -jnp.inf)
    sink_rows = jnp.tile(sinks, block_len)
    row_max = jnp.maximum(jnp.max(scores, axis=1), sink_rows)
    weights = jnp.exp(scores - row_max[:, None])
    denominator = jnp.sum(weights, axis=1) + jnp.exp(sink_rows - row_max)
    blended = (
        jnp.dot(weights.astype(jnp.bfloat16), all_values[:, 0], preferred_element_type=jnp.float32)
        / denominator[:, None]
    )
    outputs = blended.astype(jnp.bfloat16).reshape(block_len, group_size * HEAD)
    return outputs


def lane_dense(rows):
    count, length = rows.shape
    padded = -(-length // 128) * 128
    rows = jnp.pad(rows, ((0, 0), (0, padded - length)))
    return rows.reshape(count, padded // 128, 128)


def on_device(
    queries,
    new_kv,
    local_cache,
    remote_pool,
    page_index,
    lengths,
    sinks,
    out_weight,
    residual,
    norm_gain,
    routes,
    route_weights,
    expert_gate,
    expert_up,
    expert_down,
):
    groups = lax.axis_size("group")
    lane_count = remote_pool.shape[1]
    local_len = local_cache.shape[0]
    fetched = group_exchange(remote_pool.reshape(groups, -1, lane_count), 1)
    page_len = fetched.shape[1]
    length = lengths[0]
    offsets = jnp.arange(page_len, dtype=jnp.int32)
    remote_pos = local_len + page_index[0][:, None] * page_len + offsets[None, :]
    cache_valid = jnp.concatenate(
        [jnp.ones((local_len,), jnp.bool_), (remote_pos < length).reshape(-1)]
    )
    cache_kv = jnp.concatenate([local_cache, fetched.reshape(-1, lane_count)], axis=0)
    attended = attend(queries, new_kv, cache_kv, cache_valid, sinks, length)
    width = residual.shape[1]
    tp_count = lax.axis_size("tp")
    start = lax.axis_index("tp") * width
    own_gain = lax.dynamic_slice_in_dim(norm_gain, start, width, 0)
    partial_sum = jnp.dot(attended, out_weight, preferred_element_type=jnp.float32)
    partial_blocks = partial_sum.reshape(partial_sum.shape[0], tp_count, width).transpose(1, 0, 2)
    own_attn = jnp.sum(tp_exchange(partial_blocks.astype(jnp.bfloat16), 6).astype(jnp.float32), axis=0)
    own_state = own_attn + residual.astype(jnp.float32)
    square_sum = jnp.sum(own_state * own_state, axis=1, keepdims=True)
    square_high = square_sum.astype(jnp.bfloat16)
    square_low = (square_sum - square_high.astype(jnp.float32)).astype(jnp.bfloat16)
    row_width = -(-(width + 2) // 128) * 128
    scaled_own = (own_state * own_gain).astype(jnp.bfloat16)
    normed_own = jnp.concatenate(
        [scaled_own, square_high, square_low, jnp.zeros((own_state.shape[0], row_width - width - 2), jnp.bfloat16)],
        axis=1,
    )
    block_len = normed_own.shape[0]
    top_count = routes.shape[1]
    experts = groups // 2
    capacity = 5 * block_len * top_count // (4 * experts)
    member = jnp.any(
        routes[:, :, None] == jnp.arange(experts, dtype=jnp.int32)[None, None, :], axis=1
    ).astype(jnp.int32)
    slot_rank = jnp.cumsum(member, axis=0) - member
    slot_hit = member[:, :, None] * (
        slot_rank[:, :, None] == jnp.arange(capacity, dtype=jnp.int32)[None, None, :]
    ).astype(jnp.int32)
    slot_matrix = slot_hit.transpose(1, 2, 0).reshape(experts * capacity, block_len)
    send_own = jnp.dot(
        slot_matrix.astype(jnp.bfloat16), normed_own, preferred_element_type=jnp.float32
    ).astype(jnp.bfloat16)
    hidden_part = expert_gate.shape[2]
    row_width = send_own.shape[1]
    received = pair_exchange(lane_dense(send_own.reshape(experts, capacity * row_width)), 2)
    received = received.reshape(experts, -1)[:, : capacity * row_width].reshape(experts, capacity, row_width)
    sources, slot_count, part_features = received.shape
    whole = pair_gather(received.reshape(sources * slot_count, part_features), 4)
    whole = whole.reshape(tp_count, 2 * sources * slot_count, part_features)
    total_square = jnp.sum(whole[:, :, width:width + 2].astype(jnp.float32), axis=(0, 2))
    row_scale = lax.rsqrt(total_square / (width * tp_count) + EPSILON)
    tokens = whole[:, :, :width]
    gate_view = expert_gate[0].reshape(tp_count, width, hidden_part)
    up_view = expert_up[0].reshape(tp_count, width, hidden_part)
    both = jnp.concatenate(
        [
            jnp.einsum("tsf,tfh->sh", tokens, gate_view, preferred_element_type=jnp.float32),
            jnp.einsum("tsf,tfh->sh", tokens, up_view, preferred_element_type=jnp.float32),
        ],
        axis=1,
    )
    both = both * row_scale[:, None]
    gate_val = both[:, :hidden_part]
    up_val = both[:, hidden_part:]
    active = (gate_val * jax.nn.sigmoid(ALPHA * gate_val) * (up_val + 1.0)).astype(jnp.bfloat16)
    joined = tp_gather(active.T, 5)
    down_blocks = expert_down[0].reshape(tp_count, hidden_part, expert_down.shape[2])
    result = jnp.einsum("ths,thd->sd", joined, down_blocks, preferred_element_type=jnp.float32).astype(
        jnp.bfloat16
    )
    halves = result.reshape(2, experts, capacity, width)
    core = lax.rem(lax.axis_index("group"), 2)
    groups_total = lax.axis_size("group")
    swap = [(i, i + 1 - 2 * (i % 2)) for i in range(groups_total)]
    mine = lax.dynamic_index_in_dim(halves, core, 0, keepdims=False)
    theirs = lax.dynamic_index_in_dim(halves, 1 - core, 0, keepdims=False)
    other_half = lax.ppermute(theirs, "group", swap)
    joined_halves = (mine.astype(jnp.float32) + other_half.astype(jnp.float32)).astype(jnp.bfloat16)
    arrived = pair_exchange(lane_dense(joined_halves.reshape(experts, capacity * width)), 3)
    summed = arrived.reshape(experts, -1)[:, : capacity * width].astype(jnp.float32).reshape(experts * capacity, width)
    mixing = route_weights / jnp.sum(route_weights, axis=1, keepdims=True)
    expert_weight = jnp.sum(
        jnp.where(routes[:, :, None] == jnp.arange(experts, dtype=jnp.int32)[None, None, :], mixing[:, :, None], 0.0),
        axis=1,
    )
    combine = (slot_hit.astype(jnp.float32) * expert_weight[:, :, None]).reshape(block_len, experts * capacity)
    moe_out = jnp.dot(combine, summed, precision=lax.Precision.HIGHEST, preferred_element_type=jnp.float32)
    return (own_state + moe_out).astype(jnp.bfloat16)


def solution(mesh):
    return jax.shard_map(
        on_device,
        mesh=mesh,
        in_specs=(
            P("group", "tp"),
            P("group", "tp"),
            P("group", "tp"),
            P("group", "tp"),
            P("group", None),
            P("group"),
            P("tp"),
            P("tp", None),
            P("group", "tp"),
            P(),
            P("group", None),
            P("group", None),
            P("group", None, "tp"),
            P("group", None, "tp"),
            P("group", None, "tp"),
        ),
        out_specs=P("group", "tp"),
        check_vma=False,
    )
```

```python
import functools

import jax
import jax.numpy as jnp
from jax import lax
from jax.experimental import pallas as pl
from jax.experimental.pallas import tpu as pltpu
from jax.sharding import PartitionSpec as P

HEAD = 64


THETA = 150000.0
ALPHA = 1.702
EPSILON = 1e-05


def _row_parts(rows, parts=4):
    if not rows:
        return [(0, 0)]
    step = -(-rows // (parts * 16)) * 16
    return [(first, min(step, rows - first)) for first in range(0, rows, step)]


def _transfer_kernel(axis, gather, x_ref, o_ref, buf, send_sem, recv_sem, local_sem):
    count = buf.shape[0]
    group_at = lax.axis_index("group")
    tp_at = lax.axis_index("tp")
    core = lax.rem(group_at, 2)
    if axis == "tp":
        me = tp_at
    elif axis == "pair":
        me = lax.div(group_at, 2)
    else:
        me = group_at

    def device(peer):
        if axis == "tp":
            return (group_at, peer)
        if axis == "pair":
            return (2 * peer + core, tp_at)
        return (peer, tp_at)

    def piece(peer):
        return x_ref if gather else x_ref.at[peer]

    barrier = pltpu.get_barrier_semaphore()

    def greet(step, carry):
        peer = lax.rem(me + step, count)
        pl.semaphore_signal(barrier, inc=1, device_id=device(peer), device_id_type=pl.DeviceIdType.MESH)
        return carry

    lax.fori_loop(1, count, greet, 0)
    pl.semaphore_wait(barrier, count - 1)
    local = pltpu.make_async_copy(piece(me), buf.at[me], local_sem)
    local.start()

    for first, size in _row_parts(buf.shape[1] if gather else 0):

        def send(step, carry, first=first, size=size):
            peer = lax.rem(me + step, count)
            src = piece(peer)
            dst = buf.at[me]
            if size:
                src = src.at[pl.ds(first, size)]
                dst = dst.at[pl.ds(first, size)]
            pltpu.make_async_remote_copy(
                src_ref=src,
                dst_ref=dst,
                send_sem=send_sem,
                recv_sem=recv_sem,
                device_id=device(peer),
                device_id_type=pl.DeviceIdType.MESH,
            ).start()
            return carry

        lax.fori_loop(1, count, send, 0)
    local.wait()
    every = pltpu.make_async_remote_copy(
        src_ref=buf.at[pl.ds(0, count - 1)],
        dst_ref=buf.at[pl.ds(0, count - 1)],
        send_sem=send_sem,
        recv_sem=recv_sem,
        device_id=device(lax.rem(me + 1, count)),
        device_id_type=pl.DeviceIdType.MESH,
    )
    every.wait_send()
    every.wait_recv()
    o_ref[...] = buf[...]


def _transfer(x, axis, gather, collective_id):
    count = lax.axis_size("group") // 2 if axis == "pair" else lax.axis_size(axis)
    shape = ((count,) + x.shape) if gather else x.shape
    return pl.pallas_call(
        functools.partial(_transfer_kernel, axis, gather),
        out_shape=jax.ShapeDtypeStruct(shape, x.dtype),
        in_specs=[pl.BlockSpec(memory_space=pltpu.VMEM)],
        out_specs=pl.BlockSpec(memory_space=pltpu.VMEM),
        scratch_shapes=[
            pltpu.VMEM(shape, x.dtype),
            pltpu.SemaphoreType.DMA(()),
            pltpu.SemaphoreType.DMA(()),
            pltpu.SemaphoreType.DMA(()),
        ],
        compiler_params=pltpu.CompilerParams(collective_id=collective_id, has_side_effects=True),
    )(x)


def _pair_gather_kernel(x_ref, o_ref, buf, send_sem, recv_sem, local_sem, pass_send, pass_recv):
    count = buf.shape[0]
    group_at = lax.axis_index("group")
    tp_at = lax.axis_index("tp")
    core = lax.rem(group_at, 2)
    sibling = (group_at + 1 - 2 * core, tp_at)
    barrier = pltpu.get_barrier_semaphore()

    def greet(step, carry):
        peer = lax.rem(tp_at + step, count)
        pl.semaphore_signal(barrier, inc=1, device_id=(group_at, peer), device_id_type=pl.DeviceIdType.MESH)
        return carry

    lax.fori_loop(1, count, greet, 0)
    pl.semaphore_signal(barrier, inc=1, device_id=sibling, device_id_type=pl.DeviceIdType.MESH)
    pl.semaphore_wait(barrier, count)
    local = pltpu.make_async_copy(x_ref, buf.at[tp_at, core], local_sem)
    local.start()

    for first, size in _row_parts(x_ref.shape[0]):

        def send(step, carry, first=first, size=size):
            peer = lax.rem(tp_at + step, count)
            pltpu.make_async_remote_copy(
                src_ref=x_ref.at[pl.ds(first, size)],
                dst_ref=buf.at[tp_at, core, pl.ds(first, size)],
                send_sem=send_sem,
                recv_sem=recv_sem,
                device_id=(group_at, peer),
                device_id_type=pl.DeviceIdType.MESH,
            ).start()
            return carry

        lax.fori_loop(1, count, send, 0)
    local.wait()
    every = pltpu.make_async_remote_copy(
        src_ref=buf.at[pl.ds(0, count - 1), 0],
        dst_ref=buf.at[pl.ds(0, count - 1), 0],
        send_sem=send_sem,
        recv_sem=recv_sem,
        device_id=(group_at, lax.rem(tp_at + 1, count)),
        device_id_type=pl.DeviceIdType.MESH,
    )
    every.wait_recv()
    onward = pltpu.make_async_remote_copy(
        src_ref=buf.at[:, core],
        dst_ref=buf.at[:, core],
        send_sem=pass_send,
        recv_sem=pass_recv,
        device_id=sibling,
        device_id_type=pl.DeviceIdType.MESH,
    )
    onward.start()
    every.wait_send()
    onward.wait_send()
    onward.wait_recv()
    o_ref[...] = buf[...]


def pair_gather(x, collective_id):
    shape = (lax.axis_size("tp"), 2) + x.shape
    return pl.pallas_call(
        _pair_gather_kernel,
        out_shape=jax.ShapeDtypeStruct(shape, x.dtype),
        in_specs=[pl.BlockSpec(memory_space=pltpu.VMEM)],
        out_specs=pl.BlockSpec(memory_space=pltpu.VMEM),
        scratch_shapes=[pltpu.VMEM(shape, x.dtype)] + [pltpu.SemaphoreType.DMA(())] * 5,
        compiler_params=pltpu.CompilerParams(collective_id=collective_id, has_side_effects=True),
    )(x)


def pair_exchange(x, collective_id):
    return _transfer(x, "pair", False, collective_id)


def group_exchange(x, collective_id):
    return _transfer(x, "group", False, collective_id)


def tp_exchange(x, collective_id):
    return _transfer(x, "tp", False, collective_id)


def tp_gather(x, collective_id):
    return _transfer(x, "tp", True, collective_id)


def rotate(values, positions):
    half_dim = values.shape[-1] // 2
    inverse = THETA ** (-2.0 * jnp.arange(half_dim, dtype=jnp.float32) / values.shape[-1])
    angles = positions[:, None, None] * inverse[None, None, :]
    cosine = jnp.cos(angles)
    sine_part = jnp.sin(angles)
    first_part = values[..., :half_dim]
    second_part = values[..., half_dim:]
    return jnp.concatenate(
        [
            first_part * cosine - second_part * sine_part,
            second_part * cosine + first_part * sine_part,
        ],
        axis=-1,
    )


def attend(query_rows, kv_rows, cache_kv, cache_valid, sinks, length):
    block_len = query_rows.shape[0]
    kv_heads = kv_rows.shape[1] // (2 * HEAD)
    query_heads = query_rows.shape[1] // HEAD
    group_size = query_heads // kv_heads
    positions = (length + jnp.arange(block_len, dtype=jnp.int32)).astype(jnp.float32)
    query_rot = rotate(
        query_rows.astype(jnp.float32).reshape(block_len, query_heads, HEAD), positions
    ).astype(jnp.bfloat16)
    kv_parts = kv_rows.reshape(block_len, kv_heads, 2, HEAD)
    key_rot = rotate(kv_parts[:, :, 0].astype(jnp.float32), positions).astype(jnp.bfloat16)
    cache_parts = cache_kv.reshape(cache_kv.shape[0], kv_heads, 2, HEAD)
    all_keys = jnp.concatenate([cache_parts[:, :, 0], key_rot], axis=0)
    all_values = jnp.concatenate([cache_parts[:, :, 1], kv_parts[:, :, 1]], axis=0)
    token_order = jnp.arange(block_len, dtype=jnp.int32)
    causal = token_order[None, :] <= token_order[:, None]
    allowed = jnp.concatenate(
        [jnp.broadcast_to(cache_valid[None, :], (block_len, cache_valid.shape[0])), causal], axis=1
    )
    row_allowed = jnp.repeat(allowed, group_size, axis=0)
    score_scale = HEAD ** (-0.5)
    query_block = query_rot.reshape(block_len * group_size, HEAD)
    scores = (
        jnp.dot(query_block, all_keys[:, 0].T, preferred_element_type=jnp.float32) * score_scale
    )
    scores = jnp.where(row_allowed, scores, -jnp.inf)
    sink_rows = jnp.tile(sinks, block_len)
    row_max = jnp.maximum(jnp.max(scores, axis=1), sink_rows)
    weights = jnp.exp(scores - row_max[:, None])
    denominator = jnp.sum(weights, axis=1) + jnp.exp(sink_rows - row_max)
    blended = (
        jnp.dot(weights.astype(jnp.bfloat16), all_values[:, 0], preferred_element_type=jnp.float32)
        / denominator[:, None]
    )
    outputs = blended.astype(jnp.bfloat16).reshape(block_len, group_size * HEAD)
    return outputs


def lane_dense(rows):
    count, length = rows.shape
    padded = -(-length // 128) * 128
    rows = jnp.pad(rows, ((0, 0), (0, padded - length)))
    return rows.reshape(count, padded // 128, 128)


def on_device(
    queries,
    new_kv,
    local_cache,
    remote_pool,
    page_index,
    lengths,
    sinks,
    out_weight,
    residual,
    norm_gain,
    routes,
    route_weights,
    expert_gate,
    expert_up,
    expert_down,
):
    groups = lax.axis_size("group")
    lane_count = remote_pool.shape[1]
    local_len = local_cache.shape[0]
    fetched = group_exchange(remote_pool.reshape(groups, -1, lane_count), 1)
    page_len = fetched.shape[1]
    length = lengths[0]
    offsets = jnp.arange(page_len, dtype=jnp.int32)
    remote_pos = local_len + page_index[0][:, None] * page_len + offsets[None, :]
    cache_valid = jnp.concatenate(
        [jnp.ones((local_len,), jnp.bool_), (remote_pos < length).reshape(-1)]
    )
    cache_kv = jnp.concatenate([local_cache, fetched.reshape(-1, lane_count)], axis=0)
    attended = attend(queries, new_kv, cache_kv, cache_valid, sinks, length)
    width = residual.shape[1]
    tp_count = lax.axis_size("tp")
    start = lax.axis_index("tp") * width
    own_gain = lax.dynamic_slice_in_dim(norm_gain, start, width, 0)
    partial_sum = jnp.dot(attended, out_weight, preferred_element_type=jnp.float32)
    partial_blocks = partial_sum.reshape(partial_sum.shape[0], tp_count, width).transpose(1, 0, 2)
    own_attn = jnp.sum(tp_exchange(partial_blocks.astype(jnp.bfloat16), 6).astype(jnp.float32), axis=0)
    own_state = own_attn + residual.astype(jnp.float32)
    square_sum = jnp.sum(own_state * own_state, axis=1, keepdims=True)
    square_high = square_sum.astype(jnp.bfloat16)
    square_low = (square_sum - square_high.astype(jnp.float32)).astype(jnp.bfloat16)
    row_width = -(-(width + 2) // 128) * 128
    scaled_own = (own_state * own_gain).astype(jnp.bfloat16)
    normed_own = jnp.concatenate(
        [scaled_own, square_high, square_low, jnp.zeros((own_state.shape[0], row_width - width - 2), jnp.bfloat16)],
        axis=1,
    )
    block_len = normed_own.shape[0]
    top_count = routes.shape[1]
    experts = groups // 2
    capacity = 5 * block_len * top_count // (4 * experts)
    member = jnp.any(
        routes[:, :, None] == jnp.arange(experts, dtype=jnp.int32)[None, None, :], axis=1
    ).astype(jnp.int32)
    slot_rank = jnp.cumsum(member, axis=0) - member
    slot_hit = member[:, :, None] * (
        slot_rank[:, :, None] == jnp.arange(capacity, dtype=jnp.int32)[None, None, :]
    ).astype(jnp.int32)
    slot_matrix = slot_hit.transpose(1, 2, 0).reshape(experts * capacity, block_len)
    send_own = jnp.dot(
        slot_matrix.astype(jnp.bfloat16), normed_own, preferred_element_type=jnp.float32
    ).astype(jnp.bfloat16)
    hidden_part = expert_gate.shape[2]
    row_width = send_own.shape[1]
    received = pair_exchange(lane_dense(send_own.reshape(experts, capacity * row_width)), 2)
    received = received.reshape(experts, -1)[:, : capacity * row_width].reshape(experts, capacity, row_width)
    sources, slot_count, part_features = received.shape
    whole = pair_gather(received.reshape(sources * slot_count, part_features), 4)
    whole = whole.reshape(tp_count, 2 * sources * slot_count, part_features)
    total_square = jnp.sum(whole[:, :, width:width + 2].astype(jnp.float32), axis=(0, 2))
    row_scale = lax.rsqrt(total_square / (width * tp_count) + EPSILON)
    tokens = whole[:, :, :width]
    gate_view = expert_gate[0].reshape(tp_count, width, hidden_part)
    up_view = expert_up[0].reshape(tp_count, width, hidden_part)
    both = jnp.concatenate(
        [
            jnp.einsum("tsf,tfh->sh", tokens, gate_view, preferred_element_type=jnp.float32),
            jnp.einsum("tsf,tfh->sh", tokens, up_view, preferred_element_type=jnp.float32),
        ],
        axis=1,
    )
    both = both * row_scale[:, None]
    gate_val = both[:, :hidden_part]
    up_val = both[:, hidden_part:]
    active = (gate_val * jax.nn.sigmoid(ALPHA * gate_val) * (up_val + 1.0)).astype(jnp.bfloat16)
    joined = tp_gather(active.T, 5)
    down_blocks = expert_down[0].reshape(tp_count, hidden_part, expert_down.shape[2])
    result = jnp.einsum("ths,thd->sd", joined, down_blocks, preferred_element_type=jnp.float32).astype(
        jnp.bfloat16
    )
    halves = result.reshape(2, experts, capacity, width)
    core = lax.rem(lax.axis_index("group"), 2)
    groups_total = lax.axis_size("group")
    swap = [(i, i + 1 - 2 * (i % 2)) for i in range(groups_total)]
    mine = lax.dynamic_index_in_dim(halves, core, 0, keepdims=False)
    theirs = lax.dynamic_index_in_dim(halves, 1 - core, 0, keepdims=False)
    other_half = lax.ppermute(theirs, "group", swap)
    joined_halves = (mine.astype(jnp.float32) + other_half.astype(jnp.float32)).astype(jnp.bfloat16)
    arrived = pair_exchange(lane_dense(joined_halves.reshape(experts, capacity * width)), 3)
    summed = arrived.reshape(experts, -1)[:, : capacity * width].astype(jnp.float32).reshape(experts * capacity, width)
    mixing = route_weights / jnp.sum(route_weights, axis=1, keepdims=True)
    expert_weight = jnp.sum(
        jnp.where(routes[:, :, None] == jnp.arange(experts, dtype=jnp.int32)[None, None, :], mixing[:, :, None], 0.0),
        axis=1,
    )
    combine = (slot_hit.astype(jnp.float32) * expert_weight[:, :, None]).reshape(block_len, experts * capacity)
    moe_out = jnp.dot(combine, summed, precision=lax.Precision.HIGHEST, preferred_element_type=jnp.float32)
    return (own_state + moe_out).astype(jnp.bfloat16)


def solution(mesh):
    return jax.shard_map(
        on_device,
        mesh=mesh,
        in_specs=(
            P("group", "tp"),
            P("group", "tp"),
            P("group", "tp"),
            P("group", "tp"),
            P("group", None),
            P("group"),
            P("tp"),
            P("tp", None),
            P("group", "tp"),
            P(),
            P("group", None),
            P("group", None),
            P("group", None, "tp"),
            P("group", None, "tp"),
            P("group", None, "tp"),
        ),
        out_specs=P("group", "tp"),
        check_vma=False,
    )
```

```python
import functools

import jax
import jax.numpy as jnp
from jax import lax
from jax.experimental import pallas as pl
from jax.experimental.pallas import tpu as pltpu
from jax.sharding import PartitionSpec as P

HEAD = 64


THETA = 150000.0
ALPHA = 1.702
EPSILON = 1e-05


def _row_parts(rows, parts=8):
    if not rows:
        return [(0, 0)]
    step = -(-rows // (parts * 16)) * 16
    return [(first, min(step, rows - first)) for first in range(0, rows, step)]


def _transfer_kernel(axis, gather, x_ref, o_ref, buf, send_sem, recv_sem, local_sem):
    count = buf.shape[0]
    group_at = lax.axis_index("group")
    tp_at = lax.axis_index("tp")
    core = lax.rem(group_at, 2)
    if axis == "tp":
        me = tp_at
    elif axis == "pair":
        me = lax.div(group_at, 2)
    else:
        me = group_at

    def device(peer):
        if axis == "tp":
            return (group_at, peer)
        if axis == "pair":
            return (2 * peer + core, tp_at)
        return (peer, tp_at)

    def piece(peer):
        return x_ref if gather else x_ref.at[peer]

    barrier = pltpu.get_barrier_semaphore()

    def greet(step, carry):
        peer = lax.rem(me + step, count)
        pl.semaphore_signal(barrier, inc=1, device_id=device(peer), device_id_type=pl.DeviceIdType.MESH)
        return carry

    lax.fori_loop(1, count, greet, 0)
    pl.semaphore_wait(barrier, count - 1)
    local = pltpu.make_async_copy(piece(me), buf.at[me], local_sem)
    local.start()

    for first, size in _row_parts(buf.shape[1] if (gather or axis == "tp") else 0):

        def send(step, carry, first=first, size=size):
            peer = lax.rem(me + step, count)
            src = piece(peer)
            dst = buf.at[me]
            if size:
                src = src.at[pl.ds(first, size)]
                dst = dst.at[pl.ds(first, size)]
            pltpu.make_async_remote_copy(
                src_ref=src,
                dst_ref=dst,
                send_sem=send_sem,
                recv_sem=recv_sem,
                device_id=device(peer),
                device_id_type=pl.DeviceIdType.MESH,
            ).start()
            return carry

        lax.fori_loop(1, count, send, 0)
    local.wait()
    every = pltpu.make_async_remote_copy(
        src_ref=buf.at[pl.ds(0, count - 1)],
        dst_ref=buf.at[pl.ds(0, count - 1)],
        send_sem=send_sem,
        recv_sem=recv_sem,
        device_id=device(lax.rem(me + 1, count)),
        device_id_type=pl.DeviceIdType.MESH,
    )
    every.wait_send()
    every.wait_recv()
    o_ref[...] = buf[...]


def _transfer(x, axis, gather, collective_id):
    count = lax.axis_size("group") // 2 if axis == "pair" else lax.axis_size(axis)
    shape = ((count,) + x.shape) if gather else x.shape
    return pl.pallas_call(
        functools.partial(_transfer_kernel, axis, gather),
        out_shape=jax.ShapeDtypeStruct(shape, x.dtype),
        in_specs=[pl.BlockSpec(memory_space=pltpu.VMEM)],
        out_specs=pl.BlockSpec(memory_space=pltpu.VMEM),
        scratch_shapes=[
            pltpu.VMEM(shape, x.dtype),
            pltpu.SemaphoreType.DMA(()),
            pltpu.SemaphoreType.DMA(()),
            pltpu.SemaphoreType.DMA(()),
        ],
        compiler_params=pltpu.CompilerParams(collective_id=collective_id, has_side_effects=True),
    )(x)


def _pair_gather_kernel(x_ref, o_ref, buf, send_sem, recv_sem, local_sem, pass_send, pass_recv):
    count = buf.shape[0]
    group_at = lax.axis_index("group")
    tp_at = lax.axis_index("tp")
    core = lax.rem(group_at, 2)
    sibling = (group_at + 1 - 2 * core, tp_at)
    barrier = pltpu.get_barrier_semaphore()

    def greet(step, carry):
        peer = lax.rem(tp_at + step, count)
        pl.semaphore_signal(barrier, inc=1, device_id=(group_at, peer), device_id_type=pl.DeviceIdType.MESH)
        return carry

    lax.fori_loop(1, count, greet, 0)
    pl.semaphore_signal(barrier, inc=1, device_id=sibling, device_id_type=pl.DeviceIdType.MESH)
    pl.semaphore_wait(barrier, count)
    local = pltpu.make_async_copy(x_ref, buf.at[tp_at, core], local_sem)
    local.start()

    for first, size in _row_parts(x_ref.shape[0]):

        def send(step, carry, first=first, size=size):
            peer = lax.rem(tp_at + step, count)
            pltpu.make_async_remote_copy(
                src_ref=x_ref.at[pl.ds(first, size)],
                dst_ref=buf.at[tp_at, core, pl.ds(first, size)],
                send_sem=send_sem,
                recv_sem=recv_sem,
                device_id=(group_at, peer),
                device_id_type=pl.DeviceIdType.MESH,
            ).start()
            return carry

        lax.fori_loop(1, count, send, 0)
    local.wait()
    every = pltpu.make_async_remote_copy(
        src_ref=buf.at[pl.ds(0, count - 1), 0],
        dst_ref=buf.at[pl.ds(0, count - 1), 0],
        send_sem=send_sem,
        recv_sem=recv_sem,
        device_id=(group_at, lax.rem(tp_at + 1, count)),
        device_id_type=pl.DeviceIdType.MESH,
    )
    every.wait_recv()
    onward = pltpu.make_async_remote_copy(
        src_ref=buf.at[:, core],
        dst_ref=buf.at[:, core],
        send_sem=pass_send,
        recv_sem=pass_recv,
        device_id=sibling,
        device_id_type=pl.DeviceIdType.MESH,
    )
    onward.start()
    every.wait_send()
    onward.wait_send()
    onward.wait_recv()
    o_ref[...] = buf[...]


def pair_gather(x, collective_id):
    shape = (lax.axis_size("tp"), 2) + x.shape
    return pl.pallas_call(
        _pair_gather_kernel,
        out_shape=jax.ShapeDtypeStruct(shape, x.dtype),
        in_specs=[pl.BlockSpec(memory_space=pltpu.VMEM)],
        out_specs=pl.BlockSpec(memory_space=pltpu.VMEM),
        scratch_shapes=[pltpu.VMEM(shape, x.dtype)] + [pltpu.SemaphoreType.DMA(())] * 5,
        compiler_params=pltpu.CompilerParams(collective_id=collective_id, has_side_effects=True),
    )(x)


def pair_exchange(x, collective_id):
    return _transfer(x, "pair", False, collective_id)


def group_exchange(x, collective_id):
    return _transfer(x, "group", False, collective_id)


def tp_exchange(x, collective_id):
    return _transfer(x, "tp", False, collective_id)


def tp_gather(x, collective_id):
    return _transfer(x, "tp", True, collective_id)


def rotate(values, positions):
    half_dim = values.shape[-1] // 2
    inverse = THETA ** (-2.0 * jnp.arange(half_dim, dtype=jnp.float32) / values.shape[-1])
    angles = positions[:, None, None] * inverse[None, None, :]
    cosine = jnp.cos(angles)
    sine_part = jnp.sin(angles)
    first_part = values[..., :half_dim]
    second_part = values[..., half_dim:]
    return jnp.concatenate(
        [
            first_part * cosine - second_part * sine_part,
            second_part * cosine + first_part * sine_part,
        ],
        axis=-1,
    )


def attend(query_rows, kv_rows, cache_kv, cache_valid, sinks, length):
    block_len = query_rows.shape[0]
    kv_heads = kv_rows.shape[1] // (2 * HEAD)
    query_heads = query_rows.shape[1] // HEAD
    group_size = query_heads // kv_heads
    positions = (length + jnp.arange(block_len, dtype=jnp.int32)).astype(jnp.float32)
    query_rot = rotate(
        query_rows.astype(jnp.float32).reshape(block_len, query_heads, HEAD), positions
    ).astype(jnp.bfloat16)
    kv_parts = kv_rows.reshape(block_len, kv_heads, 2, HEAD)
    key_rot = rotate(kv_parts[:, :, 0].astype(jnp.float32), positions).astype(jnp.bfloat16)
    cache_parts = cache_kv.reshape(cache_kv.shape[0], kv_heads, 2, HEAD)
    all_keys = jnp.concatenate([cache_parts[:, :, 0], key_rot], axis=0)
    all_values = jnp.concatenate([cache_parts[:, :, 1], kv_parts[:, :, 1]], axis=0)
    token_order = jnp.arange(block_len, dtype=jnp.int32)
    causal = token_order[None, :] <= token_order[:, None]
    allowed = jnp.concatenate(
        [jnp.broadcast_to(cache_valid[None, :], (block_len, cache_valid.shape[0])), causal], axis=1
    )
    row_allowed = jnp.repeat(allowed, group_size, axis=0)
    score_scale = HEAD ** (-0.5)
    query_block = query_rot.reshape(block_len * group_size, HEAD)
    scores = (
        jnp.dot(query_block, all_keys[:, 0].T, preferred_element_type=jnp.float32) * score_scale
    )
    scores = jnp.where(row_allowed, scores, -jnp.inf)
    sink_rows = jnp.tile(sinks, block_len)
    row_max = jnp.maximum(jnp.max(scores, axis=1), sink_rows)
    weights = jnp.exp(scores - row_max[:, None])
    denominator = jnp.sum(weights, axis=1) + jnp.exp(sink_rows - row_max)
    blended = (
        jnp.dot(weights.astype(jnp.bfloat16), all_values[:, 0], preferred_element_type=jnp.float32)
        / denominator[:, None]
    )
    outputs = blended.astype(jnp.bfloat16).reshape(block_len, group_size * HEAD)
    return outputs


def lane_dense(rows):
    count, length = rows.shape
    padded = -(-length // 128) * 128
    rows = jnp.pad(rows, ((0, 0), (0, padded - length)))
    return rows.reshape(count, padded // 128, 128)


def on_device(
    queries,
    new_kv,
    local_cache,
    remote_pool,
    page_index,
    lengths,
    sinks,
    out_weight,
    residual,
    norm_gain,
    routes,
    route_weights,
    expert_gate,
    expert_up,
    expert_down,
):
    groups = lax.axis_size("group")
    lane_count = remote_pool.shape[1]
    local_len = local_cache.shape[0]
    fetched = group_exchange(remote_pool.reshape(groups, -1, lane_count), 1)
    page_len = fetched.shape[1]
    length = lengths[0]
    offsets = jnp.arange(page_len, dtype=jnp.int32)
    remote_pos = local_len + page_index[0][:, None] * page_len + offsets[None, :]
    cache_valid = jnp.concatenate(
        [jnp.ones((local_len,), jnp.bool_), (remote_pos < length).reshape(-1)]
    )
    cache_kv = jnp.concatenate([local_cache, fetched.reshape(-1, lane_count)], axis=0)
    attended = attend(queries, new_kv, cache_kv, cache_valid, sinks, length)
    width = residual.shape[1]
    tp_count = lax.axis_size("tp")
    start = lax.axis_index("tp") * width
    own_gain = lax.dynamic_slice_in_dim(norm_gain, start, width, 0)
    partial_sum = jnp.dot(attended, out_weight, preferred_element_type=jnp.float32)
    partial_blocks = partial_sum.reshape(partial_sum.shape[0], tp_count, width).transpose(1, 0, 2)
    own_attn = jnp.sum(tp_exchange(partial_blocks.astype(jnp.bfloat16), 6).astype(jnp.float32), axis=0)
    own_state = own_attn + residual.astype(jnp.float32)
    square_sum = jnp.sum(own_state * own_state, axis=1, keepdims=True)
    square_high = square_sum.astype(jnp.bfloat16)
    square_low = (square_sum - square_high.astype(jnp.float32)).astype(jnp.bfloat16)
    row_width = -(-(width + 2) // 128) * 128
    scaled_own = (own_state * own_gain).astype(jnp.bfloat16)
    normed_own = jnp.concatenate(
        [scaled_own, square_high, square_low, jnp.zeros((own_state.shape[0], row_width - width - 2), jnp.bfloat16)],
        axis=1,
    )
    block_len = normed_own.shape[0]
    top_count = routes.shape[1]
    experts = groups // 2
    capacity = 5 * block_len * top_count // (4 * experts)
    member = jnp.any(
        routes[:, :, None] == jnp.arange(experts, dtype=jnp.int32)[None, None, :], axis=1
    ).astype(jnp.int32)
    slot_rank = jnp.cumsum(member, axis=0) - member
    slot_hit = member[:, :, None] * (
        slot_rank[:, :, None] == jnp.arange(capacity, dtype=jnp.int32)[None, None, :]
    ).astype(jnp.int32)
    slot_matrix = slot_hit.transpose(1, 2, 0).reshape(experts * capacity, block_len)
    send_own = jnp.dot(
        slot_matrix.astype(jnp.bfloat16), normed_own, preferred_element_type=jnp.float32
    ).astype(jnp.bfloat16)
    hidden_part = expert_gate.shape[2]
    row_width = send_own.shape[1]
    received = pair_exchange(lane_dense(send_own.reshape(experts, capacity * row_width)), 2)
    received = received.reshape(experts, -1)[:, : capacity * row_width].reshape(experts, capacity, row_width)
    sources, slot_count, part_features = received.shape
    whole = pair_gather(received.reshape(sources * slot_count, part_features), 4)
    whole = whole.reshape(tp_count, 2 * sources * slot_count, part_features)
    total_square = jnp.sum(whole[:, :, width:width + 2].astype(jnp.float32), axis=(0, 2))
    row_scale = lax.rsqrt(total_square / (width * tp_count) + EPSILON)
    tokens = whole[:, :, :width]
    gate_view = expert_gate[0].reshape(tp_count, width, hidden_part)
    up_view = expert_up[0].reshape(tp_count, width, hidden_part)
    both = jnp.concatenate(
        [
            jnp.einsum("tsf,tfh->sh", tokens, gate_view, preferred_element_type=jnp.float32),
            jnp.einsum("tsf,tfh->sh", tokens, up_view, preferred_element_type=jnp.float32),
        ],
        axis=1,
    )
    both = both * row_scale[:, None]
    gate_val = both[:, :hidden_part]
    up_val = both[:, hidden_part:]
    active = (gate_val * jax.nn.sigmoid(ALPHA * gate_val) * (up_val + 1.0)).astype(jnp.bfloat16)
    joined = tp_gather(active.T, 5)
    down_blocks = expert_down[0].reshape(tp_count, hidden_part, expert_down.shape[2])
    result = jnp.einsum("ths,thd->sd", joined, down_blocks, preferred_element_type=jnp.float32).astype(
        jnp.bfloat16
    )
    halves = result.reshape(2, experts, capacity, width)
    core = lax.rem(lax.axis_index("group"), 2)
    groups_total = lax.axis_size("group")
    swap = [(i, i + 1 - 2 * (i % 2)) for i in range(groups_total)]
    mine = lax.dynamic_index_in_dim(halves, core, 0, keepdims=False)
    theirs = lax.dynamic_index_in_dim(halves, 1 - core, 0, keepdims=False)
    other_half = lax.ppermute(theirs, "group", swap)
    joined_halves = (mine.astype(jnp.float32) + other_half.astype(jnp.float32)).astype(jnp.bfloat16)
    arrived = pair_exchange(lane_dense(joined_halves.reshape(experts, capacity * width)), 3)
    summed = arrived.reshape(experts, -1)[:, : capacity * width].astype(jnp.float32).reshape(experts * capacity, width)
    mixing = route_weights / jnp.sum(route_weights, axis=1, keepdims=True)
    expert_weight = jnp.sum(
        jnp.where(routes[:, :, None] == jnp.arange(experts, dtype=jnp.int32)[None, None, :], mixing[:, :, None], 0.0),
        axis=1,
    )
    combine = (slot_hit.astype(jnp.float32) * expert_weight[:, :, None]).reshape(block_len, experts * capacity)
    moe_out = jnp.dot(combine, summed, precision=lax.Precision.HIGHEST, preferred_element_type=jnp.float32)
    return (own_state + moe_out).astype(jnp.bfloat16)


def solution(mesh):
    return jax.shard_map(
        on_device,
        mesh=mesh,
        in_specs=(
            P("group", "tp"),
            P("group", "tp"),
            P("group", "tp"),
            P("group", "tp"),
            P("group", None),
            P("group"),
            P("tp"),
            P("tp", None),
            P("group", "tp"),
            P(),
            P("group", None),
            P("group", None),
            P("group", None, "tp"),
            P("group", None, "tp"),
            P("group", None, "tp"),
        ),
        out_specs=P("group", "tp"),
        check_vma=False,
    )
```

```python
import functools

import jax
import jax.numpy as jnp
from jax import lax
from jax.experimental import pallas as pl
from jax.experimental.pallas import tpu as pltpu
from jax.sharding import PartitionSpec as P

HEAD = 64


THETA = 150000.0
ALPHA = 1.702
EPSILON = 1e-05


def _row_parts(rows, parts=8):
    if not rows:
        return [(0, 0)]
    step = -(-rows // (parts * 16)) * 16
    return [(first, min(step, rows - first)) for first in range(0, rows, step)]


def _transfer_kernel(axis, gather, x_ref, o_ref, buf, send_sem, recv_sem, local_sem):
    count = buf.shape[0]
    group_at = lax.axis_index("group")
    tp_at = lax.axis_index("tp")
    core = lax.rem(group_at, 2)
    if axis == "tp":
        me = tp_at
    elif axis == "pair":
        me = lax.div(group_at, 2)
    else:
        me = group_at

    def device(peer):
        if axis == "tp":
            return (group_at, peer)
        if axis == "pair":
            return (2 * peer + core, tp_at)
        return (peer, tp_at)

    def piece(peer):
        return x_ref if gather else x_ref.at[peer]

    barrier = pltpu.get_barrier_semaphore()

    def greet(step, carry):
        peer = lax.rem(me + step, count)
        pl.semaphore_signal(barrier, inc=1, device_id=device(peer), device_id_type=pl.DeviceIdType.MESH)
        return carry

    lax.fori_loop(1, count, greet, 0)
    pl.semaphore_wait(barrier, count - 1)
    local = pltpu.make_async_copy(piece(me), buf.at[me], local_sem)
    local.start()

    for first, size in _row_parts(buf.shape[1] if (gather or axis == "tp") else 0):

        def send(step, carry, first=first, size=size):
            peer = lax.rem(me + step, count)
            src = piece(peer)
            dst = buf.at[me]
            if size:
                src = src.at[pl.ds(first, size)]
                dst = dst.at[pl.ds(first, size)]
            pltpu.make_async_remote_copy(
                src_ref=src,
                dst_ref=dst,
                send_sem=send_sem,
                recv_sem=recv_sem,
                device_id=device(peer),
                device_id_type=pl.DeviceIdType.MESH,
            ).start()
            return carry

        lax.fori_loop(1, count, send, 0)
    local.wait()
    every = pltpu.make_async_remote_copy(
        src_ref=buf.at[pl.ds(0, count - 1)],
        dst_ref=buf.at[pl.ds(0, count - 1)],
        send_sem=send_sem,
        recv_sem=recv_sem,
        device_id=device(lax.rem(me + 1, count)),
        device_id_type=pl.DeviceIdType.MESH,
    )
    every.wait_send()
    every.wait_recv()
    o_ref[...] = buf[...]


def _transfer(x, axis, gather, collective_id):
    count = lax.axis_size("group") // 2 if axis == "pair" else lax.axis_size(axis)
    shape = ((count,) + x.shape) if gather else x.shape
    return pl.pallas_call(
        functools.partial(_transfer_kernel, axis, gather),
        out_shape=jax.ShapeDtypeStruct(shape, x.dtype),
        in_specs=[pl.BlockSpec(memory_space=pltpu.VMEM)],
        out_specs=pl.BlockSpec(memory_space=pltpu.VMEM),
        scratch_shapes=[
            pltpu.VMEM(shape, x.dtype),
            pltpu.SemaphoreType.DMA(()),
            pltpu.SemaphoreType.DMA(()),
            pltpu.SemaphoreType.DMA(()),
        ],
        compiler_params=pltpu.CompilerParams(collective_id=collective_id, has_side_effects=True),
    )(x)


def _pair_gather_kernel(x_ref, o_ref, buf, send_sem, recv_sem, local_sem, pass_send, pass_recv):
    count = buf.shape[0]
    group_at = lax.axis_index("group")
    tp_at = lax.axis_index("tp")
    core = lax.rem(group_at, 2)
    sibling = (group_at + 1 - 2 * core, tp_at)
    barrier = pltpu.get_barrier_semaphore()

    def greet(step, carry):
        peer = lax.rem(tp_at + step, count)
        pl.semaphore_signal(barrier, inc=1, device_id=(group_at, peer), device_id_type=pl.DeviceIdType.MESH)
        return carry

    lax.fori_loop(1, count, greet, 0)
    pl.semaphore_signal(barrier, inc=1, device_id=sibling, device_id_type=pl.DeviceIdType.MESH)
    pl.semaphore_wait(barrier, count)
    local = pltpu.make_async_copy(x_ref, buf.at[tp_at, core], local_sem)
    local.start()
    pltpu.make_async_remote_copy(
        src_ref=x_ref,
        dst_ref=buf.at[tp_at, core],
        send_sem=pass_send,
        recv_sem=pass_recv,
        device_id=sibling,
        device_id_type=pl.DeviceIdType.MESH,
    ).start()

    for first, size in _row_parts(x_ref.shape[0]):

        def send(step, carry, first=first, size=size):
            peer = lax.rem(tp_at + step, count)
            pltpu.make_async_remote_copy(
                src_ref=x_ref.at[pl.ds(first, size)],
                dst_ref=buf.at[tp_at, core, pl.ds(first, size)],
                send_sem=send_sem,
                recv_sem=recv_sem,
                device_id=(group_at, peer),
                device_id_type=pl.DeviceIdType.MESH,
            ).start()
            return carry

        lax.fori_loop(1, count, send, 0)
    local.wait()
    every = pltpu.make_async_remote_copy(
        src_ref=buf.at[pl.ds(0, count - 1), 0],
        dst_ref=buf.at[pl.ds(0, count - 1), 0],
        send_sem=send_sem,
        recv_sem=recv_sem,
        device_id=(group_at, lax.rem(tp_at + 1, count)),
        device_id_type=pl.DeviceIdType.MESH,
    )
    every.wait_recv()

    def relay(step, carry):
        source = lax.rem(tp_at + count - step, count)
        pltpu.make_async_remote_copy(
            src_ref=buf.at[source, core],
            dst_ref=buf.at[source, core],
            send_sem=pass_send,
            recv_sem=pass_recv,
            device_id=sibling,
            device_id_type=pl.DeviceIdType.MESH,
        ).start()
        return carry

    lax.fori_loop(1, count, relay, 0)
    onward = pltpu.make_async_remote_copy(
        src_ref=buf.at[:, core],
        dst_ref=buf.at[:, core],
        send_sem=pass_send,
        recv_sem=pass_recv,
        device_id=sibling,
        device_id_type=pl.DeviceIdType.MESH,
    )
    every.wait_send()
    onward.wait_send()
    onward.wait_recv()
    o_ref[...] = buf[...]


def pair_gather(x, collective_id):
    shape = (lax.axis_size("tp"), 2) + x.shape
    return pl.pallas_call(
        _pair_gather_kernel,
        out_shape=jax.ShapeDtypeStruct(shape, x.dtype),
        in_specs=[pl.BlockSpec(memory_space=pltpu.VMEM)],
        out_specs=pl.BlockSpec(memory_space=pltpu.VMEM),
        scratch_shapes=[pltpu.VMEM(shape, x.dtype)] + [pltpu.SemaphoreType.DMA(())] * 5,
        compiler_params=pltpu.CompilerParams(collective_id=collective_id, has_side_effects=True),
    )(x)


def pair_exchange(x, collective_id):
    return _transfer(x, "pair", False, collective_id)


def group_exchange(x, collective_id):
    return _transfer(x, "group", False, collective_id)


def tp_exchange(x, collective_id):
    return _transfer(x, "tp", False, collective_id)


def tp_gather(x, collective_id):
    return _transfer(x, "tp", True, collective_id)


def rotate(values, positions):
    half_dim = values.shape[-1] // 2
    inverse = THETA ** (-2.0 * jnp.arange(half_dim, dtype=jnp.float32) / values.shape[-1])
    angles = positions[:, None, None] * inverse[None, None, :]
    cosine = jnp.cos(angles)
    sine_part = jnp.sin(angles)
    first_part = values[..., :half_dim]
    second_part = values[..., half_dim:]
    return jnp.concatenate(
        [
            first_part * cosine - second_part * sine_part,
            second_part * cosine + first_part * sine_part,
        ],
        axis=-1,
    )


def attend(query_rows, kv_rows, cache_kv, cache_valid, sinks, length):
    block_len = query_rows.shape[0]
    kv_heads = kv_rows.shape[1] // (2 * HEAD)
    query_heads = query_rows.shape[1] // HEAD
    group_size = query_heads // kv_heads
    positions = (length + jnp.arange(block_len, dtype=jnp.int32)).astype(jnp.float32)
    query_rot = rotate(
        query_rows.astype(jnp.float32).reshape(block_len, query_heads, HEAD), positions
    ).astype(jnp.bfloat16)
    kv_parts = kv_rows.reshape(block_len, kv_heads, 2, HEAD)
    key_rot = rotate(kv_parts[:, :, 0].astype(jnp.float32), positions).astype(jnp.bfloat16)
    cache_parts = cache_kv.reshape(cache_kv.shape[0], kv_heads, 2, HEAD)
    all_keys = jnp.concatenate([cache_parts[:, :, 0], key_rot], axis=0)
    all_values = jnp.concatenate([cache_parts[:, :, 1], kv_parts[:, :, 1]], axis=0)
    token_order = jnp.arange(block_len, dtype=jnp.int32)
    causal = token_order[None, :] <= token_order[:, None]
    allowed = jnp.concatenate(
        [jnp.broadcast_to(cache_valid[None, :], (block_len, cache_valid.shape[0])), causal], axis=1
    )
    row_allowed = jnp.repeat(allowed, group_size, axis=0)
    score_scale = HEAD ** (-0.5)
    query_block = query_rot.reshape(block_len * group_size, HEAD)
    scores = (
        jnp.dot(query_block, all_keys[:, 0].T, preferred_element_type=jnp.float32) * score_scale
    )
    scores = jnp.where(row_allowed, scores, -jnp.inf)
    sink_rows = jnp.tile(sinks, block_len)
    row_max = jnp.maximum(jnp.max(scores, axis=1), sink_rows)
    weights = jnp.exp(scores - row_max[:, None])
    denominator = jnp.sum(weights, axis=1) + jnp.exp(sink_rows - row_max)
    blended = (
        jnp.dot(weights.astype(jnp.bfloat16), all_values[:, 0], preferred_element_type=jnp.float32)
        / denominator[:, None]
    )
    outputs = blended.astype(jnp.bfloat16).reshape(block_len, group_size * HEAD)
    return outputs


def lane_dense(rows):
    count, length = rows.shape
    padded = -(-length // 128) * 128
    rows = jnp.pad(rows, ((0, 0), (0, padded - length)))
    return rows.reshape(count, padded // 128, 128)


def on_device(
    queries,
    new_kv,
    local_cache,
    remote_pool,
    page_index,
    lengths,
    sinks,
    out_weight,
    residual,
    norm_gain,
    routes,
    route_weights,
    expert_gate,
    expert_up,
    expert_down,
):
    groups = lax.axis_size("group")
    lane_count = remote_pool.shape[1]
    local_len = local_cache.shape[0]
    fetched = group_exchange(remote_pool.reshape(groups, -1, lane_count), 1)
    page_len = fetched.shape[1]
    length = lengths[0]
    offsets = jnp.arange(page_len, dtype=jnp.int32)
    remote_pos = local_len + page_index[0][:, None] * page_len + offsets[None, :]
    cache_valid = jnp.concatenate(
        [jnp.ones((local_len,), jnp.bool_), (remote_pos < length).reshape(-1)]
    )
    cache_kv = jnp.concatenate([local_cache, fetched.reshape(-1, lane_count)], axis=0)
    attended = attend(queries, new_kv, cache_kv, cache_valid, sinks, length)
    width = residual.shape[1]
    tp_count = lax.axis_size("tp")
    start = lax.axis_index("tp") * width
    own_gain = lax.dynamic_slice_in_dim(norm_gain, start, width, 0)
    partial_sum = jnp.dot(attended, out_weight, preferred_element_type=jnp.float32)
    partial_blocks = partial_sum.reshape(partial_sum.shape[0], tp_count, width).transpose(1, 0, 2)
    own_attn = jnp.sum(tp_exchange(partial_blocks.astype(jnp.bfloat16), 6).astype(jnp.float32), axis=0)
    own_state = own_attn + residual.astype(jnp.float32)
    square_sum = jnp.sum(own_state * own_state, axis=1, keepdims=True)
    square_high = square_sum.astype(jnp.bfloat16)
    square_low = (square_sum - square_high.astype(jnp.float32)).astype(jnp.bfloat16)
    row_width = -(-(width + 2) // 128) * 128
    scaled_own = (own_state * own_gain).astype(jnp.bfloat16)
    normed_own = jnp.concatenate(
        [scaled_own, square_high, square_low, jnp.zeros((own_state.shape[0], row_width - width - 2), jnp.bfloat16)],
        axis=1,
    )
    block_len = normed_own.shape[0]
    top_count = routes.shape[1]
    experts = groups // 2
    capacity = 5 * block_len * top_count // (4 * experts)
    member = jnp.any(
        routes[:, :, None] == jnp.arange(experts, dtype=jnp.int32)[None, None, :], axis=1
    ).astype(jnp.int32)
    slot_rank = jnp.cumsum(member, axis=0) - member
    slot_hit = member[:, :, None] * (
        slot_rank[:, :, None] == jnp.arange(capacity, dtype=jnp.int32)[None, None, :]
    ).astype(jnp.int32)
    slot_matrix = slot_hit.transpose(1, 2, 0).reshape(experts * capacity, block_len)
    send_own = jnp.dot(
        slot_matrix.astype(jnp.bfloat16), normed_own, preferred_element_type=jnp.float32
    ).astype(jnp.bfloat16)
    hidden_part = expert_gate.shape[2]
    row_width = send_own.shape[1]
    received = pair_exchange(lane_dense(send_own.reshape(experts, capacity * row_width)), 2)
    received = received.reshape(experts, -1)[:, : capacity * row_width].reshape(experts, capacity, row_width)
    sources, slot_count, part_features = received.shape
    whole = pair_gather(received.reshape(sources * slot_count, part_features), 4)
    whole = whole.reshape(tp_count, 2 * sources * slot_count, part_features)
    total_square = jnp.sum(whole[:, :, width:width + 2].astype(jnp.float32), axis=(0, 2))
    row_scale = lax.rsqrt(total_square / (width * tp_count) + EPSILON)
    tokens = whole[:, :, :width]
    gate_view = expert_gate[0].reshape(tp_count, width, hidden_part)
    up_view = expert_up[0].reshape(tp_count, width, hidden_part)
    both = jnp.concatenate(
        [
            jnp.einsum("tsf,tfh->sh", tokens, gate_view, preferred_element_type=jnp.float32),
            jnp.einsum("tsf,tfh->sh", tokens, up_view, preferred_element_type=jnp.float32),
        ],
        axis=1,
    )
    both = both * row_scale[:, None]
    gate_val = both[:, :hidden_part]
    up_val = both[:, hidden_part:]
    active = (gate_val * jax.nn.sigmoid(ALPHA * gate_val) * (up_val + 1.0)).astype(jnp.bfloat16)
    joined = tp_gather(active.T, 5)
    down_blocks = expert_down[0].reshape(tp_count, hidden_part, expert_down.shape[2])
    result = jnp.einsum("ths,thd->sd", joined, down_blocks, preferred_element_type=jnp.float32).astype(
        jnp.bfloat16
    )
    halves = result.reshape(2, experts, capacity, width)
    core = lax.rem(lax.axis_index("group"), 2)
    groups_total = lax.axis_size("group")
    swap = [(i, i + 1 - 2 * (i % 2)) for i in range(groups_total)]
    mine = lax.dynamic_index_in_dim(halves, core, 0, keepdims=False)
    theirs = lax.dynamic_index_in_dim(halves, 1 - core, 0, keepdims=False)
    other_half = lax.ppermute(theirs, "group", swap)
    joined_halves = (mine.astype(jnp.float32) + other_half.astype(jnp.float32)).astype(jnp.bfloat16)
    arrived = pair_exchange(lane_dense(joined_halves.reshape(experts, capacity * width)), 3)
    summed = arrived.reshape(experts, -1)[:, : capacity * width].astype(jnp.float32).reshape(experts * capacity, width)
    mixing = route_weights / jnp.sum(route_weights, axis=1, keepdims=True)
    expert_weight = jnp.sum(
        jnp.where(routes[:, :, None] == jnp.arange(experts, dtype=jnp.int32)[None, None, :], mixing[:, :, None], 0.0),
        axis=1,
    )
    combine = (slot_hit.astype(jnp.float32) * expert_weight[:, :, None]).reshape(block_len, experts * capacity)
    moe_out = jnp.dot(combine, summed, precision=lax.Precision.HIGHEST, preferred_element_type=jnp.float32)
    return (own_state + moe_out).astype(jnp.bfloat16)


def solution(mesh):
    return jax.shard_map(
        on_device,
        mesh=mesh,
        in_specs=(
            P("group", "tp"),
            P("group", "tp"),
            P("group", "tp"),
            P("group", "tp"),
            P("group", None),
            P("group"),
            P("tp"),
            P("tp", None),
            P("group", "tp"),
            P(),
            P("group", None),
            P("group", None),
            P("group", None, "tp"),
            P("group", None, "tp"),
            P("group", None, "tp"),
        ),
        out_specs=P("group", "tp"),
        check_vma=False,
    )
```

```python
import functools

import jax
import jax.numpy as jnp
from jax import lax
from jax.experimental import pallas as pl
from jax.experimental.pallas import tpu as pltpu
from jax.sharding import PartitionSpec as P

HEAD = 64


THETA = 150000.0
ALPHA = 1.702
EPSILON = 1e-05


def _offset(step, count):
    odd = lax.rem(step, 2)
    return odd * lax.div(step + 1, 2) + (1 - odd) * (count - lax.div(step, 2))


def _row_parts(rows, parts=8):
    if not rows:
        return [(0, 0)]
    step = -(-rows // (parts * 16)) * 16
    return [(first, min(step, rows - first)) for first in range(0, rows, step)]


def _transfer_kernel(axis, gather, x_ref, o_ref, buf, send_sem, recv_sem, local_sem):
    count = buf.shape[0]
    group_at = lax.axis_index("group")
    tp_at = lax.axis_index("tp")
    core = lax.rem(group_at, 2)
    if axis == "tp":
        me = tp_at
    elif axis == "pair":
        me = lax.div(group_at, 2)
    else:
        me = group_at

    def device(peer):
        if axis == "tp":
            return (group_at, peer)
        if axis == "pair":
            return (2 * peer + core, tp_at)
        return (peer, tp_at)

    def piece(peer):
        return x_ref if gather else x_ref.at[peer]

    barrier = pltpu.get_barrier_semaphore()

    def greet(step, carry):
        peer = lax.rem(me + step, count)
        pl.semaphore_signal(barrier, inc=1, device_id=device(peer), device_id_type=pl.DeviceIdType.MESH)
        return carry

    lax.fori_loop(1, count, greet, 0)
    pl.semaphore_wait(barrier, count - 1)
    local = pltpu.make_async_copy(piece(me), buf.at[me], local_sem)
    local.start()

    for first, size in _row_parts(buf.shape[1] if (gather or axis == "tp") else 0):

        def send(step, carry, first=first, size=size):
            peer = lax.rem(me + _offset(step, count), count)
            src = piece(peer)
            dst = buf.at[me]
            if size:
                src = src.at[pl.ds(first, size)]
                dst = dst.at[pl.ds(first, size)]
            pltpu.make_async_remote_copy(
                src_ref=src,
                dst_ref=dst,
                send_sem=send_sem,
                recv_sem=recv_sem,
                device_id=device(peer),
                device_id_type=pl.DeviceIdType.MESH,
            ).start()
            return carry

        lax.fori_loop(1, count, send, 0)
    local.wait()
    every = pltpu.make_async_remote_copy(
        src_ref=buf.at[pl.ds(0, count - 1)],
        dst_ref=buf.at[pl.ds(0, count - 1)],
        send_sem=send_sem,
        recv_sem=recv_sem,
        device_id=device(lax.rem(me + 1, count)),
        device_id_type=pl.DeviceIdType.MESH,
    )
    every.wait_send()
    every.wait_recv()
    o_ref[...] = buf[...]


def _transfer(x, axis, gather, collective_id):
    count = lax.axis_size("group") // 2 if axis == "pair" else lax.axis_size(axis)
    shape = ((count,) + x.shape) if gather else x.shape
    return pl.pallas_call(
        functools.partial(_transfer_kernel, axis, gather),
        out_shape=jax.ShapeDtypeStruct(shape, x.dtype),
        in_specs=[pl.BlockSpec(memory_space=pltpu.VMEM)],
        out_specs=pl.BlockSpec(memory_space=pltpu.VMEM),
        scratch_shapes=[
            pltpu.VMEM(shape, x.dtype),
            pltpu.SemaphoreType.DMA(()),
            pltpu.SemaphoreType.DMA(()),
            pltpu.SemaphoreType.DMA(()),
        ],
        compiler_params=pltpu.CompilerParams(collective_id=collective_id, has_side_effects=True),
    )(x)


def _pair_gather_kernel(x_ref, o_ref, buf, send_sem, recv_sem, local_sem, pass_send, pass_recv):
    count = buf.shape[0]
    group_at = lax.axis_index("group")
    tp_at = lax.axis_index("tp")
    core = lax.rem(group_at, 2)
    sibling = (group_at + 1 - 2 * core, tp_at)
    barrier = pltpu.get_barrier_semaphore()

    def greet(step, carry):
        peer = lax.rem(tp_at + step, count)
        pl.semaphore_signal(barrier, inc=1, device_id=(group_at, peer), device_id_type=pl.DeviceIdType.MESH)
        return carry

    lax.fori_loop(1, count, greet, 0)
    pl.semaphore_signal(barrier, inc=1, device_id=sibling, device_id_type=pl.DeviceIdType.MESH)
    pl.semaphore_wait(barrier, count)
    local = pltpu.make_async_copy(x_ref, buf.at[tp_at, core], local_sem)
    local.start()
    pltpu.make_async_remote_copy(
        src_ref=x_ref,
        dst_ref=buf.at[tp_at, core],
        send_sem=pass_send,
        recv_sem=pass_recv,
        device_id=sibling,
        device_id_type=pl.DeviceIdType.MESH,
    ).start()

    for first, size in _row_parts(x_ref.shape[0]):

        def send(step, carry, first=first, size=size):
            peer = lax.rem(tp_at + _offset(step, count), count)
            pltpu.make_async_remote_copy(
                src_ref=x_ref.at[pl.ds(first, size)],
                dst_ref=buf.at[tp_at, core, pl.ds(first, size)],
                send_sem=send_sem,
                recv_sem=recv_sem,
                device_id=(group_at, peer),
                device_id_type=pl.DeviceIdType.MESH,
            ).start()
            return carry

        lax.fori_loop(1, count, send, 0)
    local.wait()
    every = pltpu.make_async_remote_copy(
        src_ref=buf.at[pl.ds(0, count - 1), 0],
        dst_ref=buf.at[pl.ds(0, count - 1), 0],
        send_sem=send_sem,
        recv_sem=recv_sem,
        device_id=(group_at, lax.rem(tp_at + 1, count)),
        device_id_type=pl.DeviceIdType.MESH,
    )
    every.wait_recv()

    def relay(step, carry):
        source = lax.rem(tp_at + count - step, count)
        pltpu.make_async_remote_copy(
            src_ref=buf.at[source, core],
            dst_ref=buf.at[source, core],
            send_sem=pass_send,
            recv_sem=pass_recv,
            device_id=sibling,
            device_id_type=pl.DeviceIdType.MESH,
        ).start()
        return carry

    lax.fori_loop(1, count, relay, 0)
    onward = pltpu.make_async_remote_copy(
        src_ref=buf.at[:, core],
        dst_ref=buf.at[:, core],
        send_sem=pass_send,
        recv_sem=pass_recv,
        device_id=sibling,
        device_id_type=pl.DeviceIdType.MESH,
    )
    every.wait_send()
    onward.wait_send()
    onward.wait_recv()
    o_ref[...] = buf[...]


def pair_gather(x, collective_id):
    shape = (lax.axis_size("tp"), 2) + x.shape
    return pl.pallas_call(
        _pair_gather_kernel,
        out_shape=jax.ShapeDtypeStruct(shape, x.dtype),
        in_specs=[pl.BlockSpec(memory_space=pltpu.VMEM)],
        out_specs=pl.BlockSpec(memory_space=pltpu.VMEM),
        scratch_shapes=[pltpu.VMEM(shape, x.dtype)] + [pltpu.SemaphoreType.DMA(())] * 5,
        compiler_params=pltpu.CompilerParams(collective_id=collective_id, has_side_effects=True),
    )(x)


def pair_exchange(x, collective_id):
    return _transfer(x, "pair", False, collective_id)


def group_exchange(x, collective_id):
    return _transfer(x, "group", False, collective_id)


def tp_exchange(x, collective_id):
    return _transfer(x, "tp", False, collective_id)


def tp_gather(x, collective_id):
    return _transfer(x, "tp", True, collective_id)


def rotate(values, positions):
    half_dim = values.shape[-1] // 2
    inverse = THETA ** (-2.0 * jnp.arange(half_dim, dtype=jnp.float32) / values.shape[-1])
    angles = positions[:, None, None] * inverse[None, None, :]
    cosine = jnp.cos(angles)
    sine_part = jnp.sin(angles)
    first_part = values[..., :half_dim]
    second_part = values[..., half_dim:]
    return jnp.concatenate(
        [
            first_part * cosine - second_part * sine_part,
            second_part * cosine + first_part * sine_part,
        ],
        axis=-1,
    )


def attend(query_rows, kv_rows, cache_kv, cache_valid, sinks, length):
    block_len = query_rows.shape[0]
    kv_heads = kv_rows.shape[1] // (2 * HEAD)
    query_heads = query_rows.shape[1] // HEAD
    group_size = query_heads // kv_heads
    positions = (length + jnp.arange(block_len, dtype=jnp.int32)).astype(jnp.float32)
    query_rot = rotate(
        query_rows.astype(jnp.float32).reshape(block_len, query_heads, HEAD), positions
    ).astype(jnp.bfloat16)
    kv_parts = kv_rows.reshape(block_len, kv_heads, 2, HEAD)
    key_rot = rotate(kv_parts[:, :, 0].astype(jnp.float32), positions).astype(jnp.bfloat16)
    cache_parts = cache_kv.reshape(cache_kv.shape[0], kv_heads, 2, HEAD)
    all_keys = jnp.concatenate([cache_parts[:, :, 0], key_rot], axis=0)
    all_values = jnp.concatenate([cache_parts[:, :, 1], kv_parts[:, :, 1]], axis=0)
    token_order = jnp.arange(block_len, dtype=jnp.int32)
    causal = token_order[None, :] <= token_order[:, None]
    allowed = jnp.concatenate(
        [jnp.broadcast_to(cache_valid[None, :], (block_len, cache_valid.shape[0])), causal], axis=1
    )
    row_allowed = jnp.repeat(allowed, group_size, axis=0)
    score_scale = HEAD ** (-0.5)
    query_block = query_rot.reshape(block_len * group_size, HEAD)
    scores = (
        jnp.dot(query_block, all_keys[:, 0].T, preferred_element_type=jnp.float32) * score_scale
    )
    scores = jnp.where(row_allowed, scores, -jnp.inf)
    sink_rows = jnp.tile(sinks, block_len)
    row_max = jnp.maximum(jnp.max(scores, axis=1), sink_rows)
    weights = jnp.exp(scores - row_max[:, None])
    denominator = jnp.sum(weights, axis=1) + jnp.exp(sink_rows - row_max)
    blended = (
        jnp.dot(weights.astype(jnp.bfloat16), all_values[:, 0], preferred_element_type=jnp.float32)
        / denominator[:, None]
    )
    outputs = blended.astype(jnp.bfloat16).reshape(block_len, group_size * HEAD)
    return outputs


def lane_dense(rows):
    count, length = rows.shape
    padded = -(-length // 128) * 128
    rows = jnp.pad(rows, ((0, 0), (0, padded - length)))
    return rows.reshape(count, padded // 128, 128)


def on_device(
    queries,
    new_kv,
    local_cache,
    remote_pool,
    page_index,
    lengths,
    sinks,
    out_weight,
    residual,
    norm_gain,
    routes,
    route_weights,
    expert_gate,
    expert_up,
    expert_down,
):
    groups = lax.axis_size("group")
    lane_count = remote_pool.shape[1]
    local_len = local_cache.shape[0]
    fetched = group_exchange(remote_pool.reshape(groups, -1, lane_count), 1)
    page_len = fetched.shape[1]
    length = lengths[0]
    offsets = jnp.arange(page_len, dtype=jnp.int32)
    remote_pos = local_len + page_index[0][:, None] * page_len + offsets[None, :]
    cache_valid = jnp.concatenate(
        [jnp.ones((local_len,), jnp.bool_), (remote_pos < length).reshape(-1)]
    )
    cache_kv = jnp.concatenate([local_cache, fetched.reshape(-1, lane_count)], axis=0)
    attended = attend(queries, new_kv, cache_kv, cache_valid, sinks, length)
    width = residual.shape[1]
    tp_count = lax.axis_size("tp")
    start = lax.axis_index("tp") * width
    own_gain = lax.dynamic_slice_in_dim(norm_gain, start, width, 0)
    partial_sum = jnp.dot(attended, out_weight, preferred_element_type=jnp.float32)
    partial_blocks = partial_sum.reshape(partial_sum.shape[0], tp_count, width).transpose(1, 0, 2)
    own_attn = jnp.sum(tp_exchange(partial_blocks.astype(jnp.bfloat16), 6).astype(jnp.float32), axis=0)
    own_state = own_attn + residual.astype(jnp.float32)
    square_sum = jnp.sum(own_state * own_state, axis=1, keepdims=True)
    square_high = square_sum.astype(jnp.bfloat16)
    square_low = (square_sum - square_high.astype(jnp.float32)).astype(jnp.bfloat16)
    row_width = -(-(width + 2) // 128) * 128
    scaled_own = (own_state * own_gain).astype(jnp.bfloat16)
    normed_own = jnp.concatenate(
        [scaled_own, square_high, square_low, jnp.zeros((own_state.shape[0], row_width - width - 2), jnp.bfloat16)],
        axis=1,
    )
    block_len = normed_own.shape[0]
    top_count = routes.shape[1]
    experts = groups // 2
    capacity = 5 * block_len * top_count // (4 * experts)
    member = jnp.any(
        routes[:, :, None] == jnp.arange(experts, dtype=jnp.int32)[None, None, :], axis=1
    ).astype(jnp.int32)
    slot_rank = jnp.cumsum(member, axis=0) - member
    slot_hit = member[:, :, None] * (
        slot_rank[:, :, None] == jnp.arange(capacity, dtype=jnp.int32)[None, None, :]
    ).astype(jnp.int32)
    slot_matrix = slot_hit.transpose(1, 2, 0).reshape(experts * capacity, block_len)
    send_own = jnp.dot(
        slot_matrix.astype(jnp.bfloat16), normed_own, preferred_element_type=jnp.float32
    ).astype(jnp.bfloat16)
    hidden_part = expert_gate.shape[2]
    row_width = send_own.shape[1]
    received = pair_exchange(lane_dense(send_own.reshape(experts, capacity * row_width)), 2)
    received = received.reshape(experts, -1)[:, : capacity * row_width].reshape(experts, capacity, row_width)
    sources, slot_count, part_features = received.shape
    whole = pair_gather(received.reshape(sources * slot_count, part_features), 4)
    whole = whole.reshape(tp_count, 2 * sources * slot_count, part_features)
    total_square = jnp.sum(whole[:, :, width:width + 2].astype(jnp.float32), axis=(0, 2))
    row_scale = lax.rsqrt(total_square / (width * tp_count) + EPSILON)
    tokens = whole[:, :, :width]
    gate_view = expert_gate[0].reshape(tp_count, width, hidden_part)
    up_view = expert_up[0].reshape(tp_count, width, hidden_part)
    both = jnp.concatenate(
        [
            jnp.einsum("tsf,tfh->sh", tokens, gate_view, preferred_element_type=jnp.float32),
            jnp.einsum("tsf,tfh->sh", tokens, up_view, preferred_element_type=jnp.float32),
        ],
        axis=1,
    )
    both = both * row_scale[:, None]
    gate_val = both[:, :hidden_part]
    up_val = both[:, hidden_part:]
    active = (gate_val * jax.nn.sigmoid(ALPHA * gate_val) * (up_val + 1.0)).astype(jnp.bfloat16)
    joined = tp_gather(active.T, 5)
    down_blocks = expert_down[0].reshape(tp_count, hidden_part, expert_down.shape[2])
    result = jnp.einsum("ths,thd->sd", joined, down_blocks, preferred_element_type=jnp.float32).astype(
        jnp.bfloat16
    )
    halves = result.reshape(2, experts, capacity, width)
    core = lax.rem(lax.axis_index("group"), 2)
    groups_total = lax.axis_size("group")
    swap = [(i, i + 1 - 2 * (i % 2)) for i in range(groups_total)]
    mine = lax.dynamic_index_in_dim(halves, core, 0, keepdims=False)
    theirs = lax.dynamic_index_in_dim(halves, 1 - core, 0, keepdims=False)
    other_half = lax.ppermute(theirs, "group", swap)
    joined_halves = (mine.astype(jnp.float32) + other_half.astype(jnp.float32)).astype(jnp.bfloat16)
    arrived = pair_exchange(lane_dense(joined_halves.reshape(experts, capacity * width)), 3)
    summed = arrived.reshape(experts, -1)[:, : capacity * width].astype(jnp.float32).reshape(experts * capacity, width)
    mixing = route_weights / jnp.sum(route_weights, axis=1, keepdims=True)
    expert_weight = jnp.sum(
        jnp.where(routes[:, :, None] == jnp.arange(experts, dtype=jnp.int32)[None, None, :], mixing[:, :, None], 0.0),
        axis=1,
    )
    combine = (slot_hit.astype(jnp.float32) * expert_weight[:, :, None]).reshape(block_len, experts * capacity)
    moe_out = jnp.dot(combine, summed, precision=lax.Precision.HIGHEST, preferred_element_type=jnp.float32)
    return (own_state + moe_out).astype(jnp.bfloat16)


def solution(mesh):
    return jax.shard_map(
        on_device,
        mesh=mesh,
        in_specs=(
            P("group", "tp"),
            P("group", "tp"),
            P("group", "tp"),
            P("group", "tp"),
            P("group", None),
            P("group"),
            P("tp"),
            P("tp", None),
            P("group", "tp"),
            P(),
            P("group", None),
            P("group", None),
            P("group", None, "tp"),
            P("group", None, "tp"),
            P("group", None, "tp"),
        ),
        out_specs=P("group", "tp"),
        check_vma=False,
    )
```

```python
import functools

import jax
import jax.numpy as jnp
from jax import lax
from jax.experimental import pallas as pl
from jax.experimental.pallas import tpu as pltpu
from jax.sharding import PartitionSpec as P

HEAD = 64


THETA = 150000.0
ALPHA = 1.702
EPSILON = 1e-05


def _row_parts(rows, parts=8):
    if not rows:
        return [(0, 0)]
    step = -(-rows // (parts * 16)) * 16
    return [(first, min(step, rows - first)) for first in range(0, rows, step)]


def _transfer_kernel(axis, gather, x_ref, buf, send_sem, recv_sem, local_sem):
    count = buf.shape[0]
    group_at = lax.axis_index("group")
    tp_at = lax.axis_index("tp")
    core = lax.rem(group_at, 2)
    if axis == "tp":
        me = tp_at
    elif axis == "pair":
        me = lax.div(group_at, 2)
    else:
        me = group_at

    def device(peer):
        if axis == "tp":
            return (group_at, peer)
        if axis == "pair":
            return (2 * peer + core, tp_at)
        return (peer, tp_at)

    def piece(peer):
        return x_ref if gather else x_ref.at[peer]

    barrier = pltpu.get_barrier_semaphore()

    def greet(step, carry):
        peer = lax.rem(me + step, count)
        pl.semaphore_signal(barrier, inc=1, device_id=device(peer), device_id_type=pl.DeviceIdType.MESH)
        return carry

    lax.fori_loop(1, count, greet, 0)
    pl.semaphore_wait(barrier, count - 1)
    local = pltpu.make_async_copy(piece(me), buf.at[me], local_sem)
    local.start()

    for first, size in _row_parts(buf.shape[1] if (gather or axis == "tp") else 0):

        def send(step, carry, first=first, size=size):
            peer = lax.rem(me + step, count)
            src = piece(peer)
            dst = buf.at[me]
            if size:
                src = src.at[pl.ds(first, size)]
                dst = dst.at[pl.ds(first, size)]
            pltpu.make_async_remote_copy(
                src_ref=src,
                dst_ref=dst,
                send_sem=send_sem,
                recv_sem=recv_sem,
                device_id=device(peer),
                device_id_type=pl.DeviceIdType.MESH,
            ).start()
            return carry

        lax.fori_loop(1, count, send, 0)
    local.wait()
    every = pltpu.make_async_remote_copy(
        src_ref=buf.at[pl.ds(0, count - 1)],
        dst_ref=buf.at[pl.ds(0, count - 1)],
        send_sem=send_sem,
        recv_sem=recv_sem,
        device_id=device(lax.rem(me + 1, count)),
        device_id_type=pl.DeviceIdType.MESH,
    )
    every.wait_send()
    every.wait_recv()


def _transfer(x, axis, gather, collective_id):
    count = lax.axis_size("group") // 2 if axis == "pair" else lax.axis_size(axis)
    shape = ((count,) + x.shape) if gather else x.shape
    return pl.pallas_call(
        functools.partial(_transfer_kernel, axis, gather),
        out_shape=jax.ShapeDtypeStruct(shape, x.dtype),
        in_specs=[pl.BlockSpec(memory_space=pltpu.VMEM)],
        out_specs=pl.BlockSpec(memory_space=pltpu.VMEM),
        scratch_shapes=[
            pltpu.SemaphoreType.DMA(()),
            pltpu.SemaphoreType.DMA(()),
            pltpu.SemaphoreType.DMA(()),
        ],
        compiler_params=pltpu.CompilerParams(collective_id=collective_id, has_side_effects=True),
    )(x)


def _pair_gather_kernel(x_ref, buf, send_sem, recv_sem, local_sem, pass_send, pass_recv):
    count = buf.shape[0]
    group_at = lax.axis_index("group")
    tp_at = lax.axis_index("tp")
    core = lax.rem(group_at, 2)
    sibling = (group_at + 1 - 2 * core, tp_at)
    barrier = pltpu.get_barrier_semaphore()

    def greet(step, carry):
        peer = lax.rem(tp_at + step, count)
        pl.semaphore_signal(barrier, inc=1, device_id=(group_at, peer), device_id_type=pl.DeviceIdType.MESH)
        return carry

    lax.fori_loop(1, count, greet, 0)
    pl.semaphore_signal(barrier, inc=1, device_id=sibling, device_id_type=pl.DeviceIdType.MESH)
    pl.semaphore_wait(barrier, count)
    local = pltpu.make_async_copy(x_ref, buf.at[tp_at, core], local_sem)
    local.start()
    pltpu.make_async_remote_copy(
        src_ref=x_ref,
        dst_ref=buf.at[tp_at, core],
        send_sem=pass_send,
        recv_sem=pass_recv,
        device_id=sibling,
        device_id_type=pl.DeviceIdType.MESH,
    ).start()

    for first, size in _row_parts(x_ref.shape[0]):

        def send(step, carry, first=first, size=size):
            peer = lax.rem(tp_at + step, count)
            pltpu.make_async_remote_copy(
                src_ref=x_ref.at[pl.ds(first, size)],
                dst_ref=buf.at[tp_at, core, pl.ds(first, size)],
                send_sem=send_sem,
                recv_sem=recv_sem,
                device_id=(group_at, peer),
                device_id_type=pl.DeviceIdType.MESH,
            ).start()
            return carry

        lax.fori_loop(1, count, send, 0)
    local.wait()
    every = pltpu.make_async_remote_copy(
        src_ref=buf.at[pl.ds(0, count - 1), 0],
        dst_ref=buf.at[pl.ds(0, count - 1), 0],
        send_sem=send_sem,
        recv_sem=recv_sem,
        device_id=(group_at, lax.rem(tp_at + 1, count)),
        device_id_type=pl.DeviceIdType.MESH,
    )
    every.wait_recv()

    def relay(step, carry):
        source = lax.rem(tp_at + count - step, count)
        pltpu.make_async_remote_copy(
            src_ref=buf.at[source, core],
            dst_ref=buf.at[source, core],
            send_sem=pass_send,
            recv_sem=pass_recv,
            device_id=sibling,
            device_id_type=pl.DeviceIdType.MESH,
        ).start()
        return carry

    lax.fori_loop(1, count, relay, 0)
    onward = pltpu.make_async_remote_copy(
        src_ref=buf.at[:, core],
        dst_ref=buf.at[:, core],
        send_sem=pass_send,
        recv_sem=pass_recv,
        device_id=sibling,
        device_id_type=pl.DeviceIdType.MESH,
    )
    every.wait_send()
    onward.wait_send()
    onward.wait_recv()


def pair_gather(x, collective_id):
    shape = (lax.axis_size("tp"), 2) + x.shape
    return pl.pallas_call(
        _pair_gather_kernel,
        out_shape=jax.ShapeDtypeStruct(shape, x.dtype),
        in_specs=[pl.BlockSpec(memory_space=pltpu.VMEM)],
        out_specs=pl.BlockSpec(memory_space=pltpu.VMEM),
        scratch_shapes=[pltpu.SemaphoreType.DMA(())] * 5,
        compiler_params=pltpu.CompilerParams(collective_id=collective_id, has_side_effects=True),
    )(x)


def pair_exchange(x, collective_id):
    return _transfer(x, "pair", False, collective_id)


def group_exchange(x, collective_id):
    return _transfer(x, "group", False, collective_id)


def tp_exchange(x, collective_id):
    return _transfer(x, "tp", False, collective_id)


def tp_gather(x, collective_id):
    return _transfer(x, "tp", True, collective_id)


def rotate(values, positions):
    half_dim = values.shape[-1] // 2
    inverse = THETA ** (-2.0 * jnp.arange(half_dim, dtype=jnp.float32) / values.shape[-1])
    angles = positions[:, None, None] * inverse[None, None, :]
    cosine = jnp.cos(angles)
    sine_part = jnp.sin(angles)
    first_part = values[..., :half_dim]
    second_part = values[..., half_dim:]
    return jnp.concatenate(
        [
            first_part * cosine - second_part * sine_part,
            second_part * cosine + first_part * sine_part,
        ],
        axis=-1,
    )


def attend(query_rows, kv_rows, cache_kv, cache_valid, sinks, length):
    block_len = query_rows.shape[0]
    kv_heads = kv_rows.shape[1] // (2 * HEAD)
    query_heads = query_rows.shape[1] // HEAD
    group_size = query_heads // kv_heads
    positions = (length + jnp.arange(block_len, dtype=jnp.int32)).astype(jnp.float32)
    query_rot = rotate(
        query_rows.astype(jnp.float32).reshape(block_len, query_heads, HEAD), positions
    ).astype(jnp.bfloat16)
    kv_parts = kv_rows.reshape(block_len, kv_heads, 2, HEAD)
    key_rot = rotate(kv_parts[:, :, 0].astype(jnp.float32), positions).astype(jnp.bfloat16)
    cache_parts = cache_kv.reshape(cache_kv.shape[0], kv_heads, 2, HEAD)
    all_keys = jnp.concatenate([cache_parts[:, :, 0], key_rot], axis=0)
    all_values = jnp.concatenate([cache_parts[:, :, 1], kv_parts[:, :, 1]], axis=0)
    token_order = jnp.arange(block_len, dtype=jnp.int32)
    causal = token_order[None, :] <= token_order[:, None]
    allowed = jnp.concatenate(
        [jnp.broadcast_to(cache_valid[None, :], (block_len, cache_valid.shape[0])), causal], axis=1
    )
    row_allowed = jnp.repeat(allowed, group_size, axis=0)
    score_scale = HEAD ** (-0.5)
    query_block = query_rot.reshape(block_len * group_size, HEAD)
    scores = (
        jnp.dot(query_block, all_keys[:, 0].T, preferred_element_type=jnp.float32) * score_scale
    )
    scores = jnp.where(row_allowed, scores, -jnp.inf)
    sink_rows = jnp.tile(sinks, block_len)
    row_max = jnp.maximum(jnp.max(scores, axis=1), sink_rows)
    weights = jnp.exp(scores - row_max[:, None])
    denominator = jnp.sum(weights, axis=1) + jnp.exp(sink_rows - row_max)
    blended = (
        jnp.dot(weights.astype(jnp.bfloat16), all_values[:, 0], preferred_element_type=jnp.float32)
        / denominator[:, None]
    )
    outputs = blended.astype(jnp.bfloat16).reshape(block_len, group_size * HEAD)
    return outputs


def lane_dense(rows):
    count, length = rows.shape
    padded = -(-length // 128) * 128
    rows = jnp.pad(rows, ((0, 0), (0, padded - length)))
    return rows.reshape(count, padded // 128, 128)


def on_device(
    queries,
    new_kv,
    local_cache,
    remote_pool,
    page_index,
    lengths,
    sinks,
    out_weight,
    residual,
    norm_gain,
    routes,
    route_weights,
    expert_gate,
    expert_up,
    expert_down,
):
    groups = lax.axis_size("group")
    lane_count = remote_pool.shape[1]
    local_len = local_cache.shape[0]
    fetched = group_exchange(remote_pool.reshape(groups, -1, lane_count), 1)
    page_len = fetched.shape[1]
    length = lengths[0]
    offsets = jnp.arange(page_len, dtype=jnp.int32)
    remote_pos = local_len + page_index[0][:, None] * page_len + offsets[None, :]
    cache_valid = jnp.concatenate(
        [jnp.ones((local_len,), jnp.bool_), (remote_pos < length).reshape(-1)]
    )
    cache_kv = jnp.concatenate([local_cache, fetched.reshape(-1, lane_count)], axis=0)
    attended = attend(queries, new_kv, cache_kv, cache_valid, sinks, length)
    width = residual.shape[1]
    tp_count = lax.axis_size("tp")
    start = lax.axis_index("tp") * width
    own_gain = lax.dynamic_slice_in_dim(norm_gain, start, width, 0)
    partial_sum = jnp.dot(attended, out_weight, preferred_element_type=jnp.float32)
    partial_blocks = partial_sum.reshape(partial_sum.shape[0], tp_count, width).transpose(1, 0, 2)
    own_attn = jnp.sum(tp_exchange(partial_blocks.astype(jnp.bfloat16), 6).astype(jnp.float32), axis=0)
    own_state = own_attn + residual.astype(jnp.float32)
    square_sum = jnp.sum(own_state * own_state, axis=1, keepdims=True)
    square_high = square_sum.astype(jnp.bfloat16)
    square_low = (square_sum - square_high.astype(jnp.float32)).astype(jnp.bfloat16)
    row_width = -(-(width + 2) // 128) * 128
    scaled_own = (own_state * own_gain).astype(jnp.bfloat16)
    normed_own = jnp.concatenate(
        [scaled_own, square_high, square_low, jnp.zeros((own_state.shape[0], row_width - width - 2), jnp.bfloat16)],
        axis=1,
    )
    block_len = normed_own.shape[0]
    top_count = routes.shape[1]
    experts = groups // 2
    capacity = 5 * block_len * top_count // (4 * experts)
    member = jnp.any(
        routes[:, :, None] == jnp.arange(experts, dtype=jnp.int32)[None, None, :], axis=1
    ).astype(jnp.int32)
    slot_rank = jnp.cumsum(member, axis=0) - member
    slot_hit = member[:, :, None] * (
        slot_rank[:, :, None] == jnp.arange(capacity, dtype=jnp.int32)[None, None, :]
    ).astype(jnp.int32)
    slot_matrix = slot_hit.transpose(1, 2, 0).reshape(experts * capacity, block_len)
    send_own = jnp.dot(
        slot_matrix.astype(jnp.bfloat16), normed_own, preferred_element_type=jnp.float32
    ).astype(jnp.bfloat16)
    hidden_part = expert_gate.shape[2]
    row_width = send_own.shape[1]
    received = pair_exchange(lane_dense(send_own.reshape(experts, capacity * row_width)), 2)
    received = received.reshape(experts, -1)[:, : capacity * row_width].reshape(experts, capacity, row_width)
    sources, slot_count, part_features = received.shape
    whole = pair_gather(received.reshape(sources * slot_count, part_features), 4)
    whole = whole.reshape(tp_count, 2 * sources * slot_count, part_features)
    total_square = jnp.sum(whole[:, :, width:width + 2].astype(jnp.float32), axis=(0, 2))
    row_scale = lax.rsqrt(total_square / (width * tp_count) + EPSILON)
    tokens = whole[:, :, :width]
    gate_view = expert_gate[0].reshape(tp_count, width, hidden_part)
    up_view = expert_up[0].reshape(tp_count, width, hidden_part)
    both = jnp.concatenate(
        [
            jnp.einsum("tsf,tfh->sh", tokens, gate_view, preferred_element_type=jnp.float32),
            jnp.einsum("tsf,tfh->sh", tokens, up_view, preferred_element_type=jnp.float32),
        ],
        axis=1,
    )
    both = both * row_scale[:, None]
    gate_val = both[:, :hidden_part]
    up_val = both[:, hidden_part:]
    active = (gate_val * jax.nn.sigmoid(ALPHA * gate_val) * (up_val + 1.0)).astype(jnp.bfloat16)
    joined = tp_gather(active.T, 5)
    down_blocks = expert_down[0].reshape(tp_count, hidden_part, expert_down.shape[2])
    result = jnp.einsum("ths,thd->sd", joined, down_blocks, preferred_element_type=jnp.float32).astype(
        jnp.bfloat16
    )
    halves = result.reshape(2, experts, capacity, width)
    core = lax.rem(lax.axis_index("group"), 2)
    groups_total = lax.axis_size("group")
    swap = [(i, i + 1 - 2 * (i % 2)) for i in range(groups_total)]
    mine = lax.dynamic_index_in_dim(halves, core, 0, keepdims=False)
    theirs = lax.dynamic_index_in_dim(halves, 1 - core, 0, keepdims=False)
    other_half = lax.ppermute(theirs, "group", swap)
    joined_halves = (mine.astype(jnp.float32) + other_half.astype(jnp.float32)).astype(jnp.bfloat16)
    arrived = pair_exchange(lane_dense(joined_halves.reshape(experts, capacity * width)), 3)
    summed = arrived.reshape(experts, -1)[:, : capacity * width].astype(jnp.float32).reshape(experts * capacity, width)
    mixing = route_weights / jnp.sum(route_weights, axis=1, keepdims=True)
    expert_weight = jnp.sum(
        jnp.where(routes[:, :, None] == jnp.arange(experts, dtype=jnp.int32)[None, None, :], mixing[:, :, None], 0.0),
        axis=1,
    )
    combine = (slot_hit.astype(jnp.float32) * expert_weight[:, :, None]).reshape(block_len, experts * capacity)
    moe_out = jnp.dot(combine, summed, precision=lax.Precision.HIGHEST, preferred_element_type=jnp.float32)
    return (own_state + moe_out).astype(jnp.bfloat16)


def solution(mesh):
    return jax.shard_map(
        on_device,
        mesh=mesh,
        in_specs=(
            P("group", "tp"),
            P("group", "tp"),
            P("group", "tp"),
            P("group", "tp"),
            P("group", None),
            P("group"),
            P("tp"),
            P("tp", None),
            P("group", "tp"),
            P(),
            P("group", None),
            P("group", None),
            P("group", None, "tp"),
            P("group", None, "tp"),
            P("group", None, "tp"),
        ),
        out_specs=P("group", "tp"),
        check_vma=False,
    )
```

```python
import functools

import jax
import jax.numpy as jnp
from jax import lax
from jax.experimental import pallas as pl
from jax.experimental.pallas import tpu as pltpu
from jax.sharding import PartitionSpec as P

HEAD = 64


THETA = 150000.0
ALPHA = 1.702
EPSILON = 1e-05


def _row_parts(rows, parts=8):
    if not rows:
        return [(0, 0)]
    step = -(-rows // (parts * 16)) * 16
    return [(first, min(step, rows - first)) for first in range(0, rows, step)]


def _transfer_kernel(axis, gather, x_ref, buf, send_sem, recv_sem, local_sem):
    count = buf.shape[0]
    group_at = lax.axis_index("group")
    tp_at = lax.axis_index("tp")
    core = lax.rem(group_at, 2)
    if axis == "tp":
        me = tp_at
    elif axis == "pair":
        me = lax.div(group_at, 2)
    else:
        me = group_at

    def device(peer):
        if axis == "tp":
            return (group_at, peer)
        if axis == "pair":
            return (2 * peer + core, tp_at)
        return (peer, tp_at)

    def piece(peer):
        return x_ref if gather else x_ref.at[peer]

    barrier = pltpu.get_barrier_semaphore()

    def greet(step, carry):
        peer = lax.rem(me + step, count)
        pl.semaphore_signal(barrier, inc=1, device_id=device(peer), device_id_type=pl.DeviceIdType.MESH)
        return carry

    lax.fori_loop(1, count, greet, 0)
    pl.semaphore_wait(barrier, count - 1)
    local = pltpu.make_async_copy(piece(me), buf.at[me], local_sem)
    local.start()

    for first, size in _row_parts(buf.shape[1] if (gather or axis == "tp") else 0):

        def send(step, carry, first=first, size=size):
            peer = lax.rem(me + step, count)
            src = piece(peer)
            dst = buf.at[me]
            if size:
                src = src.at[pl.ds(first, size)]
                dst = dst.at[pl.ds(first, size)]
            pltpu.make_async_remote_copy(
                src_ref=src,
                dst_ref=dst,
                send_sem=send_sem,
                recv_sem=recv_sem,
                device_id=device(peer),
                device_id_type=pl.DeviceIdType.MESH,
            ).start()
            return carry

        lax.fori_loop(1, count, send, 0)
    local.wait()
    every = pltpu.make_async_remote_copy(
        src_ref=buf.at[pl.ds(0, count - 1)],
        dst_ref=buf.at[pl.ds(0, count - 1)],
        send_sem=send_sem,
        recv_sem=recv_sem,
        device_id=device(lax.rem(me + 1, count)),
        device_id_type=pl.DeviceIdType.MESH,
    )
    every.wait_send()
    every.wait_recv()


def _transfer(x, axis, gather, collective_id):
    count = lax.axis_size("group") // 2 if axis == "pair" else lax.axis_size(axis)
    shape = ((count,) + x.shape) if gather else x.shape
    return pl.pallas_call(
        functools.partial(_transfer_kernel, axis, gather),
        out_shape=jax.ShapeDtypeStruct(shape, x.dtype),
        in_specs=[pl.BlockSpec(memory_space=pltpu.VMEM)],
        out_specs=pl.BlockSpec(memory_space=pltpu.VMEM),
        scratch_shapes=[
            pltpu.SemaphoreType.DMA(()),
            pltpu.SemaphoreType.DMA(()),
            pltpu.SemaphoreType.DMA(()),
        ],
        compiler_params=pltpu.CompilerParams(collective_id=collective_id, has_side_effects=True),
    )(x)


def _pair_gather_kernel(x_ref, buf, send_sem, recv_sem, local_sem, pass_send, pass_recv):
    count = buf.shape[0]
    group_at = lax.axis_index("group")
    tp_at = lax.axis_index("tp")
    core = lax.rem(group_at, 2)
    sibling = (group_at + 1 - 2 * core, tp_at)
    barrier = pltpu.get_barrier_semaphore()

    def greet(step, carry):
        peer = lax.rem(tp_at + step, count)
        pl.semaphore_signal(barrier, inc=1, device_id=(group_at, peer), device_id_type=pl.DeviceIdType.MESH)
        return carry

    lax.fori_loop(1, count, greet, 0)
    pl.semaphore_signal(barrier, inc=1, device_id=sibling, device_id_type=pl.DeviceIdType.MESH)
    pl.semaphore_wait(barrier, count)
    local = pltpu.make_async_copy(x_ref, buf.at[tp_at, core], local_sem)
    local.start()
    pltpu.make_async_remote_copy(
        src_ref=x_ref,
        dst_ref=buf.at[tp_at, core],
        send_sem=pass_send,
        recv_sem=pass_recv,
        device_id=sibling,
        device_id_type=pl.DeviceIdType.MESH,
    ).start()

    for first, size in _row_parts(x_ref.shape[0]):

        def send(step, carry, first=first, size=size):
            peer = lax.rem(tp_at + step, count)
            pltpu.make_async_remote_copy(
                src_ref=x_ref.at[pl.ds(first, size)],
                dst_ref=buf.at[tp_at, core, pl.ds(first, size)],
                send_sem=send_sem,
                recv_sem=recv_sem.at[tp_at],
                device_id=(group_at, peer),
                device_id_type=pl.DeviceIdType.MESH,
            ).start()
            return carry

        lax.fori_loop(1, count, send, 0)
    local.wait()
    every = pltpu.make_async_remote_copy(
        src_ref=buf.at[pl.ds(0, count - 1), 0],
        dst_ref=buf.at[pl.ds(0, count - 1), 0],
        send_sem=send_sem,
        recv_sem=recv_sem.at[0],
        device_id=(group_at, lax.rem(tp_at + 1, count)),
        device_id_type=pl.DeviceIdType.MESH,
    )

    def relay(step, carry):
        source = lax.rem(tp_at + count - step, count)
        pltpu.make_async_remote_copy(
            src_ref=buf.at[source, core],
            dst_ref=buf.at[source, core],
            send_sem=pass_send,
            recv_sem=recv_sem.at[source],
            device_id=sibling,
            device_id_type=pl.DeviceIdType.MESH,
        ).wait_recv()
        pltpu.make_async_remote_copy(
            src_ref=buf.at[source, core],
            dst_ref=buf.at[source, core],
            send_sem=pass_send,
            recv_sem=pass_recv,
            device_id=sibling,
            device_id_type=pl.DeviceIdType.MESH,
        ).start()
        return carry

    lax.fori_loop(1, count, relay, 0)
    onward = pltpu.make_async_remote_copy(
        src_ref=buf.at[:, core],
        dst_ref=buf.at[:, core],
        send_sem=pass_send,
        recv_sem=pass_recv,
        device_id=sibling,
        device_id_type=pl.DeviceIdType.MESH,
    )
    every.wait_send()
    onward.wait_send()
    onward.wait_recv()


def pair_gather(x, collective_id):
    shape = (lax.axis_size("tp"), 2) + x.shape
    return pl.pallas_call(
        _pair_gather_kernel,
        out_shape=jax.ShapeDtypeStruct(shape, x.dtype),
        in_specs=[pl.BlockSpec(memory_space=pltpu.VMEM)],
        out_specs=pl.BlockSpec(memory_space=pltpu.VMEM),
        scratch_shapes=[pltpu.SemaphoreType.DMA(()), pltpu.SemaphoreType.DMA((shape[0],))] + [pltpu.SemaphoreType.DMA(())] * 3,
        compiler_params=pltpu.CompilerParams(collective_id=collective_id, has_side_effects=True),
    )(x)


def pair_exchange(x, collective_id):
    return _transfer(x, "pair", False, collective_id)


def group_exchange(x, collective_id):
    return _transfer(x, "group", False, collective_id)


def tp_exchange(x, collective_id):
    return _transfer(x, "tp", False, collective_id)


def tp_gather(x, collective_id):
    return _transfer(x, "tp", True, collective_id)


def rotate(values, positions):
    half_dim = values.shape[-1] // 2
    inverse = THETA ** (-2.0 * jnp.arange(half_dim, dtype=jnp.float32) / values.shape[-1])
    angles = positions[:, None, None] * inverse[None, None, :]
    cosine = jnp.cos(angles)
    sine_part = jnp.sin(angles)
    first_part = values[..., :half_dim]
    second_part = values[..., half_dim:]
    return jnp.concatenate(
        [
            first_part * cosine - second_part * sine_part,
            second_part * cosine + first_part * sine_part,
        ],
        axis=-1,
    )


def attend(query_rows, kv_rows, cache_kv, cache_valid, sinks, length):
    block_len = query_rows.shape[0]
    kv_heads = kv_rows.shape[1] // (2 * HEAD)
    query_heads = query_rows.shape[1] // HEAD
    group_size = query_heads // kv_heads
    positions = (length + jnp.arange(block_len, dtype=jnp.int32)).astype(jnp.float32)
    query_rot = rotate(
        query_rows.astype(jnp.float32).reshape(block_len, query_heads, HEAD), positions
    ).astype(jnp.bfloat16)
    kv_parts = kv_rows.reshape(block_len, kv_heads, 2, HEAD)
    key_rot = rotate(kv_parts[:, :, 0].astype(jnp.float32), positions).astype(jnp.bfloat16)
    cache_parts = cache_kv.reshape(cache_kv.shape[0], kv_heads, 2, HEAD)
    all_keys = jnp.concatenate([cache_parts[:, :, 0], key_rot], axis=0)
    all_values = jnp.concatenate([cache_parts[:, :, 1], kv_parts[:, :, 1]], axis=0)
    token_order = jnp.arange(block_len, dtype=jnp.int32)
    causal = token_order[None, :] <= token_order[:, None]
    allowed = jnp.concatenate(
        [jnp.broadcast_to(cache_valid[None, :], (block_len, cache_valid.shape[0])), causal], axis=1
    )
    row_allowed = jnp.repeat(allowed, group_size, axis=0)
    score_scale = HEAD ** (-0.5)
    query_block = query_rot.reshape(block_len * group_size, HEAD)
    scores = (
        jnp.dot(query_block, all_keys[:, 0].T, preferred_element_type=jnp.float32) * score_scale
    )
    scores = jnp.where(row_allowed, scores, -jnp.inf)
    sink_rows = jnp.tile(sinks, block_len)
    row_max = jnp.maximum(jnp.max(scores, axis=1), sink_rows)
    weights = jnp.exp(scores - row_max[:, None])
    denominator = jnp.sum(weights, axis=1) + jnp.exp(sink_rows - row_max)
    blended = (
        jnp.dot(weights.astype(jnp.bfloat16), all_values[:, 0], preferred_element_type=jnp.float32)
        / denominator[:, None]
    )
    outputs = blended.astype(jnp.bfloat16).reshape(block_len, group_size * HEAD)
    return outputs


def lane_dense(rows):
    count, length = rows.shape
    padded = -(-length // 128) * 128
    rows = jnp.pad(rows, ((0, 0), (0, padded - length)))
    return rows.reshape(count, padded // 128, 128)


def on_device(
    queries,
    new_kv,
    local_cache,
    remote_pool,
    page_index,
    lengths,
    sinks,
    out_weight,
    residual,
    norm_gain,
    routes,
    route_weights,
    expert_gate,
    expert_up,
    expert_down,
):
    groups = lax.axis_size("group")
    lane_count = remote_pool.shape[1]
    local_len = local_cache.shape[0]
    fetched = group_exchange(remote_pool.reshape(groups, -1, lane_count), 1)
    page_len = fetched.shape[1]
    length = lengths[0]
    offsets = jnp.arange(page_len, dtype=jnp.int32)
    remote_pos = local_len + page_index[0][:, None] * page_len + offsets[None, :]
    cache_valid = jnp.concatenate(
        [jnp.ones((local_len,), jnp.bool_), (remote_pos < length).reshape(-1)]
    )
    cache_kv = jnp.concatenate([local_cache, fetched.reshape(-1, lane_count)], axis=0)
    attended = attend(queries, new_kv, cache_kv, cache_valid, sinks, length)
    width = residual.shape[1]
    tp_count = lax.axis_size("tp")
    start = lax.axis_index("tp") * width
    own_gain = lax.dynamic_slice_in_dim(norm_gain, start, width, 0)
    partial_sum = jnp.dot(attended, out_weight, preferred_element_type=jnp.float32)
    partial_blocks = partial_sum.reshape(partial_sum.shape[0], tp_count, width).transpose(1, 0, 2)
    own_attn = jnp.sum(tp_exchange(partial_blocks.astype(jnp.bfloat16), 6).astype(jnp.float32), axis=0)
    own_state = own_attn + residual.astype(jnp.float32)
    square_sum = jnp.sum(own_state * own_state, axis=1, keepdims=True)
    square_high = square_sum.astype(jnp.bfloat16)
    square_low = (square_sum - square_high.astype(jnp.float32)).astype(jnp.bfloat16)
    row_width = -(-(width + 2) // 128) * 128
    scaled_own = (own_state * own_gain).astype(jnp.bfloat16)
    normed_own = jnp.concatenate(
        [scaled_own, square_high, square_low, jnp.zeros((own_state.shape[0], row_width - width - 2), jnp.bfloat16)],
        axis=1,
    )
    block_len = normed_own.shape[0]
    top_count = routes.shape[1]
    experts = groups // 2
    capacity = 5 * block_len * top_count // (4 * experts)
    member = jnp.any(
        routes[:, :, None] == jnp.arange(experts, dtype=jnp.int32)[None, None, :], axis=1
    ).astype(jnp.int32)
    slot_rank = jnp.cumsum(member, axis=0) - member
    slot_hit = member[:, :, None] * (
        slot_rank[:, :, None] == jnp.arange(capacity, dtype=jnp.int32)[None, None, :]
    ).astype(jnp.int32)
    slot_matrix = slot_hit.transpose(1, 2, 0).reshape(experts * capacity, block_len)
    send_own = jnp.dot(
        slot_matrix.astype(jnp.bfloat16), normed_own, preferred_element_type=jnp.float32
    ).astype(jnp.bfloat16)
    hidden_part = expert_gate.shape[2]
    row_width = send_own.shape[1]
    received = pair_exchange(lane_dense(send_own.reshape(experts, capacity * row_width)), 2)
    received = received.reshape(experts, -1)[:, : capacity * row_width].reshape(experts, capacity, row_width)
    sources, slot_count, part_features = received.shape
    whole = pair_gather(received.reshape(sources * slot_count, part_features), 4)
    whole = whole.reshape(tp_count, 2 * sources * slot_count, part_features)
    total_square = jnp.sum(whole[:, :, width:width + 2].astype(jnp.float32), axis=(0, 2))
    row_scale = lax.rsqrt(total_square / (width * tp_count) + EPSILON)
    tokens = whole[:, :, :width]
    gate_view = expert_gate[0].reshape(tp_count, width, hidden_part)
    up_view = expert_up[0].reshape(tp_count, width, hidden_part)
    both = jnp.concatenate(
        [
            jnp.einsum("tsf,tfh->sh", tokens, gate_view, preferred_element_type=jnp.float32),
            jnp.einsum("tsf,tfh->sh", tokens, up_view, preferred_element_type=jnp.float32),
        ],
        axis=1,
    )
    both = both * row_scale[:, None]
    gate_val = both[:, :hidden_part]
    up_val = both[:, hidden_part:]
    active = (gate_val * jax.nn.sigmoid(ALPHA * gate_val) * (up_val + 1.0)).astype(jnp.bfloat16)
    joined = tp_gather(active.T, 5)
    down_blocks = expert_down[0].reshape(tp_count, hidden_part, expert_down.shape[2])
    result = jnp.einsum("ths,thd->sd", joined, down_blocks, preferred_element_type=jnp.float32).astype(
        jnp.bfloat16
    )
    halves = result.reshape(2, experts, capacity, width)
    core = lax.rem(lax.axis_index("group"), 2)
    groups_total = lax.axis_size("group")
    swap = [(i, i + 1 - 2 * (i % 2)) for i in range(groups_total)]
    mine = lax.dynamic_index_in_dim(halves, core, 0, keepdims=False)
    theirs = lax.dynamic_index_in_dim(halves, 1 - core, 0, keepdims=False)
    other_half = lax.ppermute(theirs, "group", swap)
    joined_halves = (mine.astype(jnp.float32) + other_half.astype(jnp.float32)).astype(jnp.bfloat16)
    arrived = pair_exchange(lane_dense(joined_halves.reshape(experts, capacity * width)), 3)
    summed = arrived.reshape(experts, -1)[:, : capacity * width].astype(jnp.float32).reshape(experts * capacity, width)
    mixing = route_weights / jnp.sum(route_weights, axis=1, keepdims=True)
    expert_weight = jnp.sum(
        jnp.where(routes[:, :, None] == jnp.arange(experts, dtype=jnp.int32)[None, None, :], mixing[:, :, None], 0.0),
        axis=1,
    )
    combine = (slot_hit.astype(jnp.float32) * expert_weight[:, :, None]).reshape(block_len, experts * capacity)
    moe_out = jnp.dot(combine, summed, precision=lax.Precision.HIGHEST, preferred_element_type=jnp.float32)
    return (own_state + moe_out).astype(jnp.bfloat16)


def solution(mesh):
    return jax.shard_map(
        on_device,
        mesh=mesh,
        in_specs=(
            P("group", "tp"),
            P("group", "tp"),
            P("group", "tp"),
            P("group", "tp"),
            P("group", None),
            P("group"),
            P("tp"),
            P("tp", None),
            P("group", "tp"),
            P(),
            P("group", None),
            P("group", None),
            P("group", None, "tp"),
            P("group", None, "tp"),
            P("group", None, "tp"),
        ),
        out_specs=P("group", "tp"),
        check_vma=False,
    )
```

```python
import functools

import jax
import jax.numpy as jnp
from jax import lax
from jax.experimental import pallas as pl
from jax.experimental.pallas import tpu as pltpu
from jax.sharding import PartitionSpec as P

HEAD = 64


THETA = 150000.0
ALPHA = 1.702
EPSILON = 1e-05


def _offset(step, count):
    odd = lax.rem(step, 2)
    return odd * lax.div(step + 1, 2) + (1 - odd) * (count - lax.div(step, 2))


def _row_parts(rows, parts=8):
    if not rows:
        return [(0, 0)]
    step = -(-rows // (parts * 16)) * 16
    return [(first, min(step, rows - first)) for first in range(0, rows, step)]


def _transfer_kernel(axis, gather, x_ref, buf, send_sem, recv_sem, local_sem):
    count = buf.shape[0]
    group_at = lax.axis_index("group")
    tp_at = lax.axis_index("tp")
    core = lax.rem(group_at, 2)
    if axis == "tp":
        me = tp_at
    elif axis == "pair":
        me = lax.div(group_at, 2)
    else:
        me = group_at

    def device(peer):
        if axis == "tp":
            return (group_at, peer)
        if axis == "pair":
            return (2 * peer + core, tp_at)
        return (peer, tp_at)

    def piece(peer):
        return x_ref if gather else x_ref.at[peer]

    barrier = pltpu.get_barrier_semaphore()

    def greet(step, carry):
        peer = lax.rem(me + step, count)
        pl.semaphore_signal(barrier, inc=1, device_id=device(peer), device_id_type=pl.DeviceIdType.MESH)
        return carry

    lax.fori_loop(1, count, greet, 0)
    pl.semaphore_wait(barrier, count - 1)
    local = pltpu.make_async_copy(piece(me), buf.at[me], local_sem)
    local.start()

    for first, size in _row_parts(buf.shape[1] if (gather or axis == "tp") else 0):

        def send(step, carry, first=first, size=size):
            peer = lax.rem(me + (_offset(step, count) if axis == "tp" else step), count)
            src = piece(peer)
            dst = buf.at[me]
            if size:
                src = src.at[pl.ds(first, size)]
                dst = dst.at[pl.ds(first, size)]
            pltpu.make_async_remote_copy(
                src_ref=src,
                dst_ref=dst,
                send_sem=send_sem,
                recv_sem=recv_sem,
                device_id=device(peer),
                device_id_type=pl.DeviceIdType.MESH,
            ).start()
            return carry

        lax.fori_loop(1, count, send, 0)
    local.wait()
    every = pltpu.make_async_remote_copy(
        src_ref=buf.at[pl.ds(0, count - 1)],
        dst_ref=buf.at[pl.ds(0, count - 1)],
        send_sem=send_sem,
        recv_sem=recv_sem,
        device_id=device(lax.rem(me + 1, count)),
        device_id_type=pl.DeviceIdType.MESH,
    )
    every.wait_send()
    every.wait_recv()


def _transfer(x, axis, gather, collective_id):
    count = lax.axis_size("group") // 2 if axis == "pair" else lax.axis_size(axis)
    shape = ((count,) + x.shape) if gather else x.shape
    return pl.pallas_call(
        functools.partial(_transfer_kernel, axis, gather),
        out_shape=jax.ShapeDtypeStruct(shape, x.dtype),
        in_specs=[pl.BlockSpec(memory_space=pltpu.VMEM)],
        out_specs=pl.BlockSpec(memory_space=pltpu.VMEM),
        scratch_shapes=[
            pltpu.SemaphoreType.DMA(()),
            pltpu.SemaphoreType.DMA(()),
            pltpu.SemaphoreType.DMA(()),
        ],
        compiler_params=pltpu.CompilerParams(collective_id=collective_id, has_side_effects=True),
    )(x)


def _pair_gather_kernel(x_ref, buf, send_sem, recv_sem, local_sem, pass_send, pass_recv):
    count = buf.shape[0]
    group_at = lax.axis_index("group")
    tp_at = lax.axis_index("tp")
    core = lax.rem(group_at, 2)
    sibling = (group_at + 1 - 2 * core, tp_at)
    barrier = pltpu.get_barrier_semaphore()

    def greet(step, carry):
        peer = lax.rem(tp_at + step, count)
        pl.semaphore_signal(barrier, inc=1, device_id=(group_at, peer), device_id_type=pl.DeviceIdType.MESH)
        return carry

    lax.fori_loop(1, count, greet, 0)
    pl.semaphore_signal(barrier, inc=1, device_id=sibling, device_id_type=pl.DeviceIdType.MESH)
    pl.semaphore_wait(barrier, count)
    local = pltpu.make_async_copy(x_ref, buf.at[tp_at, core], local_sem)
    local.start()
    pltpu.make_async_remote_copy(
        src_ref=x_ref,
        dst_ref=buf.at[tp_at, core],
        send_sem=pass_send,
        recv_sem=pass_recv,
        device_id=sibling,
        device_id_type=pl.DeviceIdType.MESH,
    ).start()

    for first, size in _row_parts(x_ref.shape[0]):

        def send(step, carry, first=first, size=size):
            peer = lax.rem(tp_at + _offset(step, count), count)
            pltpu.make_async_remote_copy(
                src_ref=x_ref.at[pl.ds(first, size)],
                dst_ref=buf.at[tp_at, core, pl.ds(first, size)],
                send_sem=send_sem,
                recv_sem=recv_sem.at[tp_at],
                device_id=(group_at, peer),
                device_id_type=pl.DeviceIdType.MESH,
            ).start()
            return carry

        lax.fori_loop(1, count, send, 0)
    local.wait()
    every = pltpu.make_async_remote_copy(
        src_ref=buf.at[pl.ds(0, count - 1), 0],
        dst_ref=buf.at[pl.ds(0, count - 1), 0],
        send_sem=send_sem,
        recv_sem=recv_sem.at[0],
        device_id=(group_at, lax.rem(tp_at + 1, count)),
        device_id_type=pl.DeviceIdType.MESH,
    )

    def relay(step, carry):
        source = lax.rem(tp_at + count - step, count)
        pltpu.make_async_remote_copy(
            src_ref=buf.at[source, core],
            dst_ref=buf.at[source, core],
            send_sem=pass_send,
            recv_sem=recv_sem.at[source],
            device_id=sibling,
            device_id_type=pl.DeviceIdType.MESH,
        ).wait_recv()
        pltpu.make_async_remote_copy(
            src_ref=buf.at[source, core],
            dst_ref=buf.at[source, core],
            send_sem=pass_send,
            recv_sem=pass_recv,
            device_id=sibling,
            device_id_type=pl.DeviceIdType.MESH,
        ).start()
        return carry

    lax.fori_loop(1, count, relay, 0)
    onward = pltpu.make_async_remote_copy(
        src_ref=buf.at[:, core],
        dst_ref=buf.at[:, core],
        send_sem=pass_send,
        recv_sem=pass_recv,
        device_id=sibling,
        device_id_type=pl.DeviceIdType.MESH,
    )
    every.wait_send()
    onward.wait_send()
    onward.wait_recv()


def pair_gather(x, collective_id):
    shape = (lax.axis_size("tp"), 2) + x.shape
    return pl.pallas_call(
        _pair_gather_kernel,
        out_shape=jax.ShapeDtypeStruct(shape, x.dtype),
        in_specs=[pl.BlockSpec(memory_space=pltpu.VMEM)],
        out_specs=pl.BlockSpec(memory_space=pltpu.VMEM),
        scratch_shapes=[pltpu.SemaphoreType.DMA(()), pltpu.SemaphoreType.DMA((shape[0],))] + [pltpu.SemaphoreType.DMA(())] * 3,
        compiler_params=pltpu.CompilerParams(collective_id=collective_id, has_side_effects=True),
    )(x)


def pair_exchange(x, collective_id):
    return _transfer(x, "pair", False, collective_id)


def group_exchange(x, collective_id):
    return _transfer(x, "group", False, collective_id)


def tp_exchange(x, collective_id):
    return _transfer(x, "tp", False, collective_id)


def tp_gather(x, collective_id):
    return _transfer(x, "tp", True, collective_id)


def rotate(values, positions):
    half_dim = values.shape[-1] // 2
    inverse = THETA ** (-2.0 * jnp.arange(half_dim, dtype=jnp.float32) / values.shape[-1])
    angles = positions[:, None, None] * inverse[None, None, :]
    cosine = jnp.cos(angles)
    sine_part = jnp.sin(angles)
    first_part = values[..., :half_dim]
    second_part = values[..., half_dim:]
    return jnp.concatenate(
        [
            first_part * cosine - second_part * sine_part,
            second_part * cosine + first_part * sine_part,
        ],
        axis=-1,
    )


def attend(query_rows, kv_rows, cache_kv, cache_valid, sinks, length):
    block_len = query_rows.shape[0]
    kv_heads = kv_rows.shape[1] // (2 * HEAD)
    query_heads = query_rows.shape[1] // HEAD
    group_size = query_heads // kv_heads
    positions = (length + jnp.arange(block_len, dtype=jnp.int32)).astype(jnp.float32)
    query_rot = rotate(
        query_rows.astype(jnp.float32).reshape(block_len, query_heads, HEAD), positions
    ).astype(jnp.bfloat16)
    kv_parts = kv_rows.reshape(block_len, kv_heads, 2, HEAD)
    key_rot = rotate(kv_parts[:, :, 0].astype(jnp.float32), positions).astype(jnp.bfloat16)
    cache_parts = cache_kv.reshape(cache_kv.shape[0], kv_heads, 2, HEAD)
    all_keys = jnp.concatenate([cache_parts[:, :, 0], key_rot], axis=0)
    all_values = jnp.concatenate([cache_parts[:, :, 1], kv_parts[:, :, 1]], axis=0)
    token_order = jnp.arange(block_len, dtype=jnp.int32)
    causal = token_order[None, :] <= token_order[:, None]
    allowed = jnp.concatenate(
        [jnp.broadcast_to(cache_valid[None, :], (block_len, cache_valid.shape[0])), causal], axis=1
    )
    row_allowed = jnp.repeat(allowed, group_size, axis=0)
    score_scale = HEAD ** (-0.5)
    query_block = query_rot.reshape(block_len * group_size, HEAD)
    scores = (
        jnp.dot(query_block, all_keys[:, 0].T, preferred_element_type=jnp.float32) * score_scale
    )
    scores = jnp.where(row_allowed, scores, -jnp.inf)
    sink_rows = jnp.tile(sinks, block_len)
    row_max = jnp.maximum(jnp.max(scores, axis=1), sink_rows)
    weights = jnp.exp(scores - row_max[:, None])
    denominator = jnp.sum(weights, axis=1) + jnp.exp(sink_rows - row_max)
    blended = (
        jnp.dot(weights.astype(jnp.bfloat16), all_values[:, 0], preferred_element_type=jnp.float32)
        / denominator[:, None]
    )
    outputs = blended.astype(jnp.bfloat16).reshape(block_len, group_size * HEAD)
    return outputs


def lane_dense(rows):
    count, length = rows.shape
    padded = -(-length // 128) * 128
    rows = jnp.pad(rows, ((0, 0), (0, padded - length)))
    return rows.reshape(count, padded // 128, 128)


def on_device(
    queries,
    new_kv,
    local_cache,
    remote_pool,
    page_index,
    lengths,
    sinks,
    out_weight,
    residual,
    norm_gain,
    routes,
    route_weights,
    expert_gate,
    expert_up,
    expert_down,
):
    groups = lax.axis_size("group")
    lane_count = remote_pool.shape[1]
    local_len = local_cache.shape[0]
    fetched = group_exchange(remote_pool.reshape(groups, -1, lane_count), 1)
    page_len = fetched.shape[1]
    length = lengths[0]
    offsets = jnp.arange(page_len, dtype=jnp.int32)
    remote_pos = local_len + page_index[0][:, None] * page_len + offsets[None, :]
    cache_valid = jnp.concatenate(
        [jnp.ones((local_len,), jnp.bool_), (remote_pos < length).reshape(-1)]
    )
    cache_kv = jnp.concatenate([local_cache, fetched.reshape(-1, lane_count)], axis=0)
    attended = attend(queries, new_kv, cache_kv, cache_valid, sinks, length)
    width = residual.shape[1]
    tp_count = lax.axis_size("tp")
    start = lax.axis_index("tp") * width
    own_gain = lax.dynamic_slice_in_dim(norm_gain, start, width, 0)
    partial_sum = jnp.dot(attended, out_weight, preferred_element_type=jnp.float32)
    partial_blocks = partial_sum.reshape(partial_sum.shape[0], tp_count, width).transpose(1, 0, 2)
    own_attn = jnp.sum(tp_exchange(partial_blocks.astype(jnp.bfloat16), 6).astype(jnp.float32), axis=0)
    own_state = own_attn + residual.astype(jnp.float32)
    square_sum = jnp.sum(own_state * own_state, axis=1, keepdims=True)
    square_high = square_sum.astype(jnp.bfloat16)
    square_low = (square_sum - square_high.astype(jnp.float32)).astype(jnp.bfloat16)
    row_width = -(-(width + 2) // 128) * 128
    scaled_own = (own_state * own_gain).astype(jnp.bfloat16)
    normed_own = jnp.concatenate(
        [scaled_own, square_high, square_low, jnp.zeros((own_state.shape[0], row_width - width - 2), jnp.bfloat16)],
        axis=1,
    )
    block_len = normed_own.shape[0]
    top_count = routes.shape[1]
    experts = groups // 2
    capacity = 5 * block_len * top_count // (4 * experts)
    member = jnp.any(
        routes[:, :, None] == jnp.arange(experts, dtype=jnp.int32)[None, None, :], axis=1
    ).astype(jnp.int32)
    slot_rank = jnp.cumsum(member, axis=0) - member
    slot_hit = member[:, :, None] * (
        slot_rank[:, :, None] == jnp.arange(capacity, dtype=jnp.int32)[None, None, :]
    ).astype(jnp.int32)
    slot_matrix = slot_hit.transpose(1, 2, 0).reshape(experts * capacity, block_len)
    send_own = jnp.dot(
        slot_matrix.astype(jnp.bfloat16), normed_own, preferred_element_type=jnp.float32
    ).astype(jnp.bfloat16)
    hidden_part = expert_gate.shape[2]
    row_width = send_own.shape[1]
    received = pair_exchange(lane_dense(send_own.reshape(experts, capacity * row_width)), 2)
    received = received.reshape(experts, -1)[:, : capacity * row_width].reshape(experts, capacity, row_width)
    sources, slot_count, part_features = received.shape
    whole = pair_gather(received.reshape(sources * slot_count, part_features), 4)
    whole = whole.reshape(tp_count, 2 * sources * slot_count, part_features)
    total_square = jnp.sum(whole[:, :, width:width + 2].astype(jnp.float32), axis=(0, 2))
    row_scale = lax.rsqrt(total_square / (width * tp_count) + EPSILON)
    tokens = whole[:, :, :width]
    gate_view = expert_gate[0].reshape(tp_count, width, hidden_part)
    up_view = expert_up[0].reshape(tp_count, width, hidden_part)
    both = jnp.concatenate(
        [
            jnp.einsum("tsf,tfh->sh", tokens, gate_view, preferred_element_type=jnp.float32),
            jnp.einsum("tsf,tfh->sh", tokens, up_view, preferred_element_type=jnp.float32),
        ],
        axis=1,
    )
    both = both * row_scale[:, None]
    gate_val = both[:, :hidden_part]
    up_val = both[:, hidden_part:]
    active = (gate_val * jax.nn.sigmoid(ALPHA * gate_val) * (up_val + 1.0)).astype(jnp.bfloat16)
    joined = tp_gather(active.T, 5)
    down_blocks = expert_down[0].reshape(tp_count, hidden_part, expert_down.shape[2])
    result = jnp.einsum("ths,thd->sd", joined, down_blocks, preferred_element_type=jnp.float32).astype(
        jnp.bfloat16
    )
    halves = result.reshape(2, experts, capacity, width)
    core = lax.rem(lax.axis_index("group"), 2)
    groups_total = lax.axis_size("group")
    swap = [(i, i + 1 - 2 * (i % 2)) for i in range(groups_total)]
    mine = lax.dynamic_index_in_dim(halves, core, 0, keepdims=False)
    theirs = lax.dynamic_index_in_dim(halves, 1 - core, 0, keepdims=False)
    other_half = lax.ppermute(theirs, "group", swap)
    joined_halves = (mine.astype(jnp.float32) + other_half.astype(jnp.float32)).astype(jnp.bfloat16)
    arrived = pair_exchange(lane_dense(joined_halves.reshape(experts, capacity * width)), 3)
    summed = arrived.reshape(experts, -1)[:, : capacity * width].astype(jnp.float32).reshape(experts * capacity, width)
    mixing = route_weights / jnp.sum(route_weights, axis=1, keepdims=True)
    expert_weight = jnp.sum(
        jnp.where(routes[:, :, None] == jnp.arange(experts, dtype=jnp.int32)[None, None, :], mixing[:, :, None], 0.0),
        axis=1,
    )
    combine = (slot_hit.astype(jnp.float32) * expert_weight[:, :, None]).reshape(block_len, experts * capacity)
    moe_out = jnp.dot(combine, summed, precision=lax.Precision.HIGHEST, preferred_element_type=jnp.float32)
    return (own_state + moe_out).astype(jnp.bfloat16)


def solution(mesh):
    return jax.shard_map(
        on_device,
        mesh=mesh,
        in_specs=(
            P("group", "tp"),
            P("group", "tp"),
            P("group", "tp"),
            P("group", "tp"),
            P("group", None),
            P("group"),
            P("tp"),
            P("tp", None),
            P("group", "tp"),
            P(),
            P("group", None),
            P("group", None),
            P("group", None, "tp"),
            P("group", None, "tp"),
            P("group", None, "tp"),
        ),
        out_specs=P("group", "tp"),
        check_vma=False,
    )
```
